32 devices in a mesh: ctx: 2 (over x), dp: 4 (over z), tp: 4 (over y, core).
Axes of the slice: x: 2, y: 2, z: 4, core: 2. Of those that a mesh axis runs over, the one named last changes fastest.
Arguments:
- query_act: bfloat16 [4, 4096, 256], P('dp', 'tp', 'ctx'), may hold values from -6 to 6
- key_act: bfloat16 [4, 4096, 256], P('dp', 'tp', 'ctx'), may hold values from -6 to 6
- value_act: bfloat16 [4, 4096, 256], P('dp', 'tp', 'ctx'), may hold values from -6 to 6
- out_grad: bfloat16 [4, 4096, 256], P('dp', 'tp', 'ctx'), may hold values from -6 to 6
- keep_mask: int32 [4, 256], P('dp', 'ctx'), may hold values 0 or 1
- filter_taps: float32 [256, 128], P('tp'), may hold values from -0.5 to 0.5
- skip_gain: float32 [4096], P('tp'), may hold values from -4 to 4
Outputs:
- operator_out: bfloat16 [4, 4096, 256], P('dp', 'tp', 'ctx')
- query_grad: bfloat16 [4, 4096, 256], P('dp', 'tp', 'ctx')
- key_grad: bfloat16 [4, 4096, 256], P('dp', 'tp', 'ctx')
- value_grad: bfloat16 [4, 4096, 256], P('dp', 'tp', 'ctx')
- filter_grad: float32 [256, 128], P('tp')
- skip_grad: float32 [4096], P('tp')
The draws below stay inside these ranges and needn't reach their ends.
All inputs are finite; a program needn't handle non-finite values. No bound on the sum of `keep_mask` on one device may be relied on, other than what follows from the above.
Results may differ from the reference program's by a relative error of at most 0.007.
Values may be sent and summed in bfloat16 or wider, within the bound.
No kernel may reach another device: no remote copies, remote signals or barrier semaphores. Data moves between devices by JAX's collectives and lax.ppermute only.
A program may use at most 64 MiB of HBM per device.

```python
import math
import jax
import jax.numpy as jnp
from jax import lax

CH = 4096
GROUP = 16
TAPS = 128
WINDOWS = 4
LEN = 256
GROUPS = 256


def place_ends(result, stream_key, smallest, top_value):
    index_at = [jax.random.randint(jax.random.fold_in(stream_key, axis), (), 0, length) for axis, length in enumerate(result.shape)]
    longest = result.shape.index(max(result.shape))
    beside = index_at[:longest] + [(index_at[longest] + 1) % result.shape[longest]] + index_at[longest + 1:]
    return result.at[tuple(index_at)].set(smallest).at[tuple(beside)].set(top_value)


def level_of(rng, extent, split, least, high):
    loudness = 1.0
    for position, shards_of in split:
        draws = jax.random.uniform(jax.random.fold_in(jax.random.fold_in(rng, 6), position), (shards_of,), jnp.float32, least / len(split), high / len(split))
        loudness = loudness * jnp.repeat(jnp.exp(draws), extent[position] // shards_of).reshape((-1,) + (1,) * (len(extent) - 1 - position))
    return loudness


def normal_values(stream_key, shape, scale, bound, split=(), dtype=jnp.bfloat16):
    values = jax.random.normal(stream_key, shape, jnp.float32) * scale
    if len(split) > 0:
        values = level_of(stream_key, shape, split, -0.22, 0.18) * values
    return jnp.clip(values, min=-bound, max=bound).astype(dtype)


def setup_inputs(seed: int = 0) -> dict:
    key_list = jax.random.split(jax.random.key(seed), 8)
    query_act = normal_values(key_list[0], (WINDOWS, CH, LEN), 1.0, 6.0, ((0, 4), (1, 4), (2, 2)))
    key_act = normal_values(key_list[1], (WINDOWS, CH, LEN), 1.0, 6.0, ((0, 4), (1, 4), (2, 2)))
    value_act = normal_values(key_list[2], (WINDOWS, CH, LEN), 1.0, 6.0, ((0, 4), (1, 4), (2, 2)))
    out_grad = normal_values(key_list[3], (WINDOWS, CH, LEN), 1.0, 6.0, ((0, 4), (1, 4), (2, 2)))
    keep_mask = place_ends((jax.random.randint(key_list[4], (WINDOWS, LEN), 0, 4) < 3).astype(jnp.int32), jax.random.fold_in(key_list[4], 1), 0, 1)
    filter_taps = normal_values(key_list[5], (GROUPS, TAPS), TAPS ** -0.5, 0.5, ((0, 4),), jnp.float32)
    skip_gain = normal_values(key_list[6], (CH,), 1.0, 4.0, ((0, 4),), jnp.float32)
    return {"query_act": query_act, "key_act": key_act, "value_act": value_act, "out_grad": out_grad, "keep_mask": keep_mask, "filter_taps": filter_taps, "skip_gain": skip_gain}


def tap_matrices(tap_rows):
    tap_len = tap_rows.shape[1]
    source = jnp.arange(tap_len)[:, None]
    target = jnp.arange(tap_len)[None, :]
    spread = tap_rows[:, jnp.mod(target - source, tap_len)]
    lower_part = jnp.where(target >= source, spread, jnp.zeros((), jnp.float32))
    upper_part = jnp.where(target < source, spread, jnp.zeros((), jnp.float32))
    forward = jnp.concatenate([upper_part, lower_part], axis=1)
    backward = jnp.concatenate([jnp.swapaxes(lower_part, 1, 2), jnp.swapaxes(upper_part, 1, 2)], axis=1)
    return (forward, backward)

def diagonal_sums(gram_sums):
    groups, tap_len, double_len = gram_sums.shape
    flattened = gram_sums.reshape(groups, tap_len * double_len)
    flattened = jnp.pad(flattened, ((0, 0), (0, tap_len)))
    skewed = flattened.reshape(groups, tap_len, double_len + 1)
    columns = lax.optimization_barrier(jnp.sum(skewed, axis=1))
    return columns[:, tap_len:0:-1]

def to_float(array):
    return array.astype(jnp.float32)

def rounded(array):
    return to_float(lax.optimization_barrier(array.astype(jnp.bfloat16)))

def reference(query_act, key_act, value_act, out_grad, keep_mask, filter_taps, skip_gain):
    forward, backward = tap_matrices(rounded(filter_taps))
    blocks = LEN // TAPS

    def one_window(packed):
        query_one, key_one, value_one, grad_one, keep_one = packed
        joined = rounded(to_float(key_one) * to_float(value_one))
        joined_blocks = joined.reshape(CH, blocks, TAPS)
        earlier = jnp.concatenate([jnp.zeros((CH, 1, TAPS), jnp.float32), joined_blocks[:, :-1, :]], axis=1)
        paired = jnp.concatenate([earlier, joined_blocks], axis=2).reshape(GROUPS, GROUP, blocks, 2 * TAPS)
        mixed_sum = jnp.einsum('gcbs,gst->gcbt', paired, forward).reshape(CH, LEN)
        mixed_sum = mixed_sum + skip_gain[:, None] * joined
        operator_out = (to_float(query_one) * mixed_sum).astype(jnp.bfloat16)
        scaled_grad = to_float(grad_one) * keep_one.astype(jnp.float32)[None, :]
        mixed_grad = rounded(scaled_grad * to_float(query_one))
        query_grad = (scaled_grad * mixed_sum).astype(jnp.bfloat16)
        grad_blocks = mixed_grad.reshape(CH, blocks, TAPS)
        next_blocks = jnp.concatenate([grad_blocks[:, 1:, :], jnp.zeros((CH, 1, TAPS), jnp.float32)], axis=1)
        paired_grad = jnp.concatenate([grad_blocks, next_blocks], axis=2).reshape(GROUPS, GROUP, blocks, 2 * TAPS)
        joined_grad = jnp.einsum('gcbs,gst->gcbt', paired_grad, backward).reshape(CH, LEN)
        joined_grad = joined_grad + skip_gain[:, None] * mixed_grad
        key_grad = (joined_grad * to_float(value_one)).astype(jnp.bfloat16)
        value_grad = (joined_grad * to_float(key_one)).astype(jnp.bfloat16)
        gram_sums = jnp.einsum('gcbt,gcbs->gts', grad_blocks.reshape(GROUPS, GROUP, blocks, TAPS), paired)
        tap_sums = diagonal_sums(gram_sums)
        skip_sums = lax.optimization_barrier(jnp.sum(mixed_grad * joined, axis=1))
        return (operator_out, query_grad, key_grad, value_grad, tap_sums, skip_sums)
    results = lax.map(one_window, (query_act, key_act, value_act, out_grad, keep_mask))
    tap_scale = 1.0 / math.sqrt(WINDOWS * LEN * GROUP)
    skip_scale = 1.0 / math.sqrt(WINDOWS * LEN)
    filter_grad = lax.optimization_barrier(jnp.sum(results[4], axis=0)) * tap_scale
    skip_grad = lax.optimization_barrier(jnp.sum(results[5], axis=0)) * skip_scale
    return (results[0], results[1], results[2], results[3], filter_grad, skip_grad)
```

```python
import functools
import math

import jax
import jax.numpy as jnp
from jax import lax
from jax.experimental import pallas as pl
from jax.experimental.pallas import tpu as pltpu
from jax.sharding import PartitionSpec as P

BF16 = jnp.bfloat16
F32 = jnp.float32
ROWS_BY_ROWS = (((1,), (1,)), ((), ()))


def iotas(rows, columns):
    return (
        lax.broadcasted_iota(jnp.int32, (rows, columns), 0),
        lax.broadcasted_iota(jnp.int32, (rows, columns), 1),
    )


def flip(block):
    length = block.shape[1]
    row, column = iotas(length, length)
    mirror = (row + column == length - 1).astype(F32).astype(BF16)
    return jnp.dot(block, mirror, preferred_element_type=F32).astype(BF16)


def lag_sums(grad, joined, per_group, wanted):
    channels, length = grad.shape
    per = length // per_group
    row, column = iotas(length, length)
    kept = wanted(row + column)
    mirrored = flip(joined)
    nothing = jnp.zeros((per_group, length), BF16)
    sums = []
    for start in range(0, channels, length):
        across = grad[start : start + length].T
        for g in range(per):
            mine = mirrored[start + g * per_group : start + (g + 1) * per_group]
            spread = jnp.concatenate([nothing] * g + [mine] + [nothing] * (per - 1 - g), axis=0)
            gram = jnp.where(kept, jnp.dot(across, spread, preferred_element_type=F32), 0.0)
            turned = pltpu.roll(gram, 0, 1, stride=1, stride_axis=0)
            sums.append(jnp.sum(turned, axis=0, keepdims=True))
    return pltpu.roll(jnp.concatenate(sums, axis=0), 1, 1)


def products(keep_ref, query_ref, key_ref, value_ref, grad_ref):
    keep = keep_ref[...].astype(F32)
    joined = (key_ref[...].astype(F32) * value_ref[...].astype(F32)).astype(BF16)
    mixed = (grad_ref[...].astype(F32) * keep * query_ref[...].astype(F32)).astype(BF16)
    return joined, mixed


def local_kernel(per_group, keep_ref, query_ref, key_ref, value_ref, grad_ref, sums_ref):
    channels, length = query_ref.shape
    groups = channels // per_group
    joined, mixed = products(keep_ref, query_ref, key_ref, value_ref, grad_ref)
    sums_ref[:groups] = lag_sums(mixed, joined, per_group, lambda total: total >= length - 1)
    both = joined.astype(F32) * mixed.astype(F32)
    high = both.astype(BF16)
    low = (both - high.astype(F32)).astype(BF16)
    ones = jnp.ones((8, length), BF16)
    direct = lax.dot_general(ones, high, ROWS_BY_ROWS, preferred_element_type=F32)
    direct += lax.dot_general(ones, low, ROWS_BY_ROWS, preferred_element_type=F32)
    for block in range(channels // length):
        sums_ref[groups + block : groups + block + 1] = direct[
            :1, block * length : (block + 1) * length
        ]


def local_sums(keep, query, key, value, grad, groups):
    channels, length = query.shape
    return pl.pallas_call(
        functools.partial(local_kernel, channels // groups),
        out_shape=jax.ShapeDtypeStruct((groups + channels // length, length), F32),
        cost_estimate=pl.CostEstimate(flops=2**26, bytes_accessed=2**23, transcendentals=0),
        name="local_sums",
    )(keep, query, key, value, grad)


def cross_kernel(per_group, swap, own_ref, halo_ref, mine_ref, other_ref, sums_ref):
    groups = own_ref.shape[0] // per_group
    length = own_ref.shape[1]
    own, halo = own_ref[...], halo_ref[...]
    if swap:
        first = lax.axis_index("ctx") == 0
        own, halo = jnp.where(first, halo, own), jnp.where(first, own, halo)
    total = mine_ref[...] + other_ref[...]
    crossed = lag_sums(own, halo, per_group, lambda total: total < length - 1)
    sums_ref[:groups] = (total[:groups] + crossed).astype(sums_ref.dtype)
    sums_ref[groups:] = total[groups:].astype(sums_ref.dtype)


def cross_sums(own, halo, mine, other, groups, swap, dtype):
    return pl.pallas_call(
        functools.partial(cross_kernel, own.shape[0] // groups, swap),
        out_shape=jax.ShapeDtypeStruct(mine.shape, dtype),
        cost_estimate=pl.CostEstimate(flops=2**26, bytes_accessed=2**23, transcendentals=0),
        name="cross_sums",
    )(own, halo, mine, other)


def output_kernel(
    per_group, one_halo, keep_ref, tap_ref, skip_ref, query_ref, key_ref, value_ref, grad_ref,
    before_ref, following_ref, out_ref, query_grad_ref, key_grad_ref, value_grad_ref,
):
    channels, length = query_ref.shape
    row, column = iotas(length, length)
    causal = column >= row
    keep = keep_ref[...].astype(F32)
    skips = skip_ref[0].T
    nothing = jnp.zeros((), BF16)
    if one_halo:
        position = lax.axis_index("ctx")
    for group in range(channels // per_group):
        part = slice(group * per_group, (group + 1) * per_group)
        query = query_ref[part].astype(F32)
        key = key_ref[part].astype(F32)
        value = value_ref[part].astype(F32)
        scaled = grad_ref[part].astype(F32) * keep
        joined = (key * value).astype(BF16)
        mixed = (scaled * query).astype(BF16)
        before, following = before_ref[part], following_ref[part]
        if one_halo:
            before = jnp.where(position == 0, nothing, before)
            following = jnp.where(position == 0, following, nothing)
        taps = jnp.broadcast_to(tap_ref[group : group + 1], (length, length))
        circle = pltpu.roll(taps, 0, 1, stride=1, stride_axis=0)
        lower = jnp.where(causal, circle, 0.0).astype(BF16)
        upper = jnp.where(causal, 0.0, circle).astype(BF16)
        start = group * per_group
        skip = skips[start % length : start % length + per_group, start // length : start // length + 1]
        forward = jnp.dot(
            jnp.concatenate([before, joined], axis=1),
            jnp.concatenate([upper, lower], axis=0),
            preferred_element_type=F32,
        )
        forward += skip * joined.astype(F32)
        backward = lax.dot_general(
            jnp.concatenate([mixed, following], axis=1),
            jnp.concatenate([lower, upper], axis=1),
            ROWS_BY_ROWS,
            preferred_element_type=F32,
        )
        backward += skip * mixed.astype(F32)
        out_ref[part] = (query * forward).astype(BF16)
        query_grad_ref[part] = (scaled * forward).astype(BF16)
        key_grad_ref[part] = (backward * value).astype(BF16)
        value_grad_ref[part] = (backward * key).astype(BF16)


def outputs(keep, taps, skip, query, key, value, grad, before, following, one_halo):
    channels, length = query.shape
    groups = taps.shape[0]
    steps = 2
    large = pl.BlockSpec((channels // steps, length), lambda i: (i, 0))
    skip_rows = skip.reshape(steps, channels // length // steps, length)
    return pl.pallas_call(
        functools.partial(output_kernel, channels // groups, one_halo),
        grid=(steps,),
        in_specs=[
            pl.BlockSpec((1, length), lambda i: (0, 0)),
            pl.BlockSpec((groups // steps, length), lambda i: (i, 0)),
            pl.BlockSpec((1,) + skip_rows.shape[1:], lambda i: (i, 0, 0)),
        ]
        + [large] * 6,
        out_specs=[large] * 4,
        out_shape=[jax.ShapeDtypeStruct((channels, length), BF16)] * 4,
        cost_estimate=pl.CostEstimate(flops=2**28, bytes_accessed=2**24, transcendentals=0),
        name="outputs",
    )(keep, taps, skip_rows, query, key, value, grad, before, following)


def sum_over(sums, axis):
    size = lax.axis_size(axis)
    if size & (size - 1):
        return lax.psum(sums.astype(F32), axis)
    terms = [sums]
    for offset in range(1, size):
        terms.append(lax.ppermute(sums, axis, [(i, i ^ offset) for i in range(size)]))
    terms = [term.astype(F32) for term in terms]
    while len(terms) > 1:
        terms = [a + b for a, b in zip(terms[::2], terms[1::2])]
    return terms[0]


def body(query_act, key_act, value_act, out_grad, keep_mask, filter_taps, skip_gain):
    windows, channels, length = query_act.shape
    groups, tap_count = filter_taps.shape
    assert windows == 1 and length == tap_count
    shards = lax.axis_size("ctx")
    per_group = channels // groups
    positions = windows * lax.axis_size("dp") * length * shards
    tap_scale = 1.0 / math.sqrt(positions * per_group)
    skip_scale = 1.0 / math.sqrt(positions)
    query, key, value, grad = query_act[0], key_act[0], value_act[0], out_grad[0]
    joined = key.astype(F32) * value.astype(F32)
    mixed = grad.astype(F32) * keep_mask.astype(F32) * query.astype(F32)
    if shards == 2:
        swap = [(0, 1), (1, 0)]
        own = jnp.where(lax.axis_index("ctx") == 0, joined, mixed).astype(BF16)
        halo = lax.ppermute(own, "ctx", swap)
        mine = local_sums(keep_mask, query, key, value, grad, groups)
        other = lax.ppermute(mine, "ctx", swap)
        sums = cross_sums(own, halo, mine, other, groups, True, BF16)
        before = following = halo
    else:
        own = mixed.astype(BF16)
        before = lax.ppermute(joined.astype(BF16), "ctx", [(i, i + 1) for i in range(shards - 1)])
        following = lax.ppermute(own, "ctx", [(i + 1, i) for i in range(shards - 1)])
        mine = local_sums(keep_mask, query, key, value, grad, groups)
        sums = cross_sums(own, before, mine, jnp.zeros_like(mine), groups, False, F32)
        sums = lax.psum(sums, "ctx")
    reduced = sum_over(sums, "dp")
    results = outputs(
        keep_mask, filter_taps, skip_gain, query, key, value, grad, before, following, shards == 2
    )
    return (
        *(result[None] for result in results),
        reduced[:groups] * tap_scale,
        reduced[groups:].reshape(channels) * skip_scale,
    )


def solution(mesh):
    large = P("dp", "tp", "ctx")
    return jax.shard_map(
        body,
        mesh=mesh,
        in_specs=(large, large, large, large, P("dp", "ctx"), P("tp", None), P("tp")),
        out_specs=(large, large, large, large, P("tp", None), P("tp")),
        check_vma=False,
    )
```

```python
import functools
import math

import jax
import jax.numpy as jnp
from jax import lax
from jax.experimental import pallas as pl
from jax.experimental.pallas import tpu as pltpu
from jax.sharding import PartitionSpec as P

BF16 = jnp.bfloat16
F32 = jnp.float32
ROWS_BY_ROWS = (((1,), (1,)), ((), ()))


def iotas(rows, columns):
    return (
        lax.broadcasted_iota(jnp.int32, (rows, columns), 0),
        lax.broadcasted_iota(jnp.int32, (rows, columns), 1),
    )


def flip(block):
    length = block.shape[1]
    row, column = iotas(length, length)
    mirror = (row + column == length - 1).astype(F32).astype(BF16)
    return jnp.dot(block, mirror, preferred_element_type=F32).astype(BF16)


def lag_sums(grad, joined, per_group, crossing):
    channels, length = grad.shape
    per = length // per_group
    phases = 4
    span = length // phases
    row, column = iotas(span, length)
    near = row + column >= span - 1
    lane = iotas(1, length)[1]
    owner = iotas(1, phases * length)[1] % length // per_group
    nothing = jnp.zeros((), BF16)
    mirrored = flip(joined)
    sums = []
    for start in range(0, channels, length):
        across = grad[start : start + length].T
        block = mirrored[start : start + length].astype(F32)
        left, right = [], []
        for phase in range(phases):
            left.append(across[phase * span : (phase + 1) * span])
            shift = span * (phase + 1)
            turned = (block if shift == length else pltpu.roll(block, shift, 1)).astype(BF16)
            if crossing:
                earlier = jnp.where(lane >= shift, turned, nothing)
                right.append(jnp.concatenate([earlier, turned], axis=1))
            else:
                right.append(jnp.where(lane < shift, turned, nothing))
        left = jnp.concatenate(left, axis=1)
        left = jnp.concatenate([jnp.where(owner == g, left, nothing) for g in range(per)], axis=0)
        grams = jnp.dot(left, jnp.concatenate(right, axis=0), preferred_element_type=F32)
        for g in range(per):
            gram = grams[g * span : (g + 1) * span]
            gram = jnp.where(near, gram[:, :length], gram[:, length:] if crossing else 0.0)
            turned = pltpu.roll(gram, 0, 1, stride=1, stride_axis=0)
            sums.append(jnp.sum(turned, axis=0, keepdims=True))
    return pltpu.roll(jnp.concatenate(sums, axis=0), length - span + 1, 1)


def products(keep_ref, query_ref, key_ref, value_ref, grad_ref):
    keep = keep_ref[...].astype(F32)
    joined = (key_ref[...].astype(F32) * value_ref[...].astype(F32)).astype(BF16)
    mixed = (grad_ref[...].astype(F32) * keep * query_ref[...].astype(F32)).astype(BF16)
    return joined, mixed


def own_kernel(
    keep_hbm, query_hbm, key_hbm, value_hbm, grad_hbm, own_ref, one_ref, two_ref, keep_ref, sems
):
    first = lax.axis_index("ctx") == 0
    parts = 2
    rows = own_ref.shape[0] // parts

    def copies(source_one, source_two):
        made = []
        for part in range(parts):
            window = pl.ds(part * rows, rows)
            for side, (source, target) in enumerate(((source_one, one_ref), (source_two, two_ref))):
                made.append(
                    pltpu.make_async_copy(
                        source.at[window], target.at[window], sems.at[2 * part + side]
                    )
                )
        return made

    keep_copy = pltpu.make_async_copy(keep_hbm, keep_ref, sems.at[2 * parts])

    @pl.when(first)
    def _():
        for copy in copies(key_hbm, value_hbm):
            copy.start()

    @pl.when(jnp.logical_not(first))
    def _():
        for copy in copies(query_hbm, grad_hbm):
            copy.start()

    keep_copy.start()
    keep_copy.wait()
    keep = jnp.where(first, 1.0, keep_ref[...].astype(F32))
    waits = copies(key_hbm, value_hbm)
    for part in range(parts):
        waits[2 * part].wait()
        waits[2 * part + 1].wait()
        window = pl.ds(part * rows, rows)
        scaled = two_ref[window].astype(F32) * keep
        own_ref[window] = (scaled * one_ref[window].astype(F32)).astype(BF16)


def own_block(keep, query, key, value, grad):
    return pl.pallas_call(
        own_kernel,
        in_specs=[pl.BlockSpec(memory_space=pl.ANY)] * 5,
        out_specs=pl.BlockSpec(memory_space=pltpu.VMEM),
        out_shape=pltpu.VMEM(query.shape, BF16),
        scratch_shapes=[
            pltpu.VMEM(query.shape, BF16),
            pltpu.VMEM(query.shape, BF16),
            pltpu.VMEM(keep.shape, keep.dtype),
            pltpu.SemaphoreType.DMA((5,)),
        ],
        name="own_block",
    )(keep, query, key, value, grad)


def local_kernel(per_group, keep_ref, query_ref, key_ref, value_ref, grad_ref, sums_ref):
    channels, length = query_ref.shape
    groups = channels // per_group
    joined, mixed = products(keep_ref, query_ref, key_ref, value_ref, grad_ref)
    sums_ref[:groups] = lag_sums(mixed, joined, per_group, False).astype(sums_ref.dtype)
    both = joined.astype(F32) * mixed.astype(F32)
    high = both.astype(BF16)
    low = (both - high.astype(F32)).astype(BF16)
    ones = jnp.ones((8, length), BF16)
    direct = lax.dot_general(ones, high, ROWS_BY_ROWS, preferred_element_type=F32)
    direct += lax.dot_general(ones, low, ROWS_BY_ROWS, preferred_element_type=F32)
    for block in range(channels // length):
        sums_ref[groups + block : groups + block + 1] = direct[
            :1, block * length : (block + 1) * length
        ].astype(sums_ref.dtype)


def local_sums(keep, query, key, value, grad, groups, dtype):
    channels, length = query.shape
    return pl.pallas_call(
        functools.partial(local_kernel, channels // groups),
        out_specs=pl.BlockSpec(memory_space=pltpu.VMEM),
        out_shape=pltpu.VMEM((groups + channels // length, length), dtype),
        cost_estimate=pl.CostEstimate(flops=2**26, bytes_accessed=2**23, transcendentals=0),
        name="local_sums",
    )(keep, query, key, value, grad)


def cross_kernel(per_group, swap, own_ref, halo_ref, sums_ref):
    own, halo = own_ref[...], halo_ref[...]
    if swap:
        first = lax.axis_index("ctx") == 0
        own, halo = jnp.where(first, halo, own), jnp.where(first, own, halo)
    sums_ref[...] = lag_sums(own, halo, per_group, True)


def in_vmem(array):
    return pltpu.with_memory_space_constraint(array, pltpu.VMEM)


def cross_sums(own, halo, groups, swap):
    channels, length = own.shape
    whole = pl.BlockSpec(memory_space=pltpu.VMEM)
    return pl.pallas_call(
        functools.partial(cross_kernel, channels // groups, swap),
        in_specs=[whole] * 2,
        out_specs=whole,
        out_shape=pltpu.VMEM((groups, length), F32),
        cost_estimate=pl.CostEstimate(flops=2**26, bytes_accessed=2**23, transcendentals=0),
        name="cross_sums",
    )(in_vmem(own), in_vmem(halo))


def output_kernel(
    per_group, one_halo, keep_ref, tap_ref, skip_ref, query_ref, key_ref, value_ref, grad_ref,
    before_ref, following_ref, out_ref, query_grad_ref, key_grad_ref, value_grad_ref,
):
    channels, length = query_ref.shape
    row, column = iotas(length, length)
    causal = column >= row
    keep = keep_ref[...].astype(F32)
    skips = skip_ref[0].T
    nothing = jnp.zeros((), BF16)
    if one_halo:
        position = lax.axis_index("ctx")
    for group in range(channels // per_group):
        part = slice(group * per_group, (group + 1) * per_group)
        query = query_ref[part].astype(F32)
        key = key_ref[part].astype(F32)
        value = value_ref[part].astype(F32)
        scaled = grad_ref[part].astype(F32) * keep
        joined = (key * value).astype(BF16)
        mixed = (scaled * query).astype(BF16)
        before, following = before_ref[part], following_ref[part]
        if one_halo:
            before = jnp.where(position == 0, nothing, before)
            following = jnp.where(position == 0, following, nothing)
        taps = jnp.broadcast_to(tap_ref[group : group + 1], (length, length))
        circle = pltpu.roll(taps, 0, 1, stride=1, stride_axis=0)
        lower = jnp.where(causal, circle, 0.0).astype(BF16)
        upper = jnp.where(causal, 0.0, circle).astype(BF16)
        start = group * per_group
        skip = skips[start % length : start % length + per_group, start // length : start // length + 1]
        forward = jnp.dot(
            jnp.concatenate([before, joined], axis=1),
            jnp.concatenate([upper, lower], axis=0),
            preferred_element_type=F32,
        )
        forward += skip * joined.astype(F32)
        backward = lax.dot_general(
            jnp.concatenate([mixed, following], axis=1),
            jnp.concatenate([lower, upper], axis=1),
            ROWS_BY_ROWS,
            preferred_element_type=F32,
        )
        backward += skip * mixed.astype(F32)
        out_ref[part] = (query * forward).astype(BF16)
        query_grad_ref[part] = (scaled * forward).astype(BF16)
        key_grad_ref[part] = (backward * value).astype(BF16)
        value_grad_ref[part] = (backward * key).astype(BF16)


def outputs(keep, taps, skip, query, key, value, grad, before, following, one_halo):
    channels, length = query.shape
    groups = taps.shape[0]
    steps = 2
    large = pl.BlockSpec((channels // steps, length), lambda i: (i, 0))
    skip_rows = skip.reshape(steps, channels // length // steps, length)
    return pl.pallas_call(
        functools.partial(output_kernel, channels // groups, one_halo),
        grid=(steps,),
        in_specs=[
            pl.BlockSpec((1, length), lambda i: (0, 0)),
            pl.BlockSpec((groups // steps, length), lambda i: (i, 0)),
            pl.BlockSpec((1,) + skip_rows.shape[1:], lambda i: (i, 0, 0)),
        ]
        + [large] * 6,
        out_specs=[large] * 4,
        out_shape=[jax.ShapeDtypeStruct((channels, length), BF16)] * 4,
        cost_estimate=pl.CostEstimate(flops=2**28, bytes_accessed=2**24, transcendentals=0),
        name="outputs",
    )(keep, taps, skip_rows, query, key, value, grad, before, following)


def gather_terms(sums, axis):
    size = lax.axis_size(axis)
    if size & (size - 1):
        return [lax.psum(sums, axis)]
    taken = {0: sums}
    for offset in reversed(range(1, size)):
        taken[offset] = lax.ppermute(sums, axis, [(i, i ^ offset) for i in range(size)])
    return [taken[offset] for offset in range(size)]


def total_kernel(groups, tap_scale, skip_scale, *refs):
    *term_refs, tap_ref, skip_ref = refs
    terms = [ref[...].astype(F32) for ref in term_refs]
    while len(terms) > 1:
        terms = [a + b for a, b in zip(terms[::2], terms[1::2])]
    tap_ref[...] = terms[0][:groups] * tap_scale
    skip_ref[...] = terms[0][groups:] * skip_scale


def totals(terms, groups, tap_scale, skip_scale):
    rows, length = terms[0].shape
    return pl.pallas_call(
        functools.partial(total_kernel, groups, tap_scale, skip_scale),
        in_specs=[pl.BlockSpec(memory_space=pltpu.VMEM)] * len(terms),
        out_shape=[
            jax.ShapeDtypeStruct((groups, length), F32),
            jax.ShapeDtypeStruct((rows - groups, length), F32),
        ],
        name="totals",
    )(*(in_vmem(term) for term in terms))


def body(query_act, key_act, value_act, out_grad, keep_mask, filter_taps, skip_gain):
    windows, channels, length = query_act.shape
    groups, tap_count = filter_taps.shape
    assert windows == 1 and length == tap_count
    shards = lax.axis_size("ctx")
    per_group = channels // groups
    positions = windows * lax.axis_size("dp") * length * shards
    tap_scale = 1.0 / math.sqrt(positions * per_group)
    skip_scale = 1.0 / math.sqrt(positions)
    query, key, value, grad = query_act[0], key_act[0], value_act[0], out_grad[0]
    if shards == 2:
        swap = [(0, 1), (1, 0)]
        own = own_block(keep_mask, query, key, value, grad)
        halo = lax.ppermute(own, "ctx", swap)
        mine = local_sums(keep_mask, query, key, value, grad, groups, BF16)
        other = lax.ppermute(mine, "ctx", swap)
        crossed = cross_sums(own, halo, groups, True)
        sums = mine.astype(F32).at[:groups].add(crossed) + other.astype(F32)
        sums = lax.reduce_precision(sums, 8, 7).astype(BF16)
        before = following = halo
    else:
        joined = (key.astype(F32) * value.astype(F32)).astype(BF16)
        own = (grad.astype(F32) * keep_mask.astype(F32) * query.astype(F32)).astype(BF16)
        before = lax.ppermute(joined, "ctx", [(i, i + 1) for i in range(shards - 1)])
        following = lax.ppermute(own, "ctx", [(i + 1, i) for i in range(shards - 1)])
        mine = local_sums(keep_mask, query, key, value, grad, groups, F32)
        crossed = cross_sums(own, before, groups, False)
        sums = lax.psum(mine.at[:groups].add(crossed), "ctx")
    terms = gather_terms(sums, "dp")
    results = outputs(
        keep_mask, filter_taps, skip_gain, query, key, value, grad, before, following, shards == 2
    )
    filter_grad, skip_grad = totals(terms, groups, tap_scale, skip_scale)
    return (*(result[None] for result in results), filter_grad, skip_grad.reshape(channels))


def solution(mesh):
    large = P("dp", "tp", "ctx")
    return jax.shard_map(
        body,
        mesh=mesh,
        in_specs=(large, large, large, large, P("dp", "ctx"), P("tp", None), P("tp")),
        out_specs=(large, large, large, large, P("tp", None), P("tp")),
        check_vma=False,
    )
```

```python
import functools
import math

import jax
import jax.numpy as jnp
from jax import lax
from jax.experimental import pallas as pl
from jax.experimental.pallas import tpu as pltpu
from jax.sharding import PartitionSpec as P

BF16 = jnp.bfloat16
F32 = jnp.float32
ROWS_BY_ROWS = (((1,), (1,)), ((), ()))


def in_hbm(array):
    return pltpu.with_memory_space_constraint(array, pltpu.HBM)


def in_vmem(array):
    return pltpu.with_memory_space_constraint(array, pltpu.VMEM)


def iotas(rows, columns):
    return (
        lax.broadcasted_iota(jnp.int32, (rows, columns), 0),
        lax.broadcasted_iota(jnp.int32, (rows, columns), 1),
    )


def flip(block):
    length = block.shape[1]
    row, column = iotas(length, length)
    mirror = (row + column == length - 1).astype(F32).astype(BF16)
    return jnp.dot(block, mirror, preferred_element_type=F32).astype(BF16)


def lag_sums(grad, joined, per_group, crossing):
    channels, length = grad.shape
    per = length // per_group
    phases = 4
    span = length // phases
    row, column = iotas(span, length)
    near = row + column >= span - 1
    lane = iotas(1, length)[1]
    owner = iotas(1, phases * length)[1] % length // per_group
    nothing = jnp.zeros((), BF16)
    mirrored = flip(joined)
    sums = []
    for start in range(0, channels, length):
        across = grad[start : start + length].T
        block = mirrored[start : start + length].astype(F32)
        left, right = [], []
        for phase in range(phases):
            left.append(across[phase * span : (phase + 1) * span])
            shift = span * (phase + 1)
            turned = (block if shift == length else pltpu.roll(block, shift, 1)).astype(BF16)
            if crossing:
                earlier = jnp.where(lane >= shift, turned, nothing)
                right.append(jnp.concatenate([earlier, turned], axis=1))
            else:
                right.append(jnp.where(lane < shift, turned, nothing))
        left = jnp.concatenate(left, axis=1)
        left = jnp.concatenate([jnp.where(owner == g, left, nothing) for g in range(per)], axis=0)
        grams = jnp.dot(left, jnp.concatenate(right, axis=0), preferred_element_type=F32)
        for g in range(per):
            gram = grams[g * span : (g + 1) * span]
            gram = jnp.where(near, gram[:, :length], gram[:, length:] if crossing else 0.0)
            turned = pltpu.roll(gram, 0, 1, stride=1, stride_axis=0)
            sums.append(jnp.sum(turned, axis=0, keepdims=True))
    return pltpu.roll(jnp.concatenate(sums, axis=0), length - span + 1, 1)


def own_kernel(
    keep_hbm, query_hbm, key_hbm, value_hbm, grad_hbm, own_ref, one_ref, two_ref, keep_ref, sems
):
    first = lax.axis_index("ctx") == 0
    parts = 2
    rows = own_ref.shape[0] // parts

    def copies(source_one, source_two):
        made = []
        for part in range(parts):
            window = pl.ds(part * rows, rows)
            for side, (source, target) in enumerate(((source_one, one_ref), (source_two, two_ref))):
                made.append(
                    pltpu.make_async_copy(
                        source.at[window], target.at[window], sems.at[2 * part + side]
                    )
                )
        return made

    keep_copy = pltpu.make_async_copy(keep_hbm, keep_ref, sems.at[2 * parts])

    @pl.when(first)
    def _():
        for copy in copies(key_hbm, value_hbm):
            copy.start()

    @pl.when(jnp.logical_not(first))
    def _():
        for copy in copies(query_hbm, grad_hbm):
            copy.start()

    keep_copy.start()
    keep_copy.wait()
    keep = jnp.where(first, 1.0, keep_ref[...].astype(F32))
    waits = copies(key_hbm, value_hbm)
    for part in range(parts):
        waits[2 * part].wait()
        waits[2 * part + 1].wait()
        window = pl.ds(part * rows, rows)
        scaled = two_ref[window].astype(F32) * keep
        own_ref[window] = (scaled * one_ref[window].astype(F32)).astype(BF16)


def own_block(keep, query, key, value, grad):
    return pl.pallas_call(
        own_kernel,
        in_specs=[pl.BlockSpec(memory_space=pltpu.HBM)] * 5,
        out_specs=pl.BlockSpec(memory_space=pltpu.VMEM),
        out_shape=pltpu.VMEM(query.shape, BF16),
        scratch_shapes=[
            pltpu.VMEM(query.shape, BF16),
            pltpu.VMEM(query.shape, BF16),
            pltpu.VMEM(keep.shape, keep.dtype),
            pltpu.SemaphoreType.DMA((5,)),
        ],
        compiler_params=pltpu.CompilerParams(vmem_limit_bytes=12 * 2**20),
        name="own_block",
    )(*map(in_hbm, (keep, query, key, value, grad)))


def local_kernel(per_group, *refs):
    sources, sums_ref, (*held, sems) = refs[:5], refs[5], refs[6:]
    copies = [
        pltpu.make_async_copy(source, target, sems.at[index])
        for index, (source, target) in enumerate(zip(sources, held))
    ]
    for copy in copies:
        copy.start()
    for copy in copies:
        copy.wait()
    keep_ref, query_ref, key_ref, value_ref, grad_ref = held
    channels, length = query_ref.shape
    groups = channels // per_group
    joined = (key_ref[...].astype(F32) * value_ref[...].astype(F32)).astype(BF16)
    scaled = grad_ref[...].astype(F32) * keep_ref[...].astype(F32)
    mixed = (scaled * query_ref[...].astype(F32)).astype(BF16)
    sums_ref[:groups] = lag_sums(mixed, joined, per_group, False).astype(sums_ref.dtype)
    both = joined.astype(F32) * mixed.astype(F32)
    high = both.astype(BF16)
    low = (both - high.astype(F32)).astype(BF16)
    ones = jnp.ones((8, length), BF16)
    direct = lax.dot_general(ones, high, ROWS_BY_ROWS, preferred_element_type=F32)
    direct += lax.dot_general(ones, low, ROWS_BY_ROWS, preferred_element_type=F32)
    for block in range(channels // length):
        sums_ref[groups + block : groups + block + 1] = direct[
            :1, block * length : (block + 1) * length
        ].astype(sums_ref.dtype)


def local_sums(keep, query, key, value, grad, groups, dtype):
    channels, length = query.shape
    sources = (keep, query, key, value, grad)
    return pl.pallas_call(
        functools.partial(local_kernel, channels // groups),
        in_specs=[pl.BlockSpec(memory_space=pltpu.HBM)] * 5,
        out_specs=[pl.BlockSpec(memory_space=pltpu.VMEM)] * 6,
        out_shape=[pltpu.VMEM((groups + channels // length, length), dtype)]
        + [pltpu.VMEM(source.shape, source.dtype) for source in sources],
        scratch_shapes=[pltpu.SemaphoreType.DMA((5,))],
        cost_estimate=pl.CostEstimate(flops=2**26, bytes_accessed=2**23, transcendentals=0),
        compiler_params=pltpu.CompilerParams(vmem_limit_bytes=12 * 2**20),
        name="local_sums",
    )(*map(in_hbm, sources))


def cross_kernel(per_group, swap, own_ref, halo_ref, sums_ref):
    own, halo = own_ref[...], halo_ref[...]
    if swap:
        first = lax.axis_index("ctx") == 0
        own, halo = jnp.where(first, halo, own), jnp.where(first, own, halo)
    sums_ref[...] = lag_sums(own, halo, per_group, True)


def cross_sums(own, halo, groups, swap):
    channels, length = own.shape
    whole = pl.BlockSpec(memory_space=pltpu.VMEM)
    return pl.pallas_call(
        functools.partial(cross_kernel, channels // groups, swap),
        in_specs=[whole] * 2,
        out_specs=whole,
        out_shape=pltpu.VMEM((groups, length), F32),
        cost_estimate=pl.CostEstimate(flops=2**26, bytes_accessed=2**23, transcendentals=0),
        compiler_params=pltpu.CompilerParams(vmem_limit_bytes=12 * 2**20),
        name="cross_sums",
    )(in_vmem(own), in_vmem(halo))


def output_kernel(
    per_group, keep_ref, tap_ref, skip_ref, query_ref, key_ref, value_ref, grad_ref,
    before_ref, following_ref, out_ref, query_grad_ref, key_grad_ref, value_grad_ref,
):
    channels, length = query_ref.shape
    row, column = iotas(length, length)
    causal = column >= row
    keep = keep_ref[...].astype(F32)
    skips = skip_ref[0].T
    for group in range(channels // per_group):
        part = slice(group * per_group, (group + 1) * per_group)
        query = query_ref[part].astype(F32)
        key = key_ref[part].astype(F32)
        value = value_ref[part].astype(F32)
        scaled = grad_ref[part].astype(F32) * keep
        joined = (key * value).astype(BF16)
        mixed = (scaled * query).astype(BF16)
        before, following = before_ref[part], following_ref[part]
        taps = jnp.broadcast_to(tap_ref[group : group + 1], (length, length))
        circle = pltpu.roll(taps, 0, 1, stride=1, stride_axis=0)
        lower = jnp.where(causal, circle, 0.0).astype(BF16)
        upper = jnp.where(causal, 0.0, circle).astype(BF16)
        start = group * per_group
        skip = skips[start % length : start % length + per_group, start // length : start // length + 1]
        forward = jnp.dot(
            jnp.concatenate([before, joined], axis=1),
            jnp.concatenate([upper, lower], axis=0),
            preferred_element_type=F32,
        )
        forward += skip * joined.astype(F32)
        backward = lax.dot_general(
            jnp.concatenate([mixed, following], axis=1),
            jnp.concatenate([lower, upper], axis=1),
            ROWS_BY_ROWS,
            preferred_element_type=F32,
        )
        backward += skip * mixed.astype(F32)
        out_ref[part] = (query * forward).astype(BF16)
        query_grad_ref[part] = (scaled * forward).astype(BF16)
        key_grad_ref[part] = (backward * value).astype(BF16)
        value_grad_ref[part] = (backward * key).astype(BF16)


def outputs(keep, taps, skip, query, key, value, grad, before, following):
    channels, length = query.shape
    groups = taps.shape[0]
    steps = 2
    large = pl.BlockSpec((channels // steps, length), lambda i: (i, 0))
    skip_rows = skip.reshape(steps, channels // length // steps, length)
    return pl.pallas_call(
        functools.partial(output_kernel, channels // groups),
        grid=(steps,),
        in_specs=[
            pl.BlockSpec((1, length), lambda i: (0, 0)),
            pl.BlockSpec((groups // steps, length), lambda i: (i, 0)),
            pl.BlockSpec((1,) + skip_rows.shape[1:], lambda i: (i, 0, 0)),
        ]
        + [large] * 6,
        out_specs=[large] * 4,
        out_shape=[jax.ShapeDtypeStruct((channels, length), BF16)] * 4,
        cost_estimate=pl.CostEstimate(flops=2**28, bytes_accessed=2**24, transcendentals=0),
        compiler_params=pltpu.CompilerParams(vmem_limit_bytes=12 * 2**20),
        name="outputs",
    )(keep, taps, skip_rows, query, key, value, grad, before, following)


def row_copies(parts, part, made_refs, out_refs, sems):
    rows = made_refs[0].shape[0] // parts
    window = pl.ds(part * rows, rows)
    return [
        pltpu.make_async_copy(made.at[window], out.at[window], sems.at[2 * part + side])
        for side, (made, out) in enumerate(zip(made_refs, out_refs))
    ]


def early_kernel(
    per_group, parts, keep_ref, tap_ref, skip_ref, query_ref, key_ref, value_ref, grad_ref,
    out_ref, query_grad_ref, key_grad_ref, value_grad_ref, rest_ref, one_ref, two_ref, upper_ref,
    made_one_ref, made_two_ref, sems,
):
    channels, length = query_ref.shape
    groups = channels // per_group
    row, column = iotas(length, length)
    causal = column >= row
    keep = keep_ref[...].astype(F32)
    skips = skip_ref[...].T
    first = lax.axis_index("ctx") == 0
    made_refs = (made_one_ref, made_two_ref)

    def send(part, *refs):
        for copy in row_copies(parts, part, made_refs, refs, sems):
            copy.start()

    for group in range(groups):
        part = slice(group * per_group, (group + 1) * per_group)
        query = query_ref[part].astype(F32)
        key = key_ref[part].astype(F32)
        value = value_ref[part].astype(F32)
        scaled = grad_ref[part].astype(F32) * keep
        joined = (key * value).astype(BF16)
        mixed = (scaled * query).astype(BF16)
        taps = jnp.broadcast_to(tap_ref[group : group + 1], (length, length))
        circle = pltpu.roll(taps, 0, 1, stride=1, stride_axis=0)
        lower = jnp.where(causal, circle, 0.0).astype(BF16)
        upper_ref[group] = jnp.where(causal, 0.0, circle).astype(BF16)
        start = group * per_group
        skip = skips[start % length : start % length + per_group, start // length : start // length + 1]
        forward = jnp.dot(joined, lower, preferred_element_type=F32)
        forward += skip * joined.astype(F32)
        backward = lax.dot_general(mixed, lower, ROWS_BY_ROWS, preferred_element_type=F32)
        backward += skip * mixed.astype(F32)
        done = jnp.where(first, forward, backward)
        made_one_ref[part] = (done * jnp.where(first, query, value)).astype(BF16)
        made_two_ref[part] = (done * jnp.where(first, scaled, key)).astype(BF16)
        rest_ref[part] = jnp.where(first, backward, forward)
        one_ref[part] = jnp.where(first, value, query).astype(BF16)
        two_ref[part] = jnp.where(first, key, scaled).astype(BF16)
        if (group + 1) % (groups // parts) == 0:
            part = group // (groups // parts)
            pl.when(first)(functools.partial(send, part, out_ref, query_grad_ref))
            pl.when(jnp.logical_not(first))(
                functools.partial(send, part, key_grad_ref, value_grad_ref)
            )
    for part in range(parts):
        for copy in row_copies(parts, part, made_refs, (out_ref, query_grad_ref), sems):
            copy.wait()


def early_outputs(keep, taps, skip, query, key, value, grad):
    channels, length = query.shape
    groups = taps.shape[0]
    parts = 2
    whole = pl.BlockSpec(memory_space=pltpu.VMEM)
    return pl.pallas_call(
        functools.partial(early_kernel, channels // groups, parts),
        in_specs=[whole] * 7,
        out_specs=[pl.BlockSpec(memory_space=pltpu.HBM)] * 4 + [whole] * 4,
        out_shape=[jax.ShapeDtypeStruct((channels, length), BF16)] * 4
        + [
            pltpu.VMEM((channels, length), F32),
            pltpu.VMEM((channels, length), BF16),
            pltpu.VMEM((channels, length), BF16),
            pltpu.VMEM((groups, length, length), BF16),
        ],
        scratch_shapes=[
            pltpu.VMEM((channels, length), BF16),
            pltpu.VMEM((channels, length), BF16),
            pltpu.SemaphoreType.DMA((2 * parts,)),
        ],
        cost_estimate=pl.CostEstimate(flops=2**28, bytes_accessed=2**23, transcendentals=0),
        compiler_params=pltpu.CompilerParams(vmem_limit_bytes=12 * 2**20),
        name="early_outputs",
    )(in_vmem(keep), taps, skip.reshape(channels // length, length), *map(in_vmem, (query, key, value, grad)))


def late_kernel(
    per_group, parts, halo_ref, rest_ref, one_ref, two_ref, upper_ref, _out, _query_grad, _key_grad,
    _value_grad, out_ref, query_grad_ref, key_grad_ref, value_grad_ref, made_one_ref, made_two_ref, sems,
):
    groups = halo_ref.shape[0] // per_group
    first = lax.axis_index("ctx") == 0
    made_refs = (made_one_ref, made_two_ref)

    def run(transposed, *out_refs):
        for group in range(groups):
            part = slice(group * per_group, (group + 1) * per_group)
            halo, upper = halo_ref[part], upper_ref[group]
            if transposed:
                crossed = lax.dot_general(halo, upper, ROWS_BY_ROWS, preferred_element_type=F32)
            else:
                crossed = jnp.dot(halo, upper, preferred_element_type=F32)
            total = rest_ref[part] + crossed
            made_one_ref[part] = (total * one_ref[part].astype(F32)).astype(BF16)
            made_two_ref[part] = (total * two_ref[part].astype(F32)).astype(BF16)
            if (group + 1) % (groups // parts) == 0:
                part = group // (groups // parts)
                for copy in row_copies(parts, part, made_refs, out_refs, sems):
                    copy.start()
        for part in range(parts):
            for copy in row_copies(parts, part, made_refs, out_refs, sems):
                copy.wait()

    @pl.when(first)
    def _():
        run(True, key_grad_ref, value_grad_ref)

    @pl.when(jnp.logical_not(first))
    def _():
        run(False, out_ref, query_grad_ref)


def late_outputs(halo, rest, one, two, upper, *results):
    channels, length = halo.shape
    groups = upper.shape[0]
    parts = 2
    whole = pl.BlockSpec(memory_space=pltpu.VMEM)
    return pl.pallas_call(
        functools.partial(late_kernel, channels // groups, parts),
        in_specs=[whole] * 5 + [pl.BlockSpec(memory_space=pltpu.HBM)] * 4,
        out_specs=[pl.BlockSpec(memory_space=pltpu.HBM)] * 4,
        out_shape=[jax.ShapeDtypeStruct((channels, length), BF16)] * 4,
        input_output_aliases={5: 0, 6: 1, 7: 2, 8: 3},
        scratch_shapes=[
            pltpu.VMEM((channels, length), BF16),
            pltpu.VMEM((channels, length), BF16),
            pltpu.SemaphoreType.DMA((2 * parts,)),
        ],
        cost_estimate=pl.CostEstimate(flops=2**28, bytes_accessed=2**23, transcendentals=0),
        compiler_params=pltpu.CompilerParams(vmem_limit_bytes=12 * 2**20),
        name="late_outputs",
    )(in_vmem(halo), in_vmem(rest), in_vmem(one), in_vmem(two), in_vmem(upper), *results)


def gather_terms(sums, axis):
    size = lax.axis_size(axis)
    if size & (size - 1):
        return [lax.psum(sums, axis)]
    taken = {0: sums}
    for offset in reversed(range(1, size)):
        taken[offset] = lax.ppermute(sums, axis, [(i, i ^ offset) for i in range(size)])
    return [taken[offset] for offset in range(size)]


def total_kernel(groups, tap_scale, skip_scale, *refs):
    *term_refs, tap_ref, skip_ref = refs
    terms = [ref[...].astype(F32) for ref in term_refs]
    while len(terms) > 1:
        terms = [a + b for a, b in zip(terms[::2], terms[1::2])]
    tap_ref[...] = terms[0][:groups] * tap_scale
    skip_ref[...] = terms[0][groups:] * skip_scale


def totals(terms, groups, tap_scale, skip_scale):
    rows, length = terms[0].shape
    return pl.pallas_call(
        functools.partial(total_kernel, groups, tap_scale, skip_scale),
        in_specs=[pl.BlockSpec(memory_space=pltpu.VMEM)] * len(terms),
        out_shape=[
            jax.ShapeDtypeStruct((groups, length), F32),
            jax.ShapeDtypeStruct((rows - groups, length), F32),
        ],
        compiler_params=pltpu.CompilerParams(vmem_limit_bytes=12 * 2**20),
        name="totals",
    )(*(in_vmem(term) for term in terms))


def body(query_act, key_act, value_act, out_grad, keep_mask, filter_taps, skip_gain):
    windows, channels, length = query_act.shape
    groups, tap_count = filter_taps.shape
    assert windows == 1 and length == tap_count
    shards = lax.axis_size("ctx")
    per_group = channels // groups
    positions = windows * lax.axis_size("dp") * length * shards
    tap_scale = 1.0 / math.sqrt(positions * per_group)
    skip_scale = 1.0 / math.sqrt(positions)
    query, key, value, grad = query_act[0], key_act[0], value_act[0], out_grad[0]
    if shards == 2:
        swap = [(0, 1), (1, 0)]
        own = own_block(keep_mask, query, key, value, grad)
        halo = lax.ppermute(own, "ctx", swap)
        mine, *near = local_sums(keep_mask, query, key, value, grad, groups, BF16)
        other = lax.ppermute(mine, "ctx", swap)
        crossed = cross_sums(own, halo, groups, True)
        sums = mine.astype(F32).at[:groups].add(crossed) + other.astype(F32)
        sums = lax.reduce_precision(sums, 8, 7).astype(BF16)
        early = early_outputs(near[0], filter_taps, skip_gain, *near[1:])
        terms = gather_terms(sums, "dp")
        results = late_outputs(halo, *early[4:], *early[:4])
    else:
        joined = (key.astype(F32) * value.astype(F32)).astype(BF16)
        own = (grad.astype(F32) * keep_mask.astype(F32) * query.astype(F32)).astype(BF16)
        before = lax.ppermute(joined, "ctx", [(i, i + 1) for i in range(shards - 1)])
        following = lax.ppermute(own, "ctx", [(i + 1, i) for i in range(shards - 1)])
        mine, *_ = local_sums(keep_mask, query, key, value, grad, groups, F32)
        crossed = cross_sums(own, before, groups, False)
        sums = lax.psum(mine.at[:groups].add(crossed), "ctx")
        terms = gather_terms(sums, "dp")
        results = outputs(keep_mask, filter_taps, skip_gain, query, key, value, grad, before, following)
    filter_grad, skip_grad = totals(terms, groups, tap_scale, skip_scale)
    return (*(result[None] for result in results), filter_grad, skip_grad.reshape(channels))


def solution(mesh):
    large = P("dp", "tp", "ctx")
    return jax.shard_map(
        body,
        mesh=mesh,
        in_specs=(large, large, large, large, P("dp", "ctx"), P("tp", None), P("tp")),
        out_specs=(large, large, large, large, P("tp", None), P("tp")),
        check_vma=False,
    )
```

```python
import functools
import math

import jax
import jax.numpy as jnp
from jax import lax
from jax.experimental import pallas as pl
from jax.experimental.pallas import tpu as pltpu
from jax.sharding import PartitionSpec as P

BF16 = jnp.bfloat16
F32 = jnp.float32
ROWS_BY_ROWS = (((1,), (1,)), ((), ()))


def in_hbm(array):
    return pltpu.with_memory_space_constraint(array, pltpu.HBM)


def in_vmem(array):
    return pltpu.with_memory_space_constraint(array, pltpu.VMEM)


def iotas(rows, columns):
    return (
        lax.broadcasted_iota(jnp.int32, (rows, columns), 0),
        lax.broadcasted_iota(jnp.int32, (rows, columns), 1),
    )


def flip(block):
    length = block.shape[1]
    row, column = iotas(length, length)
    mirror = (row + column == length - 1).astype(F32).astype(BF16)
    return jnp.dot(block, mirror, preferred_element_type=F32).astype(BF16)


def lag_sums(grad, joined, per_group, crossing):
    channels, length = grad.shape
    per = length // per_group
    phases = 4
    span = length // phases
    row, column = iotas(span, length)
    near = row + column >= span - 1
    lane = iotas(1, length)[1]
    owner = iotas(1, phases * length)[1] % length // per_group
    nothing = jnp.zeros((), BF16)
    mirrored = flip(joined)
    sums = []
    for start in range(0, channels, length):
        across = grad[start : start + length].T
        block = mirrored[start : start + length].astype(F32)
        left, right = [], []
        for phase in range(phases):
            left.append(across[phase * span : (phase + 1) * span])
            shift = span * (phase + 1)
            turned = (block if shift == length else pltpu.roll(block, shift, 1)).astype(BF16)
            if crossing:
                earlier = jnp.where(lane >= shift, turned, nothing)
                right.append(jnp.concatenate([earlier, turned], axis=1))
            else:
                right.append(jnp.where(lane < shift, turned, nothing))
        left = jnp.concatenate(left, axis=1)
        left = jnp.concatenate([jnp.where(owner == g, left, nothing) for g in range(per)], axis=0)
        grams = jnp.dot(left, jnp.concatenate(right, axis=0), preferred_element_type=F32)
        for g in range(per):
            gram = grams[g * span : (g + 1) * span]
            gram = jnp.where(near, gram[:, :length], gram[:, length:] if crossing else 0.0)
            turned = pltpu.roll(gram, 0, 1, stride=1, stride_axis=0)
            sums.append(jnp.sum(turned, axis=0, keepdims=True))
    return pltpu.roll(jnp.concatenate(sums, axis=0), length - span + 1, 1)


def own_kernel(
    keep_hbm, query_hbm, key_hbm, value_hbm, grad_hbm, own_ref, one_ref, two_ref, keep_ref, sems
):
    first = lax.axis_index("ctx") == 0
    parts = 2
    rows = own_ref.shape[0] // parts

    def copies(source_one, source_two):
        made = []
        for part in range(parts):
            window = pl.ds(part * rows, rows)
            for side, (source, target) in enumerate(((source_one, one_ref), (source_two, two_ref))):
                made.append(
                    pltpu.make_async_copy(
                        source.at[window], target.at[window], sems.at[2 * part + side]
                    )
                )
        return made

    keep_copy = pltpu.make_async_copy(keep_hbm, keep_ref, sems.at[2 * parts])

    @pl.when(first)
    def _():
        for copy in copies(key_hbm, value_hbm):
            copy.start()

    @pl.when(jnp.logical_not(first))
    def _():
        for copy in copies(query_hbm, grad_hbm):
            copy.start()

    keep_copy.start()
    keep_copy.wait()
    keep = jnp.where(first, 1.0, keep_ref[...].astype(F32))
    waits = copies(key_hbm, value_hbm)
    for part in range(parts):
        waits[2 * part].wait()
        waits[2 * part + 1].wait()
        window = pl.ds(part * rows, rows)
        scaled = two_ref[window].astype(F32) * keep
        own_ref[window] = (scaled * one_ref[window].astype(F32)).astype(BF16)


def own_block(keep, query, key, value, grad):
    return pl.pallas_call(
        own_kernel,
        in_specs=[pl.BlockSpec(memory_space=pltpu.HBM)] * 5,
        out_specs=pl.BlockSpec(memory_space=pltpu.VMEM),
        out_shape=pltpu.VMEM(query.shape, BF16),
        scratch_shapes=[
            pltpu.VMEM(query.shape, BF16),
            pltpu.VMEM(query.shape, BF16),
            pltpu.VMEM(keep.shape, keep.dtype),
            pltpu.SemaphoreType.DMA((5,)),
        ],
        compiler_params=pltpu.CompilerParams(vmem_limit_bytes=12 * 2**20),
        name="own_block",
    )(*map(in_hbm, (keep, query, key, value, grad)))


def local_kernel(per_group, *refs):
    sources, sums_ref, (*held, sems) = refs[:5], refs[5], refs[6:]
    copies = [
        pltpu.make_async_copy(source, target, sems.at[index])
        for index, (source, target) in enumerate(zip(sources, held))
    ]
    for copy in copies:
        copy.start()
    for copy in copies:
        copy.wait()
    keep_ref, query_ref, key_ref, value_ref, grad_ref = held
    channels, length = query_ref.shape
    groups = channels // per_group
    joined = (key_ref[...].astype(F32) * value_ref[...].astype(F32)).astype(BF16)
    scaled = grad_ref[...].astype(F32) * keep_ref[...].astype(F32)
    mixed = (scaled * query_ref[...].astype(F32)).astype(BF16)
    sums_ref[:groups] = lag_sums(mixed, joined, per_group, False).astype(sums_ref.dtype)
    both = joined.astype(F32) * mixed.astype(F32)
    high = both.astype(BF16)
    low = (both - high.astype(F32)).astype(BF16)
    ones = jnp.ones((8, length), BF16)
    direct = lax.dot_general(ones, high, ROWS_BY_ROWS, preferred_element_type=F32)
    direct += lax.dot_general(ones, low, ROWS_BY_ROWS, preferred_element_type=F32)
    for block in range(channels // length):
        sums_ref[groups + block : groups + block + 1] = direct[
            :1, block * length : (block + 1) * length
        ].astype(sums_ref.dtype)


def local_sums(keep, query, key, value, grad, groups, dtype):
    channels, length = query.shape
    sources = (keep, query, key, value, grad)
    return pl.pallas_call(
        functools.partial(local_kernel, channels // groups),
        in_specs=[pl.BlockSpec(memory_space=pltpu.HBM)] * 5,
        out_specs=[pl.BlockSpec(memory_space=pltpu.VMEM)] * 6,
        out_shape=[pltpu.VMEM((groups + channels // length, length), dtype)]
        + [pltpu.VMEM(source.shape, source.dtype) for source in sources],
        scratch_shapes=[pltpu.SemaphoreType.DMA((5,))],
        cost_estimate=pl.CostEstimate(flops=2**26, bytes_accessed=2**23, transcendentals=0),
        compiler_params=pltpu.CompilerParams(vmem_limit_bytes=12 * 2**20),
        name="local_sums",
    )(*map(in_hbm, sources))


def cross_kernel(per_group, swap, own_ref, halo_ref, sums_ref):
    own, halo = own_ref[...], halo_ref[...]
    if swap:
        first = lax.axis_index("ctx") == 0
        own, halo = jnp.where(first, halo, own), jnp.where(first, own, halo)
    sums_ref[...] = lag_sums(own, halo, per_group, True)


def cross_sums(own, halo, groups, swap):
    channels, length = own.shape
    whole = pl.BlockSpec(memory_space=pltpu.VMEM)
    return pl.pallas_call(
        functools.partial(cross_kernel, channels // groups, swap),
        in_specs=[whole] * 2,
        out_specs=whole,
        out_shape=pltpu.VMEM((groups, length), F32),
        cost_estimate=pl.CostEstimate(flops=2**26, bytes_accessed=2**23, transcendentals=0),
        compiler_params=pltpu.CompilerParams(vmem_limit_bytes=12 * 2**20),
        name="cross_sums",
    )(in_vmem(own), in_vmem(halo))


def output_kernel(
    per_group, keep_ref, tap_ref, skip_ref, query_ref, key_ref, value_ref, grad_ref,
    before_ref, following_ref, out_ref, query_grad_ref, key_grad_ref, value_grad_ref,
):
    channels, length = query_ref.shape
    row, column = iotas(length, length)
    causal = column >= row
    keep = keep_ref[...].astype(F32)
    skips = skip_ref[0].T
    for group in range(channels // per_group):
        part = slice(group * per_group, (group + 1) * per_group)
        query = query_ref[part].astype(F32)
        key = key_ref[part].astype(F32)
        value = value_ref[part].astype(F32)
        scaled = grad_ref[part].astype(F32) * keep
        joined = (key * value).astype(BF16)
        mixed = (scaled * query).astype(BF16)
        before, following = before_ref[part], following_ref[part]
        taps = jnp.broadcast_to(tap_ref[group : group + 1], (length, length))
        circle = pltpu.roll(taps, 0, 1, stride=1, stride_axis=0)
        lower = jnp.where(causal, circle, 0.0).astype(BF16)
        upper = jnp.where(causal, 0.0, circle).astype(BF16)
        start = group * per_group
        skip = skips[start % length : start % length + per_group, start // length : start // length + 1]
        forward = jnp.dot(
            jnp.concatenate([before, joined], axis=1),
            jnp.concatenate([upper, lower], axis=0),
            preferred_element_type=F32,
        )
        forward += skip * joined.astype(F32)
        backward = lax.dot_general(
            jnp.concatenate([mixed, following], axis=1),
            jnp.concatenate([lower, upper], axis=1),
            ROWS_BY_ROWS,
            preferred_element_type=F32,
        )
        backward += skip * mixed.astype(F32)
        out_ref[part] = (query * forward).astype(BF16)
        query_grad_ref[part] = (scaled * forward).astype(BF16)
        key_grad_ref[part] = (backward * value).astype(BF16)
        value_grad_ref[part] = (backward * key).astype(BF16)


def outputs(keep, taps, skip, query, key, value, grad, before, following):
    channels, length = query.shape
    groups = taps.shape[0]
    steps = 2
    large = pl.BlockSpec((channels // steps, length), lambda i: (i, 0))
    skip_rows = skip.reshape(steps, channels // length // steps, length)
    return pl.pallas_call(
        functools.partial(output_kernel, channels // groups),
        grid=(steps,),
        in_specs=[
            pl.BlockSpec((1, length), lambda i: (0, 0)),
            pl.BlockSpec((groups // steps, length), lambda i: (i, 0)),
            pl.BlockSpec((1,) + skip_rows.shape[1:], lambda i: (i, 0, 0)),
        ]
        + [large] * 6,
        out_specs=[large] * 4,
        out_shape=[jax.ShapeDtypeStruct((channels, length), BF16)] * 4,
        cost_estimate=pl.CostEstimate(flops=2**28, bytes_accessed=2**24, transcendentals=0),
        compiler_params=pltpu.CompilerParams(vmem_limit_bytes=12 * 2**20),
        name="outputs",
    )(keep, taps, skip_rows, query, key, value, grad, before, following)


def row_copies(parts, part, made_refs, out_refs, sems):
    rows = made_refs[0].shape[0] // parts
    window = pl.ds(part * rows, rows)
    return [
        pltpu.make_async_copy(made.at[window], out.at[window], sems.at[2 * part + side])
        for side, (made, out) in enumerate(zip(made_refs, out_refs))
    ]


def early_kernel(
    per_group, parts, keep_ref, tap_ref, skip_ref, query_ref, key_ref, value_ref, grad_ref,
    out_ref, query_grad_ref, key_grad_ref, value_grad_ref, rest_ref, one_ref, two_ref, upper_ref,
    made_one_ref, made_two_ref, sems,
):
    channels, length = query_ref.shape
    groups = channels // per_group
    row, column = iotas(length, length)
    causal = column >= row
    keep = keep_ref[...].astype(F32)
    skips = skip_ref[...].T
    first = lax.axis_index("ctx") == 0
    made_refs = (made_one_ref, made_two_ref)

    def send(part, *refs):
        for copy in row_copies(parts, part, made_refs, refs, sems):
            copy.start()

    for group in range(groups):
        part = slice(group * per_group, (group + 1) * per_group)
        query = query_ref[part].astype(F32)
        key = key_ref[part].astype(F32)
        value = value_ref[part].astype(F32)
        scaled = grad_ref[part].astype(F32) * keep
        joined = (key * value).astype(BF16)
        mixed = (scaled * query).astype(BF16)
        taps = jnp.broadcast_to(tap_ref[group : group + 1], (length, length))
        circle = pltpu.roll(taps, 0, 1, stride=1, stride_axis=0)
        lower = jnp.where(causal, circle, 0.0).astype(BF16)
        upper_ref[group] = jnp.where(causal, 0.0, circle).astype(BF16)
        start = group * per_group
        skip = skips[start % length : start % length + per_group, start // length : start // length + 1]
        forward = jnp.dot(joined, lower, preferred_element_type=F32)
        forward += skip * joined.astype(F32)
        backward = lax.dot_general(mixed, lower, ROWS_BY_ROWS, preferred_element_type=F32)
        backward += skip * mixed.astype(F32)
        done = jnp.where(first, forward, backward)
        made_one_ref[part] = (done * jnp.where(first, query, value)).astype(BF16)
        made_two_ref[part] = (done * jnp.where(first, scaled, key)).astype(BF16)
        rest_ref[part] = jnp.where(first, backward, forward)
        one_ref[part] = jnp.where(first, value, query).astype(BF16)
        two_ref[part] = jnp.where(first, key, scaled).astype(BF16)
        if (group + 1) % (groups // parts) == 0:
            part = group // (groups // parts)
            pl.when(first)(functools.partial(send, part, out_ref, query_grad_ref))
            pl.when(jnp.logical_not(first))(
                functools.partial(send, part, key_grad_ref, value_grad_ref)
            )
    for part in range(parts):
        for copy in row_copies(parts, part, made_refs, (out_ref, query_grad_ref), sems):
            copy.wait()


def early_outputs(keep, taps, skip, query, key, value, grad):
    channels, length = query.shape
    groups = taps.shape[0]
    parts = 2
    whole = pl.BlockSpec(memory_space=pltpu.VMEM)
    return pl.pallas_call(
        functools.partial(early_kernel, channels // groups, parts),
        in_specs=[whole] * 7,
        out_specs=[pl.BlockSpec(memory_space=pltpu.HBM)] * 4 + [whole] * 4,
        out_shape=[jax.ShapeDtypeStruct((channels, length), BF16)] * 4
        + [
            pltpu.VMEM((channels, length), F32),
            pltpu.VMEM((channels, length), BF16),
            pltpu.VMEM((channels, length), BF16),
            pltpu.VMEM((groups, length, length), BF16),
        ],
        scratch_shapes=[
            pltpu.VMEM((channels, length), BF16),
            pltpu.VMEM((channels, length), BF16),
            pltpu.SemaphoreType.DMA((2 * parts,)),
        ],
        cost_estimate=pl.CostEstimate(flops=2**28, bytes_accessed=2**23, transcendentals=0),
        compiler_params=pltpu.CompilerParams(vmem_limit_bytes=12 * 2**20),
        name="early_outputs",
    )(in_vmem(keep), taps, skip.reshape(channels // length, length), *map(in_vmem, (query, key, value, grad)))


def late_kernel(
    per_group, parts, halo_ref, rest_ref, one_ref, two_ref, upper_ref, _out, _query_grad, _key_grad,
    _value_grad, out_ref, query_grad_ref, key_grad_ref, value_grad_ref, made_one_ref, made_two_ref, sems,
):
    groups = halo_ref.shape[0] // per_group
    first = lax.axis_index("ctx") == 0
    made_refs = (made_one_ref, made_two_ref)

    def run(transposed, *out_refs):
        for group in range(groups):
            part = slice(group * per_group, (group + 1) * per_group)
            halo, upper = halo_ref[part], upper_ref[group]
            if transposed:
                crossed = lax.dot_general(halo, upper, ROWS_BY_ROWS, preferred_element_type=F32)
            else:
                crossed = jnp.dot(halo, upper, preferred_element_type=F32)
            total = rest_ref[part] + crossed
            made_one_ref[part] = (total * one_ref[part].astype(F32)).astype(BF16)
            made_two_ref[part] = (total * two_ref[part].astype(F32)).astype(BF16)
            if (group + 1) % (groups // parts) == 0:
                part = group // (groups // parts)
                for copy in row_copies(parts, part, made_refs, out_refs, sems):
                    copy.start()
        for part in range(parts):
            for copy in row_copies(parts, part, made_refs, out_refs, sems):
                copy.wait()

    @pl.when(first)
    def _():
        run(True, key_grad_ref, value_grad_ref)

    @pl.when(jnp.logical_not(first))
    def _():
        run(False, out_ref, query_grad_ref)


def late_outputs(halo, rest, one, two, upper, *results):
    channels, length = halo.shape
    groups = upper.shape[0]
    parts = 2
    whole = pl.BlockSpec(memory_space=pltpu.VMEM)
    return pl.pallas_call(
        functools.partial(late_kernel, channels // groups, parts),
        in_specs=[whole] * 5 + [pl.BlockSpec(memory_space=pltpu.HBM)] * 4,
        out_specs=[pl.BlockSpec(memory_space=pltpu.HBM)] * 4,
        out_shape=[jax.ShapeDtypeStruct((channels, length), BF16)] * 4,
        input_output_aliases={5: 0, 6: 1, 7: 2, 8: 3},
        scratch_shapes=[
            pltpu.VMEM((channels, length), BF16),
            pltpu.VMEM((channels, length), BF16),
            pltpu.SemaphoreType.DMA((2 * parts,)),
        ],
        cost_estimate=pl.CostEstimate(flops=2**28, bytes_accessed=2**23, transcendentals=0),
        compiler_params=pltpu.CompilerParams(vmem_limit_bytes=12 * 2**20),
        name="late_outputs",
    )(in_vmem(halo), in_vmem(rest), in_vmem(one), in_vmem(two), in_vmem(upper), *results)


def exchanges(size):
    if size == 4:
        return [(2, 3, 1, 0), (3, 2, 0, 1), (1, 0, 3, 2)]
    return [tuple((i + step) % size for i in range(size)) for step in range(1, size)]


def gather_terms(sums, axis):
    return [sums] + [
        lax.ppermute(sums, axis, list(enumerate(targets)))
        for targets in exchanges(lax.axis_size(axis))
    ]


def total_kernel(groups, tap_scale, skip_scale, axis, order, *refs):
    *term_refs, tap_ref, skip_ref = refs
    taken = [term_refs[order.index(place)][...].astype(F32) for place in range(len(term_refs))]
    size = lax.axis_size(axis)
    here = lax.axis_index(axis)
    terms = [taken[0]] * size
    for received, targets in zip(taken[1:], exchanges(size)):
        for source, target in enumerate(targets):
            if source != target:
                terms[source] = jnp.where(here == target, received, terms[source])
    total = terms[0]
    for term in terms[1:]:
        total = total + term
    tap_ref[...] = total[:groups] * tap_scale
    skip_ref[...] = total[groups:] * skip_scale


def totals(terms, groups, tap_scale, skip_scale, axis):
    rows, length = terms[0].shape
    order = list(reversed(range(len(terms))))
    return pl.pallas_call(
        functools.partial(total_kernel, groups, tap_scale, skip_scale, axis, order),
        in_specs=[pl.BlockSpec(memory_space=pltpu.VMEM)] * len(terms),
        out_shape=[
            jax.ShapeDtypeStruct((groups, length), F32),
            jax.ShapeDtypeStruct((rows - groups, length), F32),
        ],
        compiler_params=pltpu.CompilerParams(vmem_limit_bytes=12 * 2**20),
        name="totals",
    )(*(in_vmem(terms[place]) for place in order))


def body(query_act, key_act, value_act, out_grad, keep_mask, filter_taps, skip_gain):
    windows, channels, length = query_act.shape
    groups, tap_count = filter_taps.shape
    assert windows == 1 and length == tap_count
    shards = lax.axis_size("ctx")
    per_group = channels // groups
    positions = windows * lax.axis_size("dp") * length * shards
    tap_scale = 1.0 / math.sqrt(positions * per_group)
    skip_scale = 1.0 / math.sqrt(positions)
    query, key, value, grad = query_act[0], key_act[0], value_act[0], out_grad[0]
    if shards == 2:
        swap = [(0, 1), (1, 0)]
        own = own_block(keep_mask, query, key, value, grad)
        halo = lax.ppermute(own, "ctx", swap)
        mine, *near = local_sums(keep_mask, query, key, value, grad, groups, BF16)
        other = lax.ppermute(mine, "ctx", swap)
        crossed = cross_sums(own, halo, groups, True)
        sums = mine.astype(F32).at[:groups].add(crossed) + other.astype(F32)
        sums = lax.reduce_precision(sums, 8, 7).astype(BF16)
        early = early_outputs(near[0], filter_taps, skip_gain, *near[1:])
        terms = gather_terms(sums, "dp")
        results = late_outputs(halo, *early[4:], *early[:4])
    else:
        joined = (key.astype(F32) * value.astype(F32)).astype(BF16)
        own = (grad.astype(F32) * keep_mask.astype(F32) * query.astype(F32)).astype(BF16)
        before = lax.ppermute(joined, "ctx", [(i, i + 1) for i in range(shards - 1)])
        following = lax.ppermute(own, "ctx", [(i + 1, i) for i in range(shards - 1)])
        mine, *_ = local_sums(keep_mask, query, key, value, grad, groups, F32)
        crossed = cross_sums(own, before, groups, False)
        sums = lax.psum(mine.at[:groups].add(crossed), "ctx")
        terms = gather_terms(sums, "dp")
        results = outputs(keep_mask, filter_taps, skip_gain, query, key, value, grad, before, following)
    filter_grad, skip_grad = totals(terms, groups, tap_scale, skip_scale, "dp")
    return (*(result[None] for result in results), filter_grad, skip_grad.reshape(channels))


def solution(mesh):
    large = P("dp", "tp", "ctx")
    return jax.shard_map(
        body,
        mesh=mesh,
        in_specs=(large, large, large, large, P("dp", "ctx"), P("tp", None), P("tp")),
        out_specs=(large, large, large, large, P("tp", None), P("tp")),
        check_vma=False,
    )
```

```python
import functools
import math

import jax
import jax.numpy as jnp
from jax import lax
from jax.experimental import pallas as pl
from jax.experimental.pallas import tpu as pltpu
from jax.sharding import PartitionSpec as P

BF16 = jnp.bfloat16
F32 = jnp.float32
ROWS_BY_ROWS = (((1,), (1,)), ((), ()))


def in_hbm(array):
    return pltpu.with_memory_space_constraint(array, pltpu.HBM)


def in_vmem(array):
    return pltpu.with_memory_space_constraint(array, pltpu.VMEM)


def iotas(rows, columns):
    return (
        lax.broadcasted_iota(jnp.int32, (rows, columns), 0),
        lax.broadcasted_iota(jnp.int32, (rows, columns), 1),
    )


def flip(block):
    length = block.shape[1]
    row, column = iotas(length, length)
    mirror = (row + column == length - 1).astype(F32).astype(BF16)
    return jnp.dot(block, mirror, preferred_element_type=F32).astype(BF16)


def lag_sums(grad, joined, per_group, crossing):
    channels, length = grad.shape
    per = length // per_group
    phases = 4
    span = length // phases
    row, column = iotas(span, length)
    near = row + column >= span - 1
    lane = iotas(1, length)[1]
    owner = iotas(1, phases * length)[1] % length // per_group
    nothing = jnp.zeros((), BF16)
    mirrored = flip(joined)
    sums = []
    for start in range(0, channels, length):
        across = grad[start : start + length].T
        block = mirrored[start : start + length].astype(F32)
        left, right = [], []
        for phase in range(phases):
            left.append(across[phase * span : (phase + 1) * span])
            shift = span * (phase + 1)
            turned = (block if shift == length else pltpu.roll(block, shift, 1)).astype(BF16)
            if crossing:
                earlier = jnp.where(lane >= shift, turned, nothing)
                right.append(jnp.concatenate([earlier, turned], axis=1))
            else:
                right.append(jnp.where(lane < shift, turned, nothing))
        left = jnp.concatenate(left, axis=1)
        left = jnp.concatenate([jnp.where(owner == g, left, nothing) for g in range(per)], axis=0)
        grams = jnp.dot(left, jnp.concatenate(right, axis=0), preferred_element_type=F32)
        for g in range(per):
            gram = grams[g * span : (g + 1) * span]
            gram = jnp.where(near, gram[:, :length], gram[:, length:] if crossing else 0.0)
            turned = pltpu.roll(gram, 0, 1, stride=1, stride_axis=0)
            sums.append(jnp.sum(turned, axis=0, keepdims=True))
    return pltpu.roll(jnp.concatenate(sums, axis=0), length - span + 1, 1)


def own_kernel(
    keep_hbm, query_hbm, key_hbm, value_hbm, grad_hbm, large_ref, small_ref, one_ref, two_ref, keep_ref,
    sems,
):
    first = lax.axis_index("ctx") == 0
    parts = 4
    rows = small_ref.shape[0]

    def copies(source_one, source_two):
        made = []
        for part in range(parts):
            window = pl.ds(part * rows, rows)
            for side, (source, target) in enumerate(((source_one, one_ref), (source_two, two_ref))):
                made.append(
                    pltpu.make_async_copy(
                        source.at[window], target.at[window], sems.at[2 * part + side]
                    )
                )
        return made

    keep_copy = pltpu.make_async_copy(keep_hbm, keep_ref, sems.at[2 * parts])

    @pl.when(first)
    def _():
        for copy in copies(key_hbm, value_hbm):
            copy.start()

    @pl.when(jnp.logical_not(first))
    def _():
        for copy in copies(query_hbm, grad_hbm):
            copy.start()

    keep_copy.start()
    keep_copy.wait()
    keep = jnp.where(first, 1.0, keep_ref[...].astype(F32))
    waits = copies(key_hbm, value_hbm)
    for part in range(parts):
        waits[2 * part].wait()
        waits[2 * part + 1].wait()
        window = pl.ds(part * rows, rows)
        scaled = two_ref[window].astype(F32) * keep
        own = (scaled * one_ref[window].astype(F32)).astype(BF16)
        if part < parts - 1:
            large_ref[window] = own
        else:
            small_ref[...] = own


def own_block(keep, query, key, value, grad):
    channels, length = query.shape
    whole = pl.BlockSpec(memory_space=pltpu.VMEM)
    return pl.pallas_call(
        own_kernel,
        in_specs=[pl.BlockSpec(memory_space=pltpu.HBM)] * 5,
        out_specs=[whole] * 2,
        out_shape=[
            pltpu.VMEM((channels * 3 // 4, length), BF16),
            pltpu.VMEM((channels // 4, length), BF16),
        ],
        scratch_shapes=[
            pltpu.VMEM(query.shape, BF16),
            pltpu.VMEM(query.shape, BF16),
            pltpu.VMEM(keep.shape, keep.dtype),
            pltpu.SemaphoreType.DMA((9,)),
        ],
        compiler_params=pltpu.CompilerParams(vmem_limit_bytes=12 * 2**20),
        name="own_block",
    )(*map(in_hbm, (keep, query, key, value, grad)))


def local_kernel(per_group, count, *refs):
    sources, sums_ref, (*held, sems) = refs[:count], refs[count], refs[count + 1 :]
    copies = [
        pltpu.make_async_copy(source, target, sems.at[index])
        for index, (source, target) in enumerate(zip(sources, held))
    ]
    for copy in copies:
        copy.start()
    for copy in copies[:5]:
        copy.wait()
    keep_ref, query_ref, key_ref, value_ref, grad_ref = held[:5]
    channels, length = query_ref.shape
    groups = channels // per_group
    joined = (key_ref[...].astype(F32) * value_ref[...].astype(F32)).astype(BF16)
    scaled = grad_ref[...].astype(F32) * keep_ref[...].astype(F32)
    mixed = (scaled * query_ref[...].astype(F32)).astype(BF16)
    sums_ref[:groups] = lag_sums(mixed, joined, per_group, False).astype(sums_ref.dtype)
    both = joined.astype(F32) * mixed.astype(F32)
    high = both.astype(BF16)
    low = (both - high.astype(F32)).astype(BF16)
    ones = jnp.ones((8, length), BF16)
    direct = lax.dot_general(ones, high, ROWS_BY_ROWS, preferred_element_type=F32)
    direct += lax.dot_general(ones, low, ROWS_BY_ROWS, preferred_element_type=F32)
    for block in range(channels // length):
        sums_ref[groups + block : groups + block + 1] = direct[
            :1, block * length : (block + 1) * length
        ].astype(sums_ref.dtype)
    for copy in copies[5:]:
        copy.wait()


def local_sums(groups, dtype, *sources):
    channels, length = sources[1].shape
    count = len(sources)
    return pl.pallas_call(
        functools.partial(local_kernel, channels // groups, count),
        in_specs=[pl.BlockSpec(memory_space=pltpu.HBM)] * count,
        out_specs=[pl.BlockSpec(memory_space=pltpu.VMEM)] * (count + 1),
        out_shape=[pltpu.VMEM((groups + channels // length, length), dtype)]
        + [pltpu.VMEM(source.shape, source.dtype) for source in sources],
        scratch_shapes=[pltpu.SemaphoreType.DMA((count,))],
        cost_estimate=pl.CostEstimate(flops=2**26, bytes_accessed=2**23, transcendentals=0),
        compiler_params=pltpu.CompilerParams(vmem_limit_bytes=12 * 2**20),
        name="local_sums",
    )(*map(in_hbm, sources))


def by_role(own, halo):
    first = lax.axis_index("ctx") == 0
    return jnp.where(first, halo, own), jnp.where(first, own, halo)


def last_kernel(per_group, own_ref, halo_ref, crossed_ref, mine_ref, other_ref, sums_ref):
    grad, joined = by_role(own_ref[...], halo_ref[...])
    crossed = lag_sums(grad, joined, per_group, True)
    sums = mine_ref[...].astype(F32) + other_ref[...].astype(F32)
    done = crossed_ref.shape[0]
    groups = done + crossed.shape[0]
    sums_ref[:done] = (sums[:done] + crossed_ref[...]).astype(BF16)
    sums_ref[done:groups] = (sums[done:groups] + crossed).astype(BF16)
    sums_ref[groups:] = sums[groups:].astype(BF16)


def last_sums(per_group, *arrays):
    whole = pl.BlockSpec(memory_space=pltpu.VMEM)
    return pl.pallas_call(
        functools.partial(last_kernel, per_group),
        in_specs=[whole] * len(arrays),
        out_specs=whole,
        out_shape=pltpu.VMEM(arrays[-1].shape, BF16),
        cost_estimate=pl.CostEstimate(flops=2**26, bytes_accessed=2**23, transcendentals=0),
        compiler_params=pltpu.CompilerParams(vmem_limit_bytes=12 * 2**20),
        name="last_sums",
    )(*map(in_vmem, arrays))


def cross_kernel(per_group, swap, own_ref, halo_ref, sums_ref):
    grad, joined = own_ref[...], halo_ref[...]
    if swap:
        grad, joined = by_role(grad, joined)
    sums_ref[...] = lag_sums(grad, joined, per_group, True)


def cross_sums(own, halo, groups, swap):
    channels, length = own.shape
    whole = pl.BlockSpec(memory_space=pltpu.VMEM)
    return pl.pallas_call(
        functools.partial(cross_kernel, channels // groups, swap),
        in_specs=[whole] * 2,
        out_specs=whole,
        out_shape=pltpu.VMEM((groups, length), F32),
        cost_estimate=pl.CostEstimate(flops=2**26, bytes_accessed=2**23, transcendentals=0),
        compiler_params=pltpu.CompilerParams(vmem_limit_bytes=12 * 2**20),
        name="cross_sums",
    )(in_vmem(own), in_vmem(halo))


def output_kernel(
    per_group, keep_ref, tap_ref, skip_ref, query_ref, key_ref, value_ref, grad_ref,
    before_ref, following_ref, out_ref, query_grad_ref, key_grad_ref, value_grad_ref,
):
    channels, length = query_ref.shape
    row, column = iotas(length, length)
    causal = column >= row
    keep = keep_ref[...].astype(F32)
    skips = skip_ref[0].T
    for group in range(channels // per_group):
        part = slice(group * per_group, (group + 1) * per_group)
        query = query_ref[part].astype(F32)
        key = key_ref[part].astype(F32)
        value = value_ref[part].astype(F32)
        scaled = grad_ref[part].astype(F32) * keep
        joined = (key * value).astype(BF16)
        mixed = (scaled * query).astype(BF16)
        before, following = before_ref[part], following_ref[part]
        taps = jnp.broadcast_to(tap_ref[group : group + 1], (length, length))
        circle = pltpu.roll(taps, 0, 1, stride=1, stride_axis=0)
        lower = jnp.where(causal, circle, 0.0).astype(BF16)
        upper = jnp.where(causal, 0.0, circle).astype(BF16)
        start = group * per_group
        skip = skips[start % length : start % length + per_group, start // length : start // length + 1]
        forward = jnp.dot(
            jnp.concatenate([before, joined], axis=1),
            jnp.concatenate([upper, lower], axis=0),
            preferred_element_type=F32,
        )
        forward += skip * joined.astype(F32)
        backward = lax.dot_general(
            jnp.concatenate([mixed, following], axis=1),
            jnp.concatenate([lower, upper], axis=1),
            ROWS_BY_ROWS,
            preferred_element_type=F32,
        )
        backward += skip * mixed.astype(F32)
        out_ref[part] = (query * forward).astype(BF16)
        query_grad_ref[part] = (scaled * forward).astype(BF16)
        key_grad_ref[part] = (backward * value).astype(BF16)
        value_grad_ref[part] = (backward * key).astype(BF16)


def outputs(keep, taps, skip, query, key, value, grad, before, following):
    channels, length = query.shape
    groups = taps.shape[0]
    steps = 2
    large = pl.BlockSpec((channels // steps, length), lambda i: (i, 0))
    skip_rows = skip.reshape(steps, channels // length // steps, length)
    return pl.pallas_call(
        functools.partial(output_kernel, channels // groups),
        grid=(steps,),
        in_specs=[
            pl.BlockSpec((1, length), lambda i: (0, 0)),
            pl.BlockSpec((groups // steps, length), lambda i: (i, 0)),
            pl.BlockSpec((1,) + skip_rows.shape[1:], lambda i: (i, 0, 0)),
        ]
        + [large] * 6,
        out_specs=[large] * 4,
        out_shape=[jax.ShapeDtypeStruct((channels, length), BF16)] * 4,
        cost_estimate=pl.CostEstimate(flops=2**28, bytes_accessed=2**24, transcendentals=0),
        compiler_params=pltpu.CompilerParams(vmem_limit_bytes=12 * 2**20),
        name="outputs",
    )(keep, taps, skip_rows, query, key, value, grad, before, following)


def row_copies(parts, part, made_refs, out_refs, sems):
    rows = made_refs[0].shape[0] // parts
    window = pl.ds(part * rows, rows)
    return [
        pltpu.make_async_copy(
            made.at[window], out.at[window], sems.at[part * len(out_refs) + side]
        )
        for side, (made, out) in enumerate(zip(made_refs, out_refs))
    ]


def pair_kernel(
    per_group, parts, keep_ref, query_ref, key_ref, value_ref, grad_ref, tap_ref, skip_ref, *refs
):
    halo_refs, out_refs, made_refs, sems = refs[:2], refs[2:6], refs[6:10], refs[10]
    cut = halo_refs[0].shape[0]
    channels, length = query_ref.shape
    groups = channels // per_group
    size = groups // parts

    def run(first):
        row, column = iotas(length, length)
        causal = column >= row
        keep = keep_ref[...].astype(F32)
        skips = skip_ref[...].T
        for group in range(groups):
            part = slice(group * per_group, (group + 1) * per_group)
            query = query_ref[part].astype(F32)
            key = key_ref[part].astype(F32)
            value = value_ref[part].astype(F32)
            scaled = grad_ref[part].astype(F32) * keep
            joined = (key * value).astype(BF16)
            mixed = (scaled * query).astype(BF16)
            if part.start < cut:
                halo = halo_refs[0][part]
            else:
                halo = halo_refs[1][part.start - cut : part.stop - cut]
            taps = jnp.broadcast_to(tap_ref[group : group + 1], (length, length))
            circle = pltpu.roll(taps, 0, 1, stride=1, stride_axis=0)
            lower = jnp.where(causal, circle, 0.0).astype(BF16)
            upper = jnp.where(causal, 0.0, circle).astype(BF16)
            start = group * per_group
            skip = skips[
                start % length : start % length + per_group, start // length : start // length + 1
            ]
            if first:
                ahead, ahead_taps = joined, lower
                back = jnp.concatenate([mixed, halo], axis=1)
                back_taps = jnp.concatenate([lower, upper], axis=1)
            else:
                ahead = jnp.concatenate([halo, joined], axis=1)
                ahead_taps = jnp.concatenate([upper, lower], axis=0)
                back, back_taps = mixed, lower
            forward = jnp.dot(ahead, ahead_taps, preferred_element_type=F32)
            forward += skip * joined.astype(F32)
            backward = lax.dot_general(back, back_taps, ROWS_BY_ROWS, preferred_element_type=F32)
            backward += skip * mixed.astype(F32)
            results = (query * forward, scaled * forward, backward * value, backward * key)
            for made, result in zip(made_refs, results):
                made[part] = result.astype(BF16)
            if (group + 1) % size == 0:
                for copy in row_copies(parts, group // size, made_refs, out_refs, sems):
                    copy.start()
        for part in range(parts):
            for copy in row_copies(parts, part, made_refs, out_refs, sems):
                copy.wait()

    first = lax.axis_index("ctx") == 0
    pl.when(first)(functools.partial(run, True))
    pl.when(jnp.logical_not(first))(functools.partial(run, False))


def pair_outputs(keep, query, key, value, grad, taps, skips, halos):
    channels, length = query.shape
    parts = 2
    arrays = (keep, query, key, value, grad, taps, skips, *halos)
    return pl.pallas_call(
        functools.partial(pair_kernel, channels // taps.shape[0], parts),
        in_specs=[pl.BlockSpec(memory_space=pltpu.VMEM)] * len(arrays),
        out_specs=[pl.BlockSpec(memory_space=pltpu.HBM)] * 4,
        out_shape=[jax.ShapeDtypeStruct((channels, length), BF16)] * 4,
        scratch_shapes=[pltpu.VMEM((channels, length), BF16)] * 4
        + [pltpu.SemaphoreType.DMA((4 * parts,))],
        cost_estimate=pl.CostEstimate(flops=2**28, bytes_accessed=2**23, transcendentals=0),
        compiler_params=pltpu.CompilerParams(vmem_limit_bytes=12 * 2**20),
        name="pair_outputs",
    )(*map(in_vmem, arrays))


def exchanges(size):
    if size == 4:
        return [(2, 3, 1, 0), (3, 2, 0, 1), (1, 0, 3, 2)]
    return [tuple((i + step) % size for i in range(size)) for step in range(1, size)]


def gather_terms(sums, axis):
    return [sums] + [
        lax.ppermute(sums, axis, list(enumerate(targets)))
        for targets in exchanges(lax.axis_size(axis))
    ]


def total_kernel(groups, tap_scale, skip_scale, axis, order, *refs):
    *term_refs, tap_ref, skip_ref = refs
    taken = [term_refs[order.index(place)][...].astype(F32) for place in range(len(term_refs))]
    size = lax.axis_size(axis)
    here = lax.axis_index(axis)
    terms = [taken[0]] * size
    for received, targets in zip(taken[1:], exchanges(size)):
        for source, target in enumerate(targets):
            if source != target:
                terms[source] = jnp.where(here == target, received, terms[source])
    total = terms[0]
    for term in terms[1:]:
        total = total + term
    tap_ref[...] = total[:groups] * tap_scale
    skip_ref[...] = total[groups:] * skip_scale


def totals(terms, groups, tap_scale, skip_scale, axis):
    rows, length = terms[0].shape
    order = list(range(len(terms)))
    return pl.pallas_call(
        functools.partial(total_kernel, groups, tap_scale, skip_scale, axis, order),
        in_specs=[pl.BlockSpec(memory_space=pltpu.VMEM)] * len(terms),
        out_shape=[
            jax.ShapeDtypeStruct((groups, length), F32),
            jax.ShapeDtypeStruct((rows - groups, length), F32),
        ],
        compiler_params=pltpu.CompilerParams(vmem_limit_bytes=12 * 2**20),
        name="totals",
    )(*(in_vmem(terms[place]) for place in order))


def body(query_act, key_act, value_act, out_grad, keep_mask, filter_taps, skip_gain):
    windows, channels, length = query_act.shape
    groups, tap_count = filter_taps.shape
    assert windows == 1 and length == tap_count
    shards = lax.axis_size("ctx")
    per_group = channels // groups
    positions = windows * lax.axis_size("dp") * length * shards
    tap_scale = 1.0 / math.sqrt(positions * per_group)
    skip_scale = 1.0 / math.sqrt(positions)
    query, key, value, grad = query_act[0], key_act[0], value_act[0], out_grad[0]
    if shards == 2:
        swap = [(0, 1), (1, 0)]
        own = own_block(keep_mask, query, key, value, grad)
        halo = [lax.ppermute(part, "ctx", swap) for part in own]
        skips = skip_gain.reshape(channels // length, length)
        mine, *near = local_sums(
            groups, BF16, keep_mask, query, key, value, grad, filter_taps, skips
        )
        other = lax.ppermute(mine, "ctx", swap)
        crossed = cross_sums(own[0], halo[0], groups * 3 // 4, True)
        sums = last_sums(per_group, own[1], halo[1], crossed, mine, other)
        terms = gather_terms(sums, "dp")
        results = pair_outputs(*near, halo)
    else:
        joined = (key.astype(F32) * value.astype(F32)).astype(BF16)
        own = (grad.astype(F32) * keep_mask.astype(F32) * query.astype(F32)).astype(BF16)
        before = lax.ppermute(joined, "ctx", [(i, i + 1) for i in range(shards - 1)])
        following = lax.ppermute(own, "ctx", [(i + 1, i) for i in range(shards - 1)])
        mine, *_ = local_sums(groups, F32, keep_mask, query, key, value, grad)
        crossed = cross_sums(own, before, groups, False)
        sums = lax.psum(mine.at[:groups].add(crossed), "ctx")
        terms = gather_terms(sums, "dp")
        results = outputs(keep_mask, filter_taps, skip_gain, query, key, value, grad, before, following)
    filter_grad, skip_grad = totals(terms, groups, tap_scale, skip_scale, "dp")
    return (*(result[None] for result in results), filter_grad, skip_grad.reshape(channels))


def solution(mesh):
    large = P("dp", "tp", "ctx")
    return jax.shard_map(
        body,
        mesh=mesh,
        in_specs=(large, large, large, large, P("dp", "ctx"), P("tp", None), P("tp")),
        out_specs=(large, large, large, large, P("tp", None), P("tp")),
        check_vma=False,
    )
```

```python
import functools
import math

import jax
import jax.numpy as jnp
from jax import lax
from jax.experimental import pallas as pl
from jax.experimental.pallas import tpu as pltpu
from jax.sharding import PartitionSpec as P

BF16 = jnp.bfloat16
F32 = jnp.float32
PARTS = 2
ROWS_BY_ROWS = (((1,), (1,)), ((), ()))


def in_hbm(array):
    return pltpu.with_memory_space_constraint(array, pltpu.HBM)


def in_vmem(array):
    return pltpu.with_memory_space_constraint(array, pltpu.VMEM)


def iotas(rows, columns):
    return (
        lax.broadcasted_iota(jnp.int32, (rows, columns), 0),
        lax.broadcasted_iota(jnp.int32, (rows, columns), 1),
    )


def flip(block):
    length = block.shape[1]
    row, column = iotas(length, length)
    mirror = (row + column == length - 1).astype(F32).astype(BF16)
    return jnp.dot(block, mirror, preferred_element_type=F32).astype(BF16)


def lag_sums(grad, joined, per_group, crossing):
    channels, length = grad.shape
    per = length // per_group
    phases = 4
    span = length // phases
    row, column = iotas(span, length)
    near = row + column >= span - 1
    lane = iotas(1, length)[1]
    owner = iotas(1, phases * length)[1] % length // per_group
    nothing = jnp.zeros((), BF16)
    mirrored = flip(joined)
    sums = []
    for start in range(0, channels, length):
        across = grad[start : start + length].T
        block = mirrored[start : start + length].astype(F32)
        left, right = [], []
        for phase in range(phases):
            left.append(across[phase * span : (phase + 1) * span])
            shift = span * (phase + 1)
            turned = (block if shift == length else pltpu.roll(block, shift, 1)).astype(BF16)
            if crossing:
                earlier = jnp.where(lane >= shift, turned, nothing)
                right.append(jnp.concatenate([earlier, turned], axis=1))
            else:
                right.append(jnp.where(lane < shift, turned, nothing))
        left = jnp.concatenate(left, axis=1)
        left = jnp.concatenate([jnp.where(owner == g, left, nothing) for g in range(per)], axis=0)
        grams = jnp.dot(left, jnp.concatenate(right, axis=0), preferred_element_type=F32)
        for g in range(per):
            gram = grams[g * span : (g + 1) * span]
            gram = jnp.where(near, gram[:, :length], gram[:, length:] if crossing else 0.0)
            turned = pltpu.roll(gram, 0, 1, stride=1, stride_axis=0)
            sums.append(jnp.sum(turned, axis=0, keepdims=True))
    return pltpu.roll(jnp.concatenate(sums, axis=0), length - span + 1, 1)


def own_kernel(*refs):
    sources, own_ref, held, sems = refs[:7], refs[7], refs[8:15], refs[15]
    first = lax.axis_index("ctx") == 0
    keep_ref = held[0]
    channels = own_ref.shape[0]

    def run(one, two, others, masked):
        copies = {
            (index, part): pltpu.make_async_copy(
                sources[index].at[pl.ds(part * channels // PARTS, channels // PARTS)],
                held[index].at[pl.ds(part * channels // PARTS, channels // PARTS)],
                sems.at[index * PARTS + part],
            )
            for index in (one, two)
            for part in range(PARTS)
        }
        for index in (0, *others):
            copies[index, 0] = pltpu.make_async_copy(
                sources[index], held[index], sems.at[index * PARTS]
            )
        copies[0, 0].start()
        for part in range(PARTS):
            copies[one, part].start()
            copies[two, part].start()
        for index in others:
            copies[index, 0].start()
        copies[0, 0].wait()
        for part in range(PARTS):
            copies[one, part].wait()
            copies[two, part].wait()
            window = pl.ds(part * channels // PARTS, channels // PARTS)
            scaled = held[two][window].astype(F32)
            if masked:
                scaled = scaled * keep_ref[...].astype(F32)
            own_ref[window] = (scaled * held[one][window].astype(F32)).astype(BF16)
        for index in others:
            copies[index, 0].wait()

    pl.when(first)(functools.partial(run, 2, 3, (1, 4, 5, 6), False))
    pl.when(jnp.logical_not(first))(functools.partial(run, 1, 4, (2, 3, 5, 6), True))


def own_block(*sources):
    whole = pl.BlockSpec(memory_space=pltpu.VMEM)
    return pl.pallas_call(
        own_kernel,
        in_specs=[pl.BlockSpec(memory_space=pltpu.HBM)] * 7,
        out_specs=[whole] * 8,
        out_shape=[pltpu.VMEM(sources[1].shape, BF16)]
        + [pltpu.VMEM(source.shape, source.dtype) for source in sources],
        scratch_shapes=[pltpu.SemaphoreType.DMA((7 * PARTS,))],
        compiler_params=pltpu.CompilerParams(vmem_limit_bytes=12 * 2**20),
        name="own_block",
    )(*map(in_hbm, sources))


def local_kernel(per_group, turn, *refs):
    held, sums_ref = refs[:7], refs[7 if turn != 1 else 8]
    sum_local = functools.partial(local_part, per_group, held, sums_ref)
    if turn is None:
        sum_local()
        return

    @pl.when(lax.axis_index("tp") % 2 == 1 - turn)
    def _():
        sum_local()
        if turn == 0:
            filters(per_group, held, None, refs[8:12], refs[12:14], refs[14], "free")


def local_part(per_group, held, sums_ref):
    keep_ref, query_ref, key_ref, value_ref, grad_ref = held[:5]
    channels, length = query_ref.shape
    groups = channels // per_group
    joined = (key_ref[...].astype(F32) * value_ref[...].astype(F32)).astype(BF16)
    scaled = grad_ref[...].astype(F32) * keep_ref[...].astype(F32)
    mixed = (scaled * query_ref[...].astype(F32)).astype(BF16)
    sums_ref[:groups] = lag_sums(mixed, joined, per_group, False).astype(sums_ref.dtype)
    both = joined.astype(F32) * mixed.astype(F32)
    high = both.astype(BF16)
    low = (both - high.astype(F32)).astype(BF16)
    ones = jnp.ones((8, length), BF16)
    direct = lax.dot_general(ones, high, ROWS_BY_ROWS, preferred_element_type=F32)
    direct += lax.dot_general(ones, low, ROWS_BY_ROWS, preferred_element_type=F32)
    for block in range(channels // length):
        sums_ref[groups + block : groups + block + 1] = direct[
            :1, block * length : (block + 1) * length
        ].astype(sums_ref.dtype)


def local_sums(groups, dtype, held, turn=None, made=()):
    channels, length = held[1].shape
    whole = pl.BlockSpec(memory_space=pltpu.VMEM)
    free = turn == 0
    return pl.pallas_call(
        functools.partial(local_kernel, channels // groups, turn),
        in_specs=[whole] * (7 + len(made)),
        out_specs=[whole] + [pl.BlockSpec(memory_space=pltpu.HBM)] * (4 * free),
        out_shape=[pltpu.VMEM((groups + channels // length, length), dtype)]
        + [jax.ShapeDtypeStruct((channels, length), BF16)] * (4 * free),
        input_output_aliases={7 + index: index for index in range(len(made))},
        scratch_shapes=[pltpu.VMEM((channels, length), BF16)] * (2 * free)
        + [pltpu.SemaphoreType.DMA((2 * PARTS,))] * free,
        cost_estimate=pl.CostEstimate(flops=2**26, bytes_accessed=2**23, transcendentals=0),
        compiler_params=pltpu.CompilerParams(vmem_limit_bytes=12 * 2**20),
        name="local_sums",
    )(*map(in_vmem, (*held, *made)))


def by_role(own, halo):
    first = lax.axis_index("ctx") == 0
    return jnp.where(first, halo, own), jnp.where(first, own, halo)


def cross_kernel(per_group, swap, own_ref, halo_ref, sums_ref):
    grad, joined = own_ref[...], halo_ref[...]
    if swap:
        grad, joined = by_role(grad, joined)
    sums_ref[...] = lag_sums(grad, joined, per_group, True)


def cross_sums(own, halo, groups, swap):
    channels, length = own.shape
    whole = pl.BlockSpec(memory_space=pltpu.VMEM)
    return pl.pallas_call(
        functools.partial(cross_kernel, channels // groups, swap),
        in_specs=[whole] * 2,
        out_specs=whole,
        out_shape=pltpu.VMEM((groups, length), F32),
        cost_estimate=pl.CostEstimate(flops=2**26, bytes_accessed=2**23, transcendentals=0),
        compiler_params=pltpu.CompilerParams(vmem_limit_bytes=12 * 2**20),
        name="cross_sums",
    )(in_vmem(own), in_vmem(halo))


def output_kernel(
    per_group, keep_ref, tap_ref, skip_ref, query_ref, key_ref, value_ref, grad_ref,
    before_ref, following_ref, out_ref, query_grad_ref, key_grad_ref, value_grad_ref,
):
    channels, length = query_ref.shape
    row, column = iotas(length, length)
    causal = column >= row
    keep = keep_ref[...].astype(F32)
    skips = skip_ref[0].T
    for group in range(channels // per_group):
        part = slice(group * per_group, (group + 1) * per_group)
        query = query_ref[part].astype(F32)
        key = key_ref[part].astype(F32)
        value = value_ref[part].astype(F32)
        scaled = grad_ref[part].astype(F32) * keep
        joined = (key * value).astype(BF16)
        mixed = (scaled * query).astype(BF16)
        before, following = before_ref[part], following_ref[part]
        taps = jnp.broadcast_to(tap_ref[group : group + 1], (length, length))
        circle = pltpu.roll(taps, 0, 1, stride=1, stride_axis=0)
        lower = jnp.where(causal, circle, 0.0).astype(BF16)
        upper = jnp.where(causal, 0.0, circle).astype(BF16)
        start = group * per_group
        skip = skips[start % length : start % length + per_group, start // length : start // length + 1]
        forward = jnp.dot(
            jnp.concatenate([before, joined], axis=1),
            jnp.concatenate([upper, lower], axis=0),
            preferred_element_type=F32,
        )
        forward += skip * joined.astype(F32)
        backward = lax.dot_general(
            jnp.concatenate([mixed, following], axis=1),
            jnp.concatenate([lower, upper], axis=1),
            ROWS_BY_ROWS,
            preferred_element_type=F32,
        )
        backward += skip * mixed.astype(F32)
        out_ref[part] = (query * forward).astype(BF16)
        query_grad_ref[part] = (scaled * forward).astype(BF16)
        key_grad_ref[part] = (backward * value).astype(BF16)
        value_grad_ref[part] = (backward * key).astype(BF16)


def outputs(keep, taps, skip, query, key, value, grad, before, following):
    channels, length = query.shape
    groups = taps.shape[0]
    steps = 2
    large = pl.BlockSpec((channels // steps, length), lambda i: (i, 0))
    skip_rows = skip.reshape(steps, channels // length // steps, length)
    return pl.pallas_call(
        functools.partial(output_kernel, channels // groups),
        grid=(steps,),
        in_specs=[
            pl.BlockSpec((1, length), lambda i: (0, 0)),
            pl.BlockSpec((groups // steps, length), lambda i: (i, 0)),
            pl.BlockSpec((1,) + skip_rows.shape[1:], lambda i: (i, 0, 0)),
        ]
        + [large] * 6,
        out_specs=[large] * 4,
        out_shape=[jax.ShapeDtypeStruct((channels, length), BF16)] * 4,
        cost_estimate=pl.CostEstimate(flops=2**28, bytes_accessed=2**24, transcendentals=0),
        compiler_params=pltpu.CompilerParams(vmem_limit_bytes=12 * 2**20),
        name="outputs",
    )(keep, taps, skip_rows, query, key, value, grad, before, following)


def row_copies(part, made_refs, out_refs, sems):
    rows = made_refs[0].shape[0] // PARTS
    window = pl.ds(part * rows, rows)
    return [
        pltpu.make_async_copy(
            made.at[window], out.at[window], sems.at[part * len(out_refs) + side]
        )
        for side, (made, out) in enumerate(zip(made_refs, out_refs))
    ]


def filters(per_group, held, halo_ref, out_refs, made_refs, sems, chosen):
    first = lax.axis_index("ctx") == 0
    for here, place in ((True, first), (False, jnp.logical_not(first))):
        forward = chosen == "all" or (chosen == "free") == here
        backward = chosen == "all" or (chosen == "free") != here
        pl.when(place)(
            functools.partial(
                filter_groups, per_group, held, halo_ref, out_refs, made_refs, sems, here, forward, backward
            )
        )


def filter_groups(per_group, held, halo_ref, out_refs, made_refs, sems, first, forward, backward):
    keep_ref, query_ref, key_ref, value_ref, grad_ref, tap_ref, skip_ref = held
    out_refs = out_refs[0 if forward else 2 : 4 if backward else 2]
    made_refs = made_refs[: len(out_refs)]
    channels, length = query_ref.shape
    groups = channels // per_group
    size = groups // PARTS
    row, column = iotas(length, length)
    causal = column >= row
    keep = keep_ref[...].astype(F32)
    skips = skip_ref[...].T
    for group in range(groups):
        start = group * per_group
        part = slice(start, start + per_group)
        query = query_ref[part].astype(F32)
        key = key_ref[part].astype(F32)
        value = value_ref[part].astype(F32)
        scaled = grad_ref[part].astype(F32) * keep
        joined = (key * value).astype(BF16)
        mixed = (scaled * query).astype(BF16)
        taps = jnp.broadcast_to(tap_ref[group : group + 1], (length, length))
        circle = pltpu.roll(taps, 0, 1, stride=1, stride_axis=0)
        lower = jnp.where(causal, circle, 0.0).astype(BF16)
        upper = jnp.where(causal, 0.0, circle).astype(BF16)
        skip = skips[
            start % length : start % length + per_group, start // length : start // length + 1
        ]
        if halo_ref is not None:
            halo = halo_ref[part]
        results = []
        if forward:
            source, matrix = joined, lower
            if not first:
                source = jnp.concatenate([halo, joined], axis=1)
                matrix = jnp.concatenate([upper, lower], axis=0)
            mixed_sum = jnp.dot(source, matrix, preferred_element_type=F32)
            mixed_sum += skip * joined.astype(F32)
            results += [query * mixed_sum, scaled * mixed_sum]
        if backward:
            source, matrix = mixed, lower
            if first:
                source = jnp.concatenate([mixed, halo], axis=1)
                matrix = jnp.concatenate([lower, upper], axis=1)
            joined_grad = lax.dot_general(source, matrix, ROWS_BY_ROWS, preferred_element_type=F32)
            joined_grad += skip * mixed.astype(F32)
            results += [joined_grad * value, joined_grad * key]
        for made, result in zip(made_refs, results):
            made[part] = result.astype(BF16)
        if (group + 1) % size == 0:
            for copy in row_copies(group // size, made_refs, out_refs, sems):
                copy.start()
    for part in range(PARTS):
        for copy in row_copies(part, made_refs, out_refs, sems):
            copy.wait()


def pair_kernel(per_group, *refs):
    held, halo_ref, out_refs = refs[:7], refs[7], refs[12:16]
    made_refs, sems = refs[16:20], refs[20]
    even = lax.axis_index("tp") % 2 == 0
    rest = (per_group, held, halo_ref, out_refs, made_refs, sems)
    pl.when(even)(functools.partial(filters, *rest, "all"))
    pl.when(jnp.logical_not(even))(functools.partial(filters, *rest, "bound"))


def pair_outputs(held, halo, results):
    channels, length = held[1].shape
    hbm = pl.BlockSpec(memory_space=pltpu.HBM)
    return pl.pallas_call(
        functools.partial(pair_kernel, channels // held[5].shape[0]),
        in_specs=[pl.BlockSpec(memory_space=pltpu.VMEM)] * 8 + [hbm] * 4,
        out_specs=[hbm] * 4,
        out_shape=[jax.ShapeDtypeStruct((channels, length), BF16)] * 4,
        input_output_aliases={8: 0, 9: 1, 10: 2, 11: 3},
        scratch_shapes=[pltpu.VMEM((channels, length), BF16)] * 4
        + [pltpu.SemaphoreType.DMA((4 * PARTS,))],
        cost_estimate=pl.CostEstimate(flops=2**28, bytes_accessed=2**23, transcendentals=0),
        compiler_params=pltpu.CompilerParams(vmem_limit_bytes=12 * 2**20),
        name="pair_outputs",
    )(*map(in_vmem, (*held, halo)), *results)


def exchanges(size):
    if size == 4:
        return [(2, 3, 1, 0), (3, 2, 0, 1), (1, 0, 3, 2)]
    return [tuple((i + step) % size for i in range(size)) for step in range(1, size)]


def gather_terms(sums, axis):
    return [sums] + [
        lax.ppermute(sums, axis, list(enumerate(targets)))
        for targets in exchanges(lax.axis_size(axis))
    ]


def total_kernel(groups, tap_scale, skip_scale, axis, order, *refs):
    *term_refs, tap_ref, skip_ref = refs
    taken = [term_refs[order.index(place)][...].astype(F32) for place in range(len(term_refs))]
    size = lax.axis_size(axis)
    here = lax.axis_index(axis)
    terms = [taken[0]] * size
    for received, targets in zip(taken[1:], exchanges(size)):
        for source, target in enumerate(targets):
            if source != target:
                terms[source] = jnp.where(here == target, received, terms[source])
    total = terms[0]
    for term in terms[1:]:
        total = total + term
    tap_ref[...] = total[:groups] * tap_scale
    skip_ref[...] = total[groups:] * skip_scale


def totals(terms, groups, tap_scale, skip_scale, axis):
    rows, length = terms[0].shape
    order = list(range(len(terms)))
    return pl.pallas_call(
        functools.partial(total_kernel, groups, tap_scale, skip_scale, axis, order),
        in_specs=[pl.BlockSpec(memory_space=pltpu.VMEM)] * len(terms),
        out_shape=[
            jax.ShapeDtypeStruct((groups, length), F32),
            jax.ShapeDtypeStruct((rows - groups, length), F32),
        ],
        compiler_params=pltpu.CompilerParams(vmem_limit_bytes=12 * 2**20),
        name="totals",
    )(*(in_vmem(terms[place]) for place in order))


def body(query_act, key_act, value_act, out_grad, keep_mask, filter_taps, skip_gain):
    windows, channels, length = query_act.shape
    groups, tap_count = filter_taps.shape
    assert windows == 1 and length == tap_count
    shards = lax.axis_size("ctx")
    per_group = channels // groups
    positions = windows * lax.axis_size("dp") * length * shards
    tap_scale = 1.0 / math.sqrt(positions * per_group)
    skip_scale = 1.0 / math.sqrt(positions)
    query, key, value, grad = query_act[0], key_act[0], value_act[0], out_grad[0]
    if shards == 2:
        swap = [(0, 1), (1, 0)]
        skips = skip_gain.reshape(channels // length, length)
        own, *held = own_block(keep_mask, query, key, value, grad, filter_taps, skips)
        mine, *free = local_sums(groups, BF16, held, 0)
        own, mine = lax.optimization_barrier((own, mine))
        halo = lax.ppermute(own, "ctx", swap)
        (mine,) = local_sums(groups, BF16, held, 1, (mine,))
        other = lax.ppermute(mine, "ctx", swap)
        crossed = cross_sums(own, halo, groups, True)
        sums = mine.astype(F32).at[:groups].add(crossed) + other.astype(F32)
        sums = lax.reduce_precision(sums, 8, 7).astype(BF16)
        terms = gather_terms(sums, "dp")
        results = pair_outputs(held, halo, free)
    else:
        joined = (key.astype(F32) * value.astype(F32)).astype(BF16)
        own = (grad.astype(F32) * keep_mask.astype(F32) * query.astype(F32)).astype(BF16)
        before = lax.ppermute(joined, "ctx", [(i, i + 1) for i in range(shards - 1)])
        following = lax.ppermute(own, "ctx", [(i + 1, i) for i in range(shards - 1)])
        skips = skip_gain.reshape(channels // length, length)
        sources = (keep_mask, query, key, value, grad, filter_taps, skips)
        (mine,) = local_sums(groups, F32, sources)
        crossed = cross_sums(own, before, groups, False)
        sums = lax.psum(mine.at[:groups].add(crossed), "ctx")
        terms = gather_terms(sums, "dp")
        results = outputs(keep_mask, filter_taps, skip_gain, query, key, value, grad, before, following)
    filter_grad, skip_grad = totals(terms, groups, tap_scale, skip_scale, "dp")
    return (*(result[None] for result in results), filter_grad, skip_grad.reshape(channels))


def solution(mesh):
    large = P("dp", "tp", "ctx")
    return jax.shard_map(
        body,
        mesh=mesh,
        in_specs=(large, large, large, large, P("dp", "ctx"), P("tp", None), P("tp")),
        out_specs=(large, large, large, large, P("tp", None), P("tp")),
        check_vma=False,
    )
```

```python
import functools
import math

import jax
import jax.numpy as jnp
from jax import lax
from jax.experimental import pallas as pl
from jax.experimental.pallas import tpu as pltpu
from jax.sharding import PartitionSpec as P

BF16 = jnp.bfloat16
F32 = jnp.float32
PARTS = 2
ROWS_BY_ROWS = (((1,), (1,)), ((), ()))


def in_hbm(array):
    return pltpu.with_memory_space_constraint(array, pltpu.HBM)


def in_vmem(array):
    return pltpu.with_memory_space_constraint(array, pltpu.VMEM)


def iotas(rows, columns):
    return (
        lax.broadcasted_iota(jnp.int32, (rows, columns), 0),
        lax.broadcasted_iota(jnp.int32, (rows, columns), 1),
    )


def flip(block):
    length = block.shape[1]
    row, column = iotas(length, length)
    mirror = (row + column == length - 1).astype(F32).astype(BF16)
    return jnp.dot(block, mirror, preferred_element_type=F32).astype(BF16)


def lag_sums(grad, joined, per_group, crossing):
    channels, length = grad.shape
    per = length // per_group
    phases = 4
    span = length // phases
    row, column = iotas(span, length)
    near = row + column >= span - 1
    lane = iotas(1, length)[1]
    owner = iotas(1, phases * length)[1] % length // per_group
    nothing = jnp.zeros((), BF16)
    mirrored = flip(joined)
    sums = []
    for start in range(0, channels, length):
        across = grad[start : start + length].T
        block = mirrored[start : start + length].astype(F32)
        left, right = [], []
        for phase in range(phases):
            left.append(across[phase * span : (phase + 1) * span])
            shift = span * (phase + 1)
            turned = (block if shift == length else pltpu.roll(block, shift, 1)).astype(BF16)
            if crossing:
                earlier = jnp.where(lane >= shift, turned, nothing)
                right.append(jnp.concatenate([earlier, turned], axis=1))
            else:
                right.append(jnp.where(lane < shift, turned, nothing))
        left = jnp.concatenate(left, axis=1)
        left = jnp.concatenate([jnp.where(owner == g, left, nothing) for g in range(per)], axis=0)
        grams = jnp.dot(left, jnp.concatenate(right, axis=0), preferred_element_type=F32)
        for g in range(per):
            gram = grams[g * span : (g + 1) * span]
            gram = jnp.where(near, gram[:, :length], gram[:, length:] if crossing else 0.0)
            turned = pltpu.roll(gram, 0, 1, stride=1, stride_axis=0)
            sums.append(jnp.sum(turned, axis=0, keepdims=True))
    return pltpu.roll(jnp.concatenate(sums, axis=0), length - span + 1, 1)


def own_kernel(*refs):
    sources, own_ref, held, sems = refs[:5], refs[5], refs[6:13], refs[13]
    first = lax.axis_index("ctx") == 0
    channels = own_ref.shape[0]
    rows = channels // PARTS

    def run(one, two, masked):
        def copies_of(part):
            window = pl.ds(part * rows, rows)
            return [
                pltpu.make_async_copy(
                    sources[index].at[window], held[index].at[window], sems.at[2 * part + side]
                )
                for side, index in enumerate((one, two))
            ]

        keep_copy = pltpu.make_async_copy(sources[0], held[0], sems.at[2 * PARTS])
        keep_copy.start()
        for part in range(PARTS):
            for copy in copies_of(part):
                copy.start()
        keep_copy.wait()
        for part in range(PARTS):
            for copy in copies_of(part):
                copy.wait()
            window = pl.ds(part * rows, rows)
            scaled = held[two][window].astype(F32)
            if masked:
                scaled = scaled * held[0][...].astype(F32)
            own_ref[window] = (scaled * held[one][window].astype(F32)).astype(BF16)

    pl.when(first)(functools.partial(run, 2, 3, False))
    pl.when(jnp.logical_not(first))(functools.partial(run, 1, 4, True))


def own_block(*sources):
    whole = pl.BlockSpec(memory_space=pltpu.VMEM)
    return pl.pallas_call(
        own_kernel,
        in_specs=[pl.BlockSpec(memory_space=pltpu.HBM)] * 5,
        out_specs=[whole] * 8,
        out_shape=[pltpu.VMEM(sources[1].shape, BF16)]
        + [pltpu.VMEM(source.shape, source.dtype) for source in sources],
        scratch_shapes=[pltpu.SemaphoreType.DMA((2 * PARTS + 1,))],
        compiler_params=pltpu.CompilerParams(vmem_limit_bytes=12 * 2**20),
        name="own_block",
    )(*map(in_hbm, sources[:5]))


def turn_kernel(per_group, turn, *refs):
    sources = refs[:6]
    if turn == 0:
        held, sums_ref, out_refs = refs[13:20], refs[20], refs[21:25]
        sems, made_refs, out_sems = refs[25], refs[26:28], refs[28]
    else:
        held, sums_ref, sems = refs[14:21], refs[21], refs[22]
    query, key, value, grad, taps, skips = zip(sources, held[1:])

    def load(*pairs):
        return [
            pltpu.make_async_copy(source, target, sems.at[index])
            for index, (source, target) in enumerate(pairs)
        ]

    @pl.when(lax.axis_index("tp") % 2 == 1 - turn)
    def _():
        first = lax.axis_index("ctx") == 0

        @pl.when(first)
        def _():
            for copy in load(query, grad, taps, skips):
                copy.start()

        @pl.when(jnp.logical_not(first))
        def _():
            for copy in load(key, value, taps, skips):
                copy.start()

        for copy in load(key, value, taps, skips):
            copy.wait()
        local_part(per_group, held, sums_ref)
        if turn == 0:
            bounds = (0, 3 * held[5].shape[0] // 8, 3 * held[5].shape[0] // 4)
            filters(per_group, held, None, out_refs, made_refs, out_sems, [("free", bounds)])


def turn_sums(turn, sources, held, made=()):
    channels, length = held[1].shape
    groups = held[5].shape[0]
    whole = pl.BlockSpec(memory_space=pltpu.VMEM)
    hbm = pl.BlockSpec(memory_space=pltpu.HBM)
    free = turn == 0
    given = (*held, *made)
    return pl.pallas_call(
        functools.partial(turn_kernel, channels // groups, turn),
        in_specs=[hbm] * 6 + [whole] * len(given),
        out_specs=[whole] * 8 + [hbm] * (4 * free),
        out_shape=[pltpu.VMEM(array.shape, array.dtype) for array in held]
        + [pltpu.VMEM((groups + channels // length, length), BF16)]
        + [jax.ShapeDtypeStruct((channels, length), BF16)] * (4 * free),
        input_output_aliases={6 + index: index for index in range(len(given))},
        scratch_shapes=[pltpu.SemaphoreType.DMA((4,))]
        + [pltpu.VMEM((channels, length), BF16)] * (2 * free)
        + [pltpu.SemaphoreType.DMA((8,))] * free,
        cost_estimate=pl.CostEstimate(flops=2**26, bytes_accessed=2**23, transcendentals=0),
        compiler_params=pltpu.CompilerParams(vmem_limit_bytes=12 * 2**20),
        name="turn_sums",
    )(*map(in_hbm, sources[1:]), *map(in_vmem, given))


def local_kernel(per_group, *refs):
    local_part(per_group, refs[:5], refs[5])


def local_part(per_group, held, sums_ref):
    keep_ref, query_ref, key_ref, value_ref, grad_ref = held[:5]
    channels, length = query_ref.shape
    groups = channels // per_group
    joined = (key_ref[...].astype(F32) * value_ref[...].astype(F32)).astype(BF16)
    scaled = grad_ref[...].astype(F32) * keep_ref[...].astype(F32)
    mixed = (scaled * query_ref[...].astype(F32)).astype(BF16)
    sums_ref[:groups] = lag_sums(mixed, joined, per_group, False).astype(sums_ref.dtype)
    both = joined.astype(F32) * mixed.astype(F32)
    high = both.astype(BF16)
    low = (both - high.astype(F32)).astype(BF16)
    ones = jnp.ones((8, length), BF16)
    direct = lax.dot_general(ones, high, ROWS_BY_ROWS, preferred_element_type=F32)
    direct += lax.dot_general(ones, low, ROWS_BY_ROWS, preferred_element_type=F32)
    for block in range(channels // length):
        sums_ref[groups + block : groups + block + 1] = direct[
            :1, block * length : (block + 1) * length
        ].astype(sums_ref.dtype)


def local_sums(groups, *arrays):
    channels, length = arrays[1].shape
    return pl.pallas_call(
        functools.partial(local_kernel, channels // groups),
        out_shape=jax.ShapeDtypeStruct((groups + channels // length, length), F32),
        cost_estimate=pl.CostEstimate(flops=2**26, bytes_accessed=2**23, transcendentals=0),
        name="local_sums",
    )(*arrays)


def by_role(own, halo):
    first = lax.axis_index("ctx") == 0
    return jnp.where(first, halo, own), jnp.where(first, own, halo)


def cross_kernel(per_group, swap, own_ref, halo_ref, sums_ref):
    grad, joined = own_ref[...], halo_ref[...]
    if swap:
        grad, joined = by_role(grad, joined)
    sums_ref[...] = lag_sums(grad, joined, per_group, True)


def cross_sums(own, halo, groups, swap):
    channels, length = own.shape
    whole = pl.BlockSpec(memory_space=pltpu.VMEM)
    return pl.pallas_call(
        functools.partial(cross_kernel, channels // groups, swap),
        in_specs=[whole] * 2,
        out_specs=whole,
        out_shape=pltpu.VMEM((groups, length), F32),
        cost_estimate=pl.CostEstimate(flops=2**26, bytes_accessed=2**23, transcendentals=0),
        compiler_params=pltpu.CompilerParams(vmem_limit_bytes=12 * 2**20),
        name="cross_sums",
    )(in_vmem(own), in_vmem(halo))


def output_kernel(
    per_group, keep_ref, tap_ref, skip_ref, query_ref, key_ref, value_ref, grad_ref,
    before_ref, following_ref, out_ref, query_grad_ref, key_grad_ref, value_grad_ref,
):
    channels, length = query_ref.shape
    row, column = iotas(length, length)
    causal = column >= row
    keep = keep_ref[...].astype(F32)
    skips = skip_ref[0].T
    for group in range(channels // per_group):
        part = slice(group * per_group, (group + 1) * per_group)
        query = query_ref[part].astype(F32)
        key = key_ref[part].astype(F32)
        value = value_ref[part].astype(F32)
        scaled = grad_ref[part].astype(F32) * keep
        joined = (key * value).astype(BF16)
        mixed = (scaled * query).astype(BF16)
        before, following = before_ref[part], following_ref[part]
        taps = jnp.broadcast_to(tap_ref[group : group + 1], (length, length))
        circle = pltpu.roll(taps, 0, 1, stride=1, stride_axis=0)
        lower = jnp.where(causal, circle, 0.0).astype(BF16)
        upper = jnp.where(causal, 0.0, circle).astype(BF16)
        start = group * per_group
        skip = skips[start % length : start % length + per_group, start // length : start // length + 1]
        forward = jnp.dot(
            jnp.concatenate([before, joined], axis=1),
            jnp.concatenate([upper, lower], axis=0),
            preferred_element_type=F32,
        )
        forward += skip * joined.astype(F32)
        backward = lax.dot_general(
            jnp.concatenate([mixed, following], axis=1),
            jnp.concatenate([lower, upper], axis=1),
            ROWS_BY_ROWS,
            preferred_element_type=F32,
        )
        backward += skip * mixed.astype(F32)
        out_ref[part] = (query * forward).astype(BF16)
        query_grad_ref[part] = (scaled * forward).astype(BF16)
        key_grad_ref[part] = (backward * value).astype(BF16)
        value_grad_ref[part] = (backward * key).astype(BF16)


def outputs(keep, taps, skip, query, key, value, grad, before, following):
    channels, length = query.shape
    groups = taps.shape[0]
    steps = 2
    large = pl.BlockSpec((channels // steps, length), lambda i: (i, 0))
    skip_rows = skip.reshape(steps, channels // length // steps, length)
    return pl.pallas_call(
        functools.partial(output_kernel, channels // groups),
        grid=(steps,),
        in_specs=[
            pl.BlockSpec((1, length), lambda i: (0, 0)),
            pl.BlockSpec((groups // steps, length), lambda i: (i, 0)),
            pl.BlockSpec((1,) + skip_rows.shape[1:], lambda i: (i, 0, 0)),
        ]
        + [large] * 6,
        out_specs=[large] * 4,
        out_shape=[jax.ShapeDtypeStruct((channels, length), BF16)] * 4,
        cost_estimate=pl.CostEstimate(flops=2**28, bytes_accessed=2**24, transcendentals=0),
        compiler_params=pltpu.CompilerParams(vmem_limit_bytes=12 * 2**20),
        name="outputs",
    )(keep, taps, skip_rows, query, key, value, grad, before, following)


def filters(per_group, held, halo_ref, out_refs, made_refs, sems, tasks):
    first = lax.axis_index("ctx") == 0

    def run(here):
        copies = []
        for index, (chosen, bounds) in enumerate(tasks):
            forward = chosen == "all" or (chosen == "free") == here
            backward = chosen == "all" or (chosen == "free") != here
            copies += filter_groups(
                per_group, held, halo_ref, out_refs, made_refs, sems, here, forward, backward, bounds, 8 * index
            )
        for copy in copies:
            copy.wait()

    pl.when(first)(functools.partial(run, True))
    pl.when(jnp.logical_not(first))(functools.partial(run, False))


def filter_groups(
    per_group, held, halo_ref, out_refs, made_refs, sems, first, forward, backward, bounds, sem
):
    keep_ref, query_ref, key_ref, value_ref, grad_ref, tap_ref, skip_ref = held
    out_refs = out_refs[0 if forward else 2 : 4 if backward else 2]
    made_refs = made_refs[: len(out_refs)]
    length = query_ref.shape[1]
    row, column = iotas(length, length)
    causal = column >= row
    keep = keep_ref[...].astype(F32)
    skips = skip_ref[...].T
    copies = []
    for group in range(bounds[0], bounds[-1]):
        start = group * per_group
        part = slice(start, start + per_group)
        query = query_ref[part].astype(F32)
        key = key_ref[part].astype(F32)
        value = value_ref[part].astype(F32)
        scaled = grad_ref[part].astype(F32) * keep
        joined = (key * value).astype(BF16)
        mixed = (scaled * query).astype(BF16)
        taps = jnp.broadcast_to(tap_ref[group : group + 1], (length, length))
        circle = pltpu.roll(taps, 0, 1, stride=1, stride_axis=0)
        lower = jnp.where(causal, circle, 0.0).astype(BF16)
        upper = jnp.where(causal, 0.0, circle).astype(BF16)
        skip = skips[
            start % length : start % length + per_group, start // length : start // length + 1
        ]
        if halo_ref is not None:
            halo = halo_ref[part]
        results = []
        if forward:
            source, matrix = joined, lower
            if not first:
                source = jnp.concatenate([halo, joined], axis=1)
                matrix = jnp.concatenate([upper, lower], axis=0)
            mixed_sum = jnp.dot(source, matrix, preferred_element_type=F32)
            mixed_sum += skip * joined.astype(F32)
            results += [query * mixed_sum, scaled * mixed_sum]
        if backward:
            source, matrix = mixed, lower
            if first:
                source = jnp.concatenate([mixed, halo], axis=1)
                matrix = jnp.concatenate([lower, upper], axis=1)
            joined_grad = lax.dot_general(source, matrix, ROWS_BY_ROWS, preferred_element_type=F32)
            joined_grad += skip * mixed.astype(F32)
            results += [joined_grad * value, joined_grad * key]
        for made, result in zip(made_refs, results):
            made[part] = result.astype(BF16)
        if group + 1 in bounds:
            begin = bounds[bounds.index(group + 1) - 1] * per_group
            window = pl.ds(begin, start + per_group - begin)
            for made, out in zip(made_refs, out_refs):
                copies.append(
                    pltpu.make_async_copy(made.at[window], out.at[window], sems.at[sem + len(copies)])
                )
                copies[-1].start()
    return copies


def pair_kernel(per_group, *refs):
    held, halo_ref, out_refs = refs[:7], refs[7], refs[12:16]
    made_refs, sems = refs[16:20], refs[20]
    groups = held[5].shape[0]
    even = lax.axis_index("tp") % 2 == 0
    rest = (per_group, held, halo_ref, out_refs, made_refs, sems)
    pl.when(even)(functools.partial(filters, *rest, [("all", (0, groups // 2, groups))]))
    tasks = [("bound", (0, 3 * groups // 8, 3 * groups // 4)), ("all", (3 * groups // 4, groups))]
    pl.when(jnp.logical_not(even))(functools.partial(filters, *rest, tasks))


def pair_outputs(held, halo, results):
    channels, length = held[1].shape
    hbm = pl.BlockSpec(memory_space=pltpu.HBM)
    return pl.pallas_call(
        functools.partial(pair_kernel, channels // held[5].shape[0]),
        in_specs=[pl.BlockSpec(memory_space=pltpu.VMEM)] * 8 + [hbm] * 4,
        out_specs=[hbm] * 4,
        out_shape=[jax.ShapeDtypeStruct((channels, length), BF16)] * 4,
        input_output_aliases={8: 0, 9: 1, 10: 2, 11: 3},
        scratch_shapes=[pltpu.VMEM((channels, length), BF16)] * 4
        + [pltpu.SemaphoreType.DMA((16,))],
        cost_estimate=pl.CostEstimate(flops=2**28, bytes_accessed=2**23, transcendentals=0),
        compiler_params=pltpu.CompilerParams(vmem_limit_bytes=12 * 2**20),
        name="pair_outputs",
    )(*map(in_vmem, (*held, halo)), *results)


def exchanges(size):
    if size == 4:
        return [(2, 3, 1, 0), (3, 2, 0, 1), (1, 0, 3, 2)]
    return [tuple((i + step) % size for i in range(size)) for step in range(1, size)]


def gather_terms(sums, axis):
    return [sums] + [
        lax.ppermute(sums, axis, list(enumerate(targets)))
        for targets in exchanges(lax.axis_size(axis))
    ]


def total_kernel(groups, tap_scale, skip_scale, axis, order, *refs):
    *term_refs, tap_ref, skip_ref = refs
    taken = [term_refs[order.index(place)][...].astype(F32) for place in range(len(term_refs))]
    size = lax.axis_size(axis)
    here = lax.axis_index(axis)
    terms = [taken[0]] * size
    for received, targets in zip(taken[1:], exchanges(size)):
        for source, target in enumerate(targets):
            if source != target:
                terms[source] = jnp.where(here == target, received, terms[source])
    total = terms[0]
    for term in terms[1:]:
        total = total + term
    tap_ref[...] = total[:groups] * tap_scale
    skip_ref[...] = total[groups:] * skip_scale


def totals(terms, groups, tap_scale, skip_scale, axis):
    rows, length = terms[0].shape
    order = list(range(len(terms)))
    return pl.pallas_call(
        functools.partial(total_kernel, groups, tap_scale, skip_scale, axis, order),
        in_specs=[pl.BlockSpec(memory_space=pltpu.VMEM)] * len(terms),
        out_shape=[
            jax.ShapeDtypeStruct((groups, length), F32),
            jax.ShapeDtypeStruct((rows - groups, length), F32),
        ],
        compiler_params=pltpu.CompilerParams(vmem_limit_bytes=12 * 2**20),
        name="totals",
    )(*(in_vmem(terms[place]) for place in order))


def body(query_act, key_act, value_act, out_grad, keep_mask, filter_taps, skip_gain):
    windows, channels, length = query_act.shape
    groups, tap_count = filter_taps.shape
    assert windows == 1 and length == tap_count
    shards = lax.axis_size("ctx")
    per_group = channels // groups
    positions = windows * lax.axis_size("dp") * length * shards
    tap_scale = 1.0 / math.sqrt(positions * per_group)
    skip_scale = 1.0 / math.sqrt(positions)
    query, key, value, grad = query_act[0], key_act[0], value_act[0], out_grad[0]
    if shards == 2:
        swap = [(0, 1), (1, 0)]
        skips = skip_gain.reshape(channels // length, length)
        sources = (keep_mask, query, key, value, grad, filter_taps, skips)
        own, *held = own_block(*sources)
        made = turn_sums(0, sources, held)
        own, made = lax.optimization_barrier((own, made))
        halo = lax.ppermute(own, "ctx", swap)
        *held, mine = turn_sums(1, sources, made[:7], made[7:8])
        other = lax.ppermute(mine, "ctx", swap)
        crossed = cross_sums(own, halo, groups, True)
        sums = mine.astype(F32).at[:groups].add(crossed) + other.astype(F32)
        sums = lax.reduce_precision(sums, 8, 7).astype(BF16)
        terms = gather_terms(sums, "dp")
        results = pair_outputs(held, halo, made[8:])
    else:
        joined = (key.astype(F32) * value.astype(F32)).astype(BF16)
        own = (grad.astype(F32) * keep_mask.astype(F32) * query.astype(F32)).astype(BF16)
        before = lax.ppermute(joined, "ctx", [(i, i + 1) for i in range(shards - 1)])
        following = lax.ppermute(own, "ctx", [(i + 1, i) for i in range(shards - 1)])
        mine = local_sums(groups, keep_mask, query, key, value, grad)
        crossed = cross_sums(own, before, groups, False)
        sums = lax.psum(mine.at[:groups].add(crossed), "ctx")
        terms = gather_terms(sums, "dp")
        results = outputs(keep_mask, filter_taps, skip_gain, query, key, value, grad, before, following)
    filter_grad, skip_grad = totals(terms, groups, tap_scale, skip_scale, "dp")
    return (*(result[None] for result in results), filter_grad, skip_grad.reshape(channels))


def solution(mesh):
    large = P("dp", "tp", "ctx")
    return jax.shard_map(
        body,
        mesh=mesh,
        in_specs=(large, large, large, large, P("dp", "ctx"), P("tp", None), P("tp")),
        out_specs=(large, large, large, large, P("tp", None), P("tp")),
        check_vma=False,
    )
```

```python
import functools
import math

import jax
import jax.numpy as jnp
from jax import lax
from jax.experimental import pallas as pl
from jax.experimental.pallas import tpu as pltpu
from jax.sharding import PartitionSpec as P

BF16 = jnp.bfloat16
F32 = jnp.float32
PARTS = 2
PHASES = 4
ROWS_BY_ROWS = (((1,), (1,)), ((), ()))


def in_hbm(array):
    return pltpu.with_memory_space_constraint(array, pltpu.HBM)


def in_vmem(array):
    return pltpu.with_memory_space_constraint(array, pltpu.VMEM)


def iotas(rows, columns):
    return (
        lax.broadcasted_iota(jnp.int32, (rows, columns), 0),
        lax.broadcasted_iota(jnp.int32, (rows, columns), 1),
    )


def flip(block):
    length = block.shape[1]
    row, column = iotas(length, length)
    mirror = (row + column == length - 1).astype(F32).astype(BF16)
    return jnp.dot(block, mirror, preferred_element_type=F32).astype(BF16)


def grad_side(grad, per_group):
    length = grad.shape[1]
    span = length // PHASES
    across = grad.T
    left = jnp.concatenate([across[p * span : (p + 1) * span] for p in range(PHASES)], axis=1)
    owner = iotas(1, PHASES * length)[1] % length // per_group
    nothing = jnp.zeros((), BF16)
    return jnp.concatenate(
        [jnp.where(owner == g, left, nothing) for g in range(length // per_group)], axis=0
    )


def joined_side(joined, crossing):
    length = joined.shape[1]
    lane = iotas(1, length)[1]
    nothing = jnp.zeros((), BF16)
    mirrored = flip(joined).astype(F32)
    right = []
    for phase in range(PHASES):
        shift = length // PHASES * (phase + 1)
        turned = (mirrored if shift == length else pltpu.roll(mirrored, shift, 1)).astype(BF16)
        if crossing:
            earlier = jnp.where(lane >= shift, turned, nothing)
            right.append(jnp.concatenate([earlier, turned], axis=1))
        else:
            right.append(jnp.where(lane < shift, turned, nothing))
    return jnp.concatenate(right, axis=0)


def side_sums(sides, length, crossing):
    span = length // PHASES
    row, column = iotas(span, length)
    near = row + column >= span - 1
    sums = []
    for left, right in sides:
        grams = jnp.dot(left, right, preferred_element_type=F32)
        for start in range(0, grams.shape[0], span):
            gram = grams[start : start + span]
            gram = jnp.where(near, gram[:, :length], gram[:, length:] if crossing else 0.0)
            turned = pltpu.roll(gram, 0, 1, stride=1, stride_axis=0)
            sums.append(jnp.sum(turned, axis=0, keepdims=True))
    return pltpu.roll(jnp.concatenate(sums, axis=0), length - span + 1, 1)


def blocks_of(array):
    length = array.shape[1]
    return [array[start : start + length] for start in range(0, array.shape[0], length)]


def lag_sums(grad, joined, per_group, crossing):
    sides = [
        (grad_side(one, per_group), joined_side(two, crossing))
        for one, two in zip(blocks_of(grad), blocks_of(joined))
    ]
    return side_sums(sides, grad.shape[1], crossing)


def own_kernel(*refs):
    sources, own_ref, held, sems = refs[:5], refs[5], refs[6:13], refs[13]
    first = lax.axis_index("ctx") == 0
    channels = own_ref.shape[0]
    rows = channels // PARTS

    def run(one, two, masked):
        def copies_of(part):
            window = pl.ds(part * rows, rows)
            return [
                pltpu.make_async_copy(
                    sources[index].at[window], held[index].at[window], sems.at[2 * part + side]
                )
                for side, index in enumerate((one, two))
            ]

        keep_copy = pltpu.make_async_copy(sources[0], held[0], sems.at[2 * PARTS])
        keep_copy.start()
        for part in range(PARTS):
            for copy in copies_of(part):
                copy.start()
        keep_copy.wait()
        for part in range(PARTS):
            for copy in copies_of(part):
                copy.wait()
            window = pl.ds(part * rows, rows)
            scaled = held[two][window].astype(F32)
            if masked:
                scaled = scaled * held[0][...].astype(F32)
            own_ref[window] = (scaled * held[one][window].astype(F32)).astype(BF16)

    pl.when(first)(functools.partial(run, 2, 3, False))
    pl.when(jnp.logical_not(first))(functools.partial(run, 1, 4, True))


def own_block(*sources):
    whole = pl.BlockSpec(memory_space=pltpu.VMEM)
    return pl.pallas_call(
        own_kernel,
        in_specs=[pl.BlockSpec(memory_space=pltpu.HBM)] * 5,
        out_specs=[whole] * 8,
        out_shape=[pltpu.VMEM(sources[1].shape, BF16)]
        + [pltpu.VMEM(source.shape, source.dtype) for source in sources],
        scratch_shapes=[pltpu.SemaphoreType.DMA((2 * PARTS + 1,))],
        compiler_params=pltpu.CompilerParams(vmem_limit_bytes=12 * 2**20),
        name="own_block",
    )(*map(in_hbm, sources[:5]))


def turn_kernel(per_group, turn, *refs):
    sources = refs[:6]
    if turn == 0:
        held, sums_ref, out_refs = refs[13:20], refs[20], refs[21:25]
        sems, made_refs, out_sems = refs[25], refs[26:28], refs[28]
    else:
        held, sums_ref, sems = refs[14:21], refs[21], refs[22]
    query, key, value, grad, taps, skips = zip(sources, held[1:])

    def load(*pairs):
        return [
            pltpu.make_async_copy(source, target, sems.at[index])
            for index, (source, target) in enumerate(pairs)
        ]

    @pl.when(lax.axis_index("tp") % 2 == 1 - turn)
    def _():
        first = lax.axis_index("ctx") == 0

        @pl.when(first)
        def _():
            for copy in load(query, grad, taps, skips):
                copy.start()

        @pl.when(jnp.logical_not(first))
        def _():
            for copy in load(key, value, taps, skips):
                copy.start()

        for copy in load(key, value, taps, skips):
            copy.wait()
        local_part(per_group, held, sums_ref)
        if turn == 0:
            bounds = (0, 3 * held[5].shape[0] // 8, 3 * held[5].shape[0] // 4)
            filters(per_group, held, None, out_refs, made_refs, out_sems, [("free", bounds)])


def turn_sums(turn, sources, held, made=()):
    channels, length = held[1].shape
    groups = held[5].shape[0]
    whole = pl.BlockSpec(memory_space=pltpu.VMEM)
    hbm = pl.BlockSpec(memory_space=pltpu.HBM)
    free = turn == 0
    given = (*held, *made)
    return pl.pallas_call(
        functools.partial(turn_kernel, channels // groups, turn),
        in_specs=[hbm] * 6 + [whole] * len(given),
        out_specs=[whole] * 8 + [hbm] * (4 * free),
        out_shape=[pltpu.VMEM(array.shape, array.dtype) for array in held]
        + [pltpu.VMEM((groups + channels // length, length), BF16)]
        + [jax.ShapeDtypeStruct((channels, length), BF16)] * (4 * free),
        input_output_aliases={6 + index: index for index in range(len(given))},
        scratch_shapes=[pltpu.SemaphoreType.DMA((4,))]
        + [pltpu.VMEM((channels, length), BF16)] * (2 * free)
        + [pltpu.SemaphoreType.DMA((8,))] * free,
        cost_estimate=pl.CostEstimate(flops=2**26, bytes_accessed=2**23, transcendentals=0),
        compiler_params=pltpu.CompilerParams(vmem_limit_bytes=12 * 2**20),
        name="turn_sums",
    )(*map(in_hbm, sources[1:]), *map(in_vmem, given))


def local_kernel(per_group, *refs):
    local_part(per_group, refs[:5], refs[5])


def local_part(per_group, held, sums_ref):
    keep_ref, query_ref, key_ref, value_ref, grad_ref = held[:5]
    channels, length = query_ref.shape
    groups = channels // per_group
    joined = (key_ref[...].astype(F32) * value_ref[...].astype(F32)).astype(BF16)
    scaled = grad_ref[...].astype(F32) * keep_ref[...].astype(F32)
    mixed = (scaled * query_ref[...].astype(F32)).astype(BF16)
    sums_ref[:groups] = lag_sums(mixed, joined, per_group, False).astype(sums_ref.dtype)
    both = joined.astype(F32) * mixed.astype(F32)
    high = both.astype(BF16)
    low = (both - high.astype(F32)).astype(BF16)
    ones = jnp.ones((8, length), BF16)
    direct = lax.dot_general(ones, high, ROWS_BY_ROWS, preferred_element_type=F32)
    direct += lax.dot_general(ones, low, ROWS_BY_ROWS, preferred_element_type=F32)
    for block in range(channels // length):
        sums_ref[groups + block : groups + block + 1] = direct[
            :1, block * length : (block + 1) * length
        ].astype(sums_ref.dtype)


def local_sums(groups, *arrays):
    channels, length = arrays[1].shape
    return pl.pallas_call(
        functools.partial(local_kernel, channels // groups),
        out_shape=jax.ShapeDtypeStruct((groups + channels // length, length), F32),
        cost_estimate=pl.CostEstimate(flops=2**26, bytes_accessed=2**23, transcendentals=0),
        name="local_sums",
    )(*arrays)


def cross_kernel(per_group, own_ref, halo_ref, sums_ref):
    sums_ref[...] = lag_sums(own_ref[...], halo_ref[...], per_group, True)


def cross_sums(own, halo, groups):
    channels, length = own.shape
    return pl.pallas_call(
        functools.partial(cross_kernel, channels // groups),
        out_shape=jax.ShapeDtypeStruct((groups, length), F32),
        cost_estimate=pl.CostEstimate(flops=2**26, bytes_accessed=2**23, transcendentals=0),
        name="cross_sums",
    )(own, halo)


def ready_kernel(per_group, own_ref, _, left_ref, right_ref):
    first = lax.axis_index("ctx") == 0

    @pl.when(first)
    def _():
        for block, own in enumerate(blocks_of(own_ref[...])):
            right_ref[block] = joined_side(own, True)

    @pl.when(jnp.logical_not(first))
    def _():
        for block, own in enumerate(blocks_of(own_ref[...])):
            left_ref[block] = grad_side(own, per_group)


def halo_kernel(per_group, halo_ref, left_ref, right_ref, sums_ref):
    length = halo_ref.shape[1]
    first = lax.axis_index("ctx") == 0

    @pl.when(first)
    def _():
        grads = blocks_of(halo_ref[...])
        sides = [(grad_side(grad, per_group), right_ref[block]) for block, grad in enumerate(grads)]
        sums_ref[...] = side_sums(sides, length, True)

    @pl.when(jnp.logical_not(first))
    def _():
        sides = [
            (left_ref[block], joined_side(joined, True))
            for block, joined in enumerate(blocks_of(halo_ref[...]))
        ]
        sums_ref[...] = side_sums(sides, length, True)


def ready_sides(own, per_group, after):
    channels, length = own.shape
    blocks = channels // length
    spread = length // PHASES * (length // per_group)
    whole = pl.BlockSpec(memory_space=pltpu.VMEM)
    return pl.pallas_call(
        functools.partial(ready_kernel, per_group),
        in_specs=[whole] * 2,
        out_specs=[whole] * 2,
        out_shape=[
            pltpu.VMEM((blocks, spread, PHASES * length), BF16),
            pltpu.VMEM((blocks, PHASES * length, 2 * length), BF16),
        ],
        cost_estimate=pl.CostEstimate(flops=2**26, bytes_accessed=2**23, transcendentals=0),
        compiler_params=pltpu.CompilerParams(vmem_limit_bytes=12 * 2**20),
        name="ready_sides",
    )(in_vmem(own), in_vmem(after))


def halo_sums(halo, sides, per_group):
    channels, length = halo.shape
    whole = pl.BlockSpec(memory_space=pltpu.VMEM)
    return pl.pallas_call(
        functools.partial(halo_kernel, per_group),
        in_specs=[whole] * 3,
        out_specs=whole,
        out_shape=pltpu.VMEM((channels // per_group, length), F32),
        cost_estimate=pl.CostEstimate(flops=2**26, bytes_accessed=2**23, transcendentals=0),
        compiler_params=pltpu.CompilerParams(vmem_limit_bytes=12 * 2**20),
        name="halo_sums",
    )(in_vmem(halo), *map(in_vmem, sides))


def output_kernel(
    per_group, keep_ref, tap_ref, skip_ref, query_ref, key_ref, value_ref, grad_ref,
    before_ref, following_ref, out_ref, query_grad_ref, key_grad_ref, value_grad_ref,
):
    channels, length = query_ref.shape
    row, column = iotas(length, length)
    causal = column >= row
    keep = keep_ref[...].astype(F32)
    skips = skip_ref[0].T
    for group in range(channels // per_group):
        part = slice(group * per_group, (group + 1) * per_group)
        query = query_ref[part].astype(F32)
        key = key_ref[part].astype(F32)
        value = value_ref[part].astype(F32)
        scaled = grad_ref[part].astype(F32) * keep
        joined = (key * value).astype(BF16)
        mixed = (scaled * query).astype(BF16)
        before, following = before_ref[part], following_ref[part]
        taps = jnp.broadcast_to(tap_ref[group : group + 1], (length, length))
        circle = pltpu.roll(taps, 0, 1, stride=1, stride_axis=0)
        lower = jnp.where(causal, circle, 0.0).astype(BF16)
        upper = jnp.where(causal, 0.0, circle).astype(BF16)
        start = group * per_group
        skip = skips[start % length : start % length + per_group, start // length : start // length + 1]
        forward = jnp.dot(
            jnp.concatenate([before, joined], axis=1),
            jnp.concatenate([upper, lower], axis=0),
            preferred_element_type=F32,
        )
        forward += skip * joined.astype(F32)
        backward = lax.dot_general(
            jnp.concatenate([mixed, following], axis=1),
            jnp.concatenate([lower, upper], axis=1),
            ROWS_BY_ROWS,
            preferred_element_type=F32,
        )
        backward += skip * mixed.astype(F32)
        out_ref[part] = (query * forward).astype(BF16)
        query_grad_ref[part] = (scaled * forward).astype(BF16)
        key_grad_ref[part] = (backward * value).astype(BF16)
        value_grad_ref[part] = (backward * key).astype(BF16)


def outputs(keep, taps, skip, query, key, value, grad, before, following):
    channels, length = query.shape
    groups = taps.shape[0]
    steps = 2
    large = pl.BlockSpec((channels // steps, length), lambda i: (i, 0))
    skip_rows = skip.reshape(steps, channels // length // steps, length)
    return pl.pallas_call(
        functools.partial(output_kernel, channels // groups),
        grid=(steps,),
        in_specs=[
            pl.BlockSpec((1, length), lambda i: (0, 0)),
            pl.BlockSpec((groups // steps, length), lambda i: (i, 0)),
            pl.BlockSpec((1,) + skip_rows.shape[1:], lambda i: (i, 0, 0)),
        ]
        + [large] * 6,
        out_specs=[large] * 4,
        out_shape=[jax.ShapeDtypeStruct((channels, length), BF16)] * 4,
        cost_estimate=pl.CostEstimate(flops=2**28, bytes_accessed=2**24, transcendentals=0),
        compiler_params=pltpu.CompilerParams(vmem_limit_bytes=12 * 2**20),
        name="outputs",
    )(keep, taps, skip_rows, query, key, value, grad, before, following)


def filters(per_group, held, halo_ref, out_refs, made_refs, sems, tasks):
    first = lax.axis_index("ctx") == 0

    def run(here):
        copies = []
        for index, (chosen, bounds) in enumerate(tasks):
            forward = chosen == "all" or (chosen == "free") == here
            backward = chosen == "all" or (chosen == "free") != here
            copies += filter_groups(
                per_group, held, halo_ref, out_refs, made_refs, sems, here, forward, backward, bounds, 8 * index
            )
        for copy in copies:
            copy.wait()

    pl.when(first)(functools.partial(run, True))
    pl.when(jnp.logical_not(first))(functools.partial(run, False))


def filter_groups(
    per_group, held, halo_ref, out_refs, made_refs, sems, first, forward, backward, bounds, sem
):
    keep_ref, query_ref, key_ref, value_ref, grad_ref, tap_ref, skip_ref = held
    out_refs = out_refs[0 if forward else 2 : 4 if backward else 2]
    made_refs = made_refs[: len(out_refs)]
    length = query_ref.shape[1]
    row, column = iotas(length, length)
    causal = column >= row
    keep = keep_ref[...].astype(F32)
    skips = skip_ref[...].T
    copies = []
    for group in range(bounds[0], bounds[-1]):
        start = group * per_group
        part = slice(start, start + per_group)
        query = query_ref[part].astype(F32)
        key = key_ref[part].astype(F32)
        value = value_ref[part].astype(F32)
        scaled = grad_ref[part].astype(F32) * keep
        joined = (key * value).astype(BF16)
        mixed = (scaled * query).astype(BF16)
        taps = jnp.broadcast_to(tap_ref[group : group + 1], (length, length))
        circle = pltpu.roll(taps, 0, 1, stride=1, stride_axis=0)
        lower = jnp.where(causal, circle, 0.0).astype(BF16)
        upper = jnp.where(causal, 0.0, circle).astype(BF16)
        skip = skips[
            start % length : start % length + per_group, start // length : start // length + 1
        ]
        if halo_ref is not None:
            halo = halo_ref[part]
        results = []
        if forward:
            source, matrix = joined, lower
            if not first:
                source = jnp.concatenate([halo, joined], axis=1)
                matrix = jnp.concatenate([upper, lower], axis=0)
            mixed_sum = jnp.dot(source, matrix, preferred_element_type=F32)
            mixed_sum += skip * joined.astype(F32)
            results += [query * mixed_sum, scaled * mixed_sum]
        if backward:
            source, matrix = mixed, lower
            if first:
                source = jnp.concatenate([mixed, halo], axis=1)
                matrix = jnp.concatenate([lower, upper], axis=1)
            joined_grad = lax.dot_general(source, matrix, ROWS_BY_ROWS, preferred_element_type=F32)
            joined_grad += skip * mixed.astype(F32)
            results += [joined_grad * value, joined_grad * key]
        for made, result in zip(made_refs, results):
            made[part] = result.astype(BF16)
        if group + 1 in bounds:
            begin = bounds[bounds.index(group + 1) - 1] * per_group
            window = pl.ds(begin, start + per_group - begin)
            for made, out in zip(made_refs, out_refs):
                copies.append(
                    pltpu.make_async_copy(made.at[window], out.at[window], sems.at[sem + len(copies)])
                )
                copies[-1].start()
    return copies


def pair_kernel(per_group, *refs):
    held, halo_ref, out_refs = refs[:7], refs[7], refs[12:16]
    made_refs, sems = refs[16:20], refs[20]
    groups = held[5].shape[0]
    even = lax.axis_index("tp") % 2 == 0
    rest = (per_group, held, halo_ref, out_refs, made_refs, sems)
    pl.when(even)(functools.partial(filters, *rest, [("all", (0, groups // 2, groups))]))
    tasks = [("bound", (0, 3 * groups // 8, 3 * groups // 4)), ("all", (3 * groups // 4, groups))]
    pl.when(jnp.logical_not(even))(functools.partial(filters, *rest, tasks))


def pair_outputs(held, halo, results):
    channels, length = held[1].shape
    hbm = pl.BlockSpec(memory_space=pltpu.HBM)
    return pl.pallas_call(
        functools.partial(pair_kernel, channels // held[5].shape[0]),
        in_specs=[pl.BlockSpec(memory_space=pltpu.VMEM)] * 8 + [hbm] * 4,
        out_specs=[hbm] * 4,
        out_shape=[jax.ShapeDtypeStruct((channels, length), BF16)] * 4,
        input_output_aliases={8: 0, 9: 1, 10: 2, 11: 3},
        scratch_shapes=[pltpu.VMEM((channels, length), BF16)] * 4
        + [pltpu.SemaphoreType.DMA((16,))],
        cost_estimate=pl.CostEstimate(flops=2**28, bytes_accessed=2**23, transcendentals=0),
        compiler_params=pltpu.CompilerParams(vmem_limit_bytes=12 * 2**20),
        name="pair_outputs",
    )(*map(in_vmem, (*held, halo)), *results)


def exchanges(size):
    if size == 4:
        return [(2, 3, 1, 0), (3, 2, 0, 1), (1, 0, 3, 2)]
    return [tuple((i + step) % size for i in range(size)) for step in range(1, size)]


def gather_terms(sums, axis):
    return [sums] + [
        lax.ppermute(sums, axis, list(enumerate(targets)))
        for targets in exchanges(lax.axis_size(axis))
    ]


def total_kernel(groups, tap_scale, skip_scale, axis, order, *refs):
    *term_refs, tap_ref, skip_ref = refs
    taken = [term_refs[order.index(place)][...].astype(F32) for place in range(len(term_refs))]
    size = lax.axis_size(axis)
    here = lax.axis_index(axis)
    terms = [taken[0]] * size
    for received, targets in zip(taken[1:], exchanges(size)):
        for source, target in enumerate(targets):
            if source != target:
                terms[source] = jnp.where(here == target, received, terms[source])
    total = terms[0]
    for term in terms[1:]:
        total = total + term
    tap_ref[...] = total[:groups] * tap_scale
    skip_ref[...] = total[groups:] * skip_scale


def totals(terms, groups, tap_scale, skip_scale, axis):
    rows, length = terms[0].shape
    order = list(range(len(terms)))
    return pl.pallas_call(
        functools.partial(total_kernel, groups, tap_scale, skip_scale, axis, order),
        in_specs=[pl.BlockSpec(memory_space=pltpu.VMEM)] * len(terms),
        out_shape=[
            jax.ShapeDtypeStruct((groups, length), F32),
            jax.ShapeDtypeStruct((rows - groups, length), F32),
        ],
        compiler_params=pltpu.CompilerParams(vmem_limit_bytes=12 * 2**20),
        name="totals",
    )(*(in_vmem(terms[place]) for place in order))


def body(query_act, key_act, value_act, out_grad, keep_mask, filter_taps, skip_gain):
    windows, channels, length = query_act.shape
    groups, tap_count = filter_taps.shape
    assert windows == 1 and length == tap_count
    shards = lax.axis_size("ctx")
    per_group = channels // groups
    positions = windows * lax.axis_size("dp") * length * shards
    tap_scale = 1.0 / math.sqrt(positions * per_group)
    skip_scale = 1.0 / math.sqrt(positions)
    query, key, value, grad = query_act[0], key_act[0], value_act[0], out_grad[0]
    if shards == 2:
        swap = [(0, 1), (1, 0)]
        skips = skip_gain.reshape(channels // length, length)
        sources = (keep_mask, query, key, value, grad, filter_taps, skips)
        own, *held = own_block(*sources)
        made = turn_sums(0, sources, held)
        own, made = lax.optimization_barrier((own, made))
        halo = lax.ppermute(own, "ctx", swap)
        *held, mine = turn_sums(1, sources, made[:7], made[7:8])
        other = lax.ppermute(mine, "ctx", swap)
        crossed = halo_sums(halo, ready_sides(own, per_group, mine), per_group)
        sums = mine.astype(F32).at[:groups].add(crossed) + other.astype(F32)
        sums = lax.reduce_precision(sums, 8, 7).astype(BF16)
        terms = gather_terms(sums, "dp")
        results = pair_outputs(held, halo, made[8:])
    else:
        joined = (key.astype(F32) * value.astype(F32)).astype(BF16)
        own = (grad.astype(F32) * keep_mask.astype(F32) * query.astype(F32)).astype(BF16)
        before = lax.ppermute(joined, "ctx", [(i, i + 1) for i in range(shards - 1)])
        following = lax.ppermute(own, "ctx", [(i + 1, i) for i in range(shards - 1)])
        mine = local_sums(groups, keep_mask, query, key, value, grad)
        crossed = cross_sums(own, before, groups)
        sums = lax.psum(mine.at[:groups].add(crossed), "ctx")
        terms = gather_terms(sums, "dp")
        results = outputs(keep_mask, filter_taps, skip_gain, query, key, value, grad, before, following)
    filter_grad, skip_grad = totals(terms, groups, tap_scale, skip_scale, "dp")
    return (*(result[None] for result in results), filter_grad, skip_grad.reshape(channels))


def solution(mesh):
    large = P("dp", "tp", "ctx")
    return jax.shard_map(
        body,
        mesh=mesh,
        in_specs=(large, large, large, large, P("dp", "ctx"), P("tp", None), P("tp")),
        out_specs=(large, large, large, large, P("tp", None), P("tp")),
        check_vma=False,
    )
```

```python
import functools
import math

import jax
import jax.numpy as jnp
from jax import lax
from jax.experimental import pallas as pl
from jax.experimental.pallas import tpu as pltpu
from jax.sharding import PartitionSpec as P

BF16 = jnp.bfloat16
F32 = jnp.float32
PARTS = 2
PHASES = 4
ROWS_BY_ROWS = (((1,), (1,)), ((), ()))


def in_hbm(array):
    return pltpu.with_memory_space_constraint(array, pltpu.HBM)


def in_vmem(array):
    return pltpu.with_memory_space_constraint(array, pltpu.VMEM)


def iotas(rows, columns):
    return (
        lax.broadcasted_iota(jnp.int32, (rows, columns), 0),
        lax.broadcasted_iota(jnp.int32, (rows, columns), 1),
    )


def flip(block):
    length = block.shape[1]
    row, column = iotas(length, length)
    mirror = (row + column == length - 1).astype(F32).astype(BF16)
    return jnp.dot(block, mirror, preferred_element_type=F32).astype(BF16)


def grad_side(grad, per_group):
    length = grad.shape[1]
    span = length // PHASES
    across = grad.T
    left = jnp.concatenate([across[p * span : (p + 1) * span] for p in range(PHASES)], axis=1)
    owner = iotas(1, PHASES * length)[1] % length // per_group
    nothing = jnp.zeros((), BF16)
    return jnp.concatenate(
        [jnp.where(owner == g, left, nothing) for g in range(length // per_group)], axis=0
    )


def joined_side(joined, crossing):
    length = joined.shape[1]
    lane = iotas(1, length)[1]
    nothing = jnp.zeros((), BF16)
    mirrored = flip(joined).astype(F32)
    right = []
    for phase in range(PHASES):
        shift = length // PHASES * (phase + 1)
        turned = (mirrored if shift == length else pltpu.roll(mirrored, shift, 1)).astype(BF16)
        if crossing:
            earlier = jnp.where(lane >= shift, turned, nothing)
            right.append(jnp.concatenate([earlier, turned], axis=1))
        else:
            right.append(jnp.where(lane < shift, turned, nothing))
    return jnp.concatenate(right, axis=0)


def side_sums(sides, length, crossing):
    span = length // PHASES
    row, column = iotas(span, length)
    near = row + column >= span - 1
    sums = []
    for left, right in sides:
        grams = jnp.dot(left, right, preferred_element_type=F32)
        for start in range(0, grams.shape[0], span):
            gram = grams[start : start + span]
            gram = jnp.where(near, gram[:, :length], gram[:, length:] if crossing else 0.0)
            turned = pltpu.roll(gram, 0, 1, stride=1, stride_axis=0)
            sums.append(jnp.sum(turned, axis=0, keepdims=True))
    return pltpu.roll(jnp.concatenate(sums, axis=0), length - span + 1, 1)


def blocks_of(array):
    length = array.shape[1]
    return [array[start : start + length] for start in range(0, array.shape[0], length)]


def lag_sums(grad, joined, per_group, crossing):
    sides = [
        (grad_side(one, per_group), joined_side(two, crossing))
        for one, two in zip(blocks_of(grad), blocks_of(joined))
    ]
    return side_sums(sides, grad.shape[1], crossing)


def own_kernel(*refs):
    sources, own_ref, held, sems = refs[:5], refs[5], refs[6:13], refs[13]
    first = lax.axis_index("ctx") == 0
    channels = own_ref.shape[0]
    rows = channels // PARTS

    def run(one, two, masked):
        def copies_of(part):
            window = pl.ds(part * rows, rows)
            return [
                pltpu.make_async_copy(
                    sources[index].at[window], held[index].at[window], sems.at[2 * part + side]
                )
                for side, index in enumerate((one, two))
            ]

        keep_copy = pltpu.make_async_copy(sources[0], held[0], sems.at[2 * PARTS])
        keep_copy.start()
        for part in range(PARTS):
            for copy in copies_of(part):
                copy.start()
        keep_copy.wait()
        for part in range(PARTS):
            for copy in copies_of(part):
                copy.wait()
            window = pl.ds(part * rows, rows)
            scaled = held[two][window].astype(F32)
            if masked:
                scaled = scaled * held[0][...].astype(F32)
            own_ref[window] = (scaled * held[one][window].astype(F32)).astype(BF16)

    pl.when(first)(functools.partial(run, 2, 3, False))
    pl.when(jnp.logical_not(first))(functools.partial(run, 1, 4, True))


def own_block(*sources):
    whole = pl.BlockSpec(memory_space=pltpu.VMEM)
    return pl.pallas_call(
        own_kernel,
        in_specs=[pl.BlockSpec(memory_space=pltpu.HBM)] * 5,
        out_specs=[whole] * 8,
        out_shape=[pltpu.VMEM(sources[1].shape, BF16)]
        + [pltpu.VMEM(source.shape, source.dtype) for source in sources],
        scratch_shapes=[pltpu.SemaphoreType.DMA((2 * PARTS + 1,))],
        compiler_params=pltpu.CompilerParams(vmem_limit_bytes=12 * 2**20),
        name="own_block",
    )(*map(in_hbm, sources[:5]))


def turn_kernel(per_group, turn, *refs):
    sources = refs[:6]
    if turn == 0:
        held, sums_ref, out_refs = refs[13:20], refs[20], refs[21:25]
        sems, made_refs, out_sems = refs[25], refs[26:28], refs[28]
    else:
        held, sums_ref, sems = refs[14:21], refs[21], refs[22]
    query, key, value, grad, taps, skips = zip(sources, held[1:])

    def load(*pairs):
        return [
            pltpu.make_async_copy(source, target, sems.at[index])
            for index, (source, target) in enumerate(pairs)
        ]

    @pl.when(lax.axis_index("tp") % 2 == 1 - turn)
    def _():
        first = lax.axis_index("ctx") == 0

        @pl.when(first)
        def _():
            for copy in load(query, grad, taps, skips):
                copy.start()

        @pl.when(jnp.logical_not(first))
        def _():
            for copy in load(key, value, taps, skips):
                copy.start()

        for copy in load(key, value, taps, skips):
            copy.wait()
        local_part(per_group, held, sums_ref)
        if turn == 0:
            filters(per_group, held, None, out_refs, made_refs, out_sems, ahead)


def turn_sums(turn, sources, held, made=()):
    channels, length = held[1].shape
    groups = held[5].shape[0]
    whole = pl.BlockSpec(memory_space=pltpu.VMEM)
    hbm = pl.BlockSpec(memory_space=pltpu.HBM)
    free = turn == 0
    given = (*held, *made)
    return pl.pallas_call(
        functools.partial(turn_kernel, channels // groups, turn),
        in_specs=[hbm] * 6 + [whole] * len(given),
        out_specs=[whole] * 8 + [hbm] * (4 * free),
        out_shape=[pltpu.VMEM(array.shape, array.dtype) for array in held]
        + [pltpu.VMEM((groups + channels // length, length), BF16)]
        + [jax.ShapeDtypeStruct((channels, length), BF16)] * (4 * free),
        input_output_aliases={6 + index: index for index in range(len(given))},
        scratch_shapes=[pltpu.SemaphoreType.DMA((4,))]
        + [pltpu.VMEM((channels, length), BF16)] * (2 * free)
        + [pltpu.SemaphoreType.DMA((8,))] * free,
        cost_estimate=pl.CostEstimate(flops=2**26, bytes_accessed=2**23, transcendentals=0),
        compiler_params=pltpu.CompilerParams(vmem_limit_bytes=12 * 2**20),
        name="turn_sums",
    )(*map(in_hbm, sources[1:]), *map(in_vmem, given))


def local_kernel(per_group, *refs):
    local_part(per_group, refs[:5], refs[5])


def local_part(per_group, held, sums_ref):
    keep_ref, query_ref, key_ref, value_ref, grad_ref = held[:5]
    channels, length = query_ref.shape
    groups = channels // per_group
    joined = (key_ref[...].astype(F32) * value_ref[...].astype(F32)).astype(BF16)
    scaled = grad_ref[...].astype(F32) * keep_ref[...].astype(F32)
    mixed = (scaled * query_ref[...].astype(F32)).astype(BF16)
    sums_ref[:groups] = lag_sums(mixed, joined, per_group, False).astype(sums_ref.dtype)
    both = joined.astype(F32) * mixed.astype(F32)
    high = both.astype(BF16)
    low = (both - high.astype(F32)).astype(BF16)
    ones = jnp.ones((8, length), BF16)
    direct = lax.dot_general(ones, high, ROWS_BY_ROWS, preferred_element_type=F32)
    direct += lax.dot_general(ones, low, ROWS_BY_ROWS, preferred_element_type=F32)
    for block in range(channels // length):
        sums_ref[groups + block : groups + block + 1] = direct[
            :1, block * length : (block + 1) * length
        ].astype(sums_ref.dtype)


def local_sums(groups, *arrays):
    channels, length = arrays[1].shape
    return pl.pallas_call(
        functools.partial(local_kernel, channels // groups),
        out_shape=jax.ShapeDtypeStruct((groups + channels // length, length), F32),
        cost_estimate=pl.CostEstimate(flops=2**26, bytes_accessed=2**23, transcendentals=0),
        name="local_sums",
    )(*arrays)


def cross_kernel(per_group, own_ref, halo_ref, sums_ref):
    sums_ref[...] = lag_sums(own_ref[...], halo_ref[...], per_group, True)


def cross_sums(own, halo, groups):
    channels, length = own.shape
    return pl.pallas_call(
        functools.partial(cross_kernel, channels // groups),
        out_shape=jax.ShapeDtypeStruct((groups, length), F32),
        cost_estimate=pl.CostEstimate(flops=2**26, bytes_accessed=2**23, transcendentals=0),
        name="cross_sums",
    )(own, halo)


def ready_kernel(per_group, own_ref, _, left_ref, right_ref):
    first = lax.axis_index("ctx") == 0

    @pl.when(first)
    def _():
        for block, own in enumerate(blocks_of(own_ref[...])):
            right_ref[block] = joined_side(own, True)

    @pl.when(jnp.logical_not(first))
    def _():
        for block, own in enumerate(blocks_of(own_ref[...])):
            left_ref[block] = grad_side(own, per_group)


def halo_kernel(per_group, halo_ref, left_ref, right_ref, sums_ref):
    length = halo_ref.shape[1]
    first = lax.axis_index("ctx") == 0

    @pl.when(first)
    def _():
        grads = blocks_of(halo_ref[...])
        sides = [(grad_side(grad, per_group), right_ref[block]) for block, grad in enumerate(grads)]
        sums_ref[...] = side_sums(sides, length, True)

    @pl.when(jnp.logical_not(first))
    def _():
        sides = [
            (left_ref[block], joined_side(joined, True))
            for block, joined in enumerate(blocks_of(halo_ref[...]))
        ]
        sums_ref[...] = side_sums(sides, length, True)


def ready_sides(own, per_group, after):
    channels, length = own.shape
    blocks = channels // length
    spread = length // PHASES * (length // per_group)
    whole = pl.BlockSpec(memory_space=pltpu.VMEM)
    return pl.pallas_call(
        functools.partial(ready_kernel, per_group),
        in_specs=[whole] * 2,
        out_specs=[whole] * 2,
        out_shape=[
            pltpu.VMEM((blocks, spread, PHASES * length), BF16),
            pltpu.VMEM((blocks, PHASES * length, 2 * length), BF16),
        ],
        cost_estimate=pl.CostEstimate(flops=2**26, bytes_accessed=2**23, transcendentals=0),
        compiler_params=pltpu.CompilerParams(vmem_limit_bytes=12 * 2**20),
        name="ready_sides",
    )(in_vmem(own), in_vmem(after))


def halo_sums(halo, sides, per_group):
    channels, length = halo.shape
    whole = pl.BlockSpec(memory_space=pltpu.VMEM)
    return pl.pallas_call(
        functools.partial(halo_kernel, per_group),
        in_specs=[whole] * 3,
        out_specs=whole,
        out_shape=pltpu.VMEM((channels // per_group, length), F32),
        cost_estimate=pl.CostEstimate(flops=2**26, bytes_accessed=2**23, transcendentals=0),
        compiler_params=pltpu.CompilerParams(vmem_limit_bytes=12 * 2**20),
        name="halo_sums",
    )(in_vmem(halo), *map(in_vmem, sides))


def output_kernel(
    per_group, keep_ref, tap_ref, skip_ref, query_ref, key_ref, value_ref, grad_ref,
    before_ref, following_ref, out_ref, query_grad_ref, key_grad_ref, value_grad_ref,
):
    channels, length = query_ref.shape
    row, column = iotas(length, length)
    causal = column >= row
    keep = keep_ref[...].astype(F32)
    skips = skip_ref[0].T
    for group in range(channels // per_group):
        part = slice(group * per_group, (group + 1) * per_group)
        query = query_ref[part].astype(F32)
        key = key_ref[part].astype(F32)
        value = value_ref[part].astype(F32)
        scaled = grad_ref[part].astype(F32) * keep
        joined = (key * value).astype(BF16)
        mixed = (scaled * query).astype(BF16)
        before, following = before_ref[part], following_ref[part]
        taps = jnp.broadcast_to(tap_ref[group : group + 1], (length, length))
        circle = pltpu.roll(taps, 0, 1, stride=1, stride_axis=0)
        lower = jnp.where(causal, circle, 0.0).astype(BF16)
        upper = jnp.where(causal, 0.0, circle).astype(BF16)
        start = group * per_group
        skip = skips[start % length : start % length + per_group, start // length : start // length + 1]
        forward = jnp.dot(
            jnp.concatenate([before, joined], axis=1),
            jnp.concatenate([upper, lower], axis=0),
            preferred_element_type=F32,
        )
        forward += skip * joined.astype(F32)
        backward = lax.dot_general(
            jnp.concatenate([mixed, following], axis=1),
            jnp.concatenate([lower, upper], axis=1),
            ROWS_BY_ROWS,
            preferred_element_type=F32,
        )
        backward += skip * mixed.astype(F32)
        out_ref[part] = (query * forward).astype(BF16)
        query_grad_ref[part] = (scaled * forward).astype(BF16)
        key_grad_ref[part] = (backward * value).astype(BF16)
        value_grad_ref[part] = (backward * key).astype(BF16)


def outputs(keep, taps, skip, query, key, value, grad, before, following):
    channels, length = query.shape
    groups = taps.shape[0]
    steps = 2
    large = pl.BlockSpec((channels // steps, length), lambda i: (i, 0))
    skip_rows = skip.reshape(steps, channels // length // steps, length)
    return pl.pallas_call(
        functools.partial(output_kernel, channels // groups),
        grid=(steps,),
        in_specs=[
            pl.BlockSpec((1, length), lambda i: (0, 0)),
            pl.BlockSpec((groups // steps, length), lambda i: (i, 0)),
            pl.BlockSpec((1,) + skip_rows.shape[1:], lambda i: (i, 0, 0)),
        ]
        + [large] * 6,
        out_specs=[large] * 4,
        out_shape=[jax.ShapeDtypeStruct((channels, length), BF16)] * 4,
        cost_estimate=pl.CostEstimate(flops=2**28, bytes_accessed=2**24, transcendentals=0),
        compiler_params=pltpu.CompilerParams(vmem_limit_bytes=12 * 2**20),
        name="outputs",
    )(keep, taps, skip_rows, query, key, value, grad, before, following)


def ahead(groups, first):
    share = groups * (12 if first else 8) // 16
    return [("free", (0, share // 2, share))]


def behind(groups, first):
    bounds = ahead(groups, first)[0][1]
    return [("bound", bounds)] + [("all", (bounds[-1], groups))] * (bounds[-1] < groups)


def whole(groups, first):
    return [("all", (0, groups // 2, groups))]


def filters(per_group, held, halo_ref, out_refs, made_refs, sems, tasks):
    first = lax.axis_index("ctx") == 0

    def run(here):
        copies = []
        for index, (chosen, bounds) in enumerate(tasks(held[5].shape[0], here)):
            forward = chosen == "all" or (chosen == "free") == here
            backward = chosen == "all" or (chosen == "free") != here
            copies += filter_groups(
                per_group, held, halo_ref, out_refs, made_refs, sems, here, forward, backward, bounds, 8 * index
            )
        for copy in copies:
            copy.wait()

    pl.when(first)(functools.partial(run, True))
    pl.when(jnp.logical_not(first))(functools.partial(run, False))


def filter_groups(
    per_group, held, halo_ref, out_refs, made_refs, sems, first, forward, backward, bounds, sem
):
    keep_ref, query_ref, key_ref, value_ref, grad_ref, tap_ref, skip_ref = held
    out_refs = out_refs[0 if forward else 2 : 4 if backward else 2]
    made_refs = made_refs[: len(out_refs)]
    length = query_ref.shape[1]
    row, column = iotas(length, length)
    causal = column >= row
    keep = keep_ref[...].astype(F32)
    skips = skip_ref[...].T
    copies = []
    for group in range(bounds[0], bounds[-1]):
        start = group * per_group
        part = slice(start, start + per_group)
        query = query_ref[part].astype(F32)
        key = key_ref[part].astype(F32)
        value = value_ref[part].astype(F32)
        scaled = grad_ref[part].astype(F32) * keep
        joined = (key * value).astype(BF16)
        mixed = (scaled * query).astype(BF16)
        taps = jnp.broadcast_to(tap_ref[group : group + 1], (length, length))
        circle = pltpu.roll(taps, 0, 1, stride=1, stride_axis=0)
        lower = jnp.where(causal, circle, 0.0).astype(BF16)
        upper = jnp.where(causal, 0.0, circle).astype(BF16)
        skip = skips[
            start % length : start % length + per_group, start // length : start // length + 1
        ]
        if halo_ref is not None:
            halo = halo_ref[part]
        results = []
        if forward:
            source, matrix = joined, lower
            if not first:
                source = jnp.concatenate([halo, joined], axis=1)
                matrix = jnp.concatenate([upper, lower], axis=0)
            mixed_sum = jnp.dot(source, matrix, preferred_element_type=F32)
            mixed_sum += skip * joined.astype(F32)
            results += [query * mixed_sum, scaled * mixed_sum]
        if backward:
            source, matrix = mixed, lower
            if first:
                source = jnp.concatenate([mixed, halo], axis=1)
                matrix = jnp.concatenate([lower, upper], axis=1)
            joined_grad = lax.dot_general(source, matrix, ROWS_BY_ROWS, preferred_element_type=F32)
            joined_grad += skip * mixed.astype(F32)
            results += [joined_grad * value, joined_grad * key]
        for made, result in zip(made_refs, results):
            made[part] = result.astype(BF16)
        if group + 1 in bounds:
            begin = bounds[bounds.index(group + 1) - 1] * per_group
            window = pl.ds(begin, start + per_group - begin)
            for made, out in zip(made_refs, out_refs):
                copies.append(
                    pltpu.make_async_copy(made.at[window], out.at[window], sems.at[sem + len(copies)])
                )
                copies[-1].start()
    return copies


def pair_kernel(per_group, *refs):
    held, halo_ref, out_refs = refs[:7], refs[7], refs[12:16]
    made_refs, sems = refs[16:20], refs[20]
    even = lax.axis_index("tp") % 2 == 0
    rest = (per_group, held, halo_ref, out_refs, made_refs, sems)
    pl.when(even)(functools.partial(filters, *rest, whole))
    pl.when(jnp.logical_not(even))(functools.partial(filters, *rest, behind))


def pair_outputs(held, halo, results):
    channels, length = held[1].shape
    hbm = pl.BlockSpec(memory_space=pltpu.HBM)
    return pl.pallas_call(
        functools.partial(pair_kernel, channels // held[5].shape[0]),
        in_specs=[pl.BlockSpec(memory_space=pltpu.VMEM)] * 8 + [hbm] * 4,
        out_specs=[hbm] * 4,
        out_shape=[jax.ShapeDtypeStruct((channels, length), BF16)] * 4,
        input_output_aliases={8: 0, 9: 1, 10: 2, 11: 3},
        scratch_shapes=[pltpu.VMEM((channels, length), BF16)] * 4
        + [pltpu.SemaphoreType.DMA((16,))],
        cost_estimate=pl.CostEstimate(flops=2**28, bytes_accessed=2**23, transcendentals=0),
        compiler_params=pltpu.CompilerParams(vmem_limit_bytes=12 * 2**20),
        name="pair_outputs",
    )(*map(in_vmem, (*held, halo)), *results)


def exchanges(size):
    if size == 4:
        return [(2, 3, 1, 0), (3, 2, 0, 1), (1, 0, 3, 2)]
    return [tuple((i + step) % size for i in range(size)) for step in range(1, size)]


def gather_terms(sums, axis):
    return [sums] + [
        lax.ppermute(sums, axis, list(enumerate(targets)))
        for targets in exchanges(lax.axis_size(axis))
    ]


def total_kernel(groups, tap_scale, skip_scale, axis, order, *refs):
    *term_refs, tap_ref, skip_ref = refs
    taken = [term_refs[order.index(place)][...].astype(F32) for place in range(len(term_refs))]
    size = lax.axis_size(axis)
    here = lax.axis_index(axis)
    terms = [taken[0]] * size
    for received, targets in zip(taken[1:], exchanges(size)):
        for source, target in enumerate(targets):
            if source != target:
                terms[source] = jnp.where(here == target, received, terms[source])
    total = terms[0]
    for term in terms[1:]:
        total = total + term
    tap_ref[...] = total[:groups] * tap_scale
    skip_ref[...] = total[groups:] * skip_scale


def totals(terms, groups, tap_scale, skip_scale, axis):
    rows, length = terms[0].shape
    order = list(range(len(terms)))
    return pl.pallas_call(
        functools.partial(total_kernel, groups, tap_scale, skip_scale, axis, order),
        in_specs=[pl.BlockSpec(memory_space=pltpu.VMEM)] * len(terms),
        out_shape=[
            jax.ShapeDtypeStruct((groups, length), F32),
            jax.ShapeDtypeStruct((rows - groups, length), F32),
        ],
        compiler_params=pltpu.CompilerParams(vmem_limit_bytes=12 * 2**20),
        name="totals",
    )(*(in_vmem(terms[place]) for place in order))


def body(query_act, key_act, value_act, out_grad, keep_mask, filter_taps, skip_gain):
    windows, channels, length = query_act.shape
    groups, tap_count = filter_taps.shape
    assert windows == 1 and length == tap_count
    shards = lax.axis_size("ctx")
    per_group = channels // groups
    positions = windows * lax.axis_size("dp") * length * shards
    tap_scale = 1.0 / math.sqrt(positions * per_group)
    skip_scale = 1.0 / math.sqrt(positions)
    query, key, value, grad = query_act[0], key_act[0], value_act[0], out_grad[0]
    if shards == 2:
        swap = [(0, 1), (1, 0)]
        skips = skip_gain.reshape(channels // length, length)
        sources = (keep_mask, query, key, value, grad, filter_taps, skips)
        own, *held = own_block(*sources)
        made = turn_sums(0, sources, held)
        own, made = lax.optimization_barrier((own, made))
        halo = lax.ppermute(own, "ctx", swap)
        *held, mine = turn_sums(1, sources, made[:7], made[7:8])
        other = lax.ppermute(mine, "ctx", swap)
        crossed = halo_sums(halo, ready_sides(own, per_group, mine), per_group)
        sums = mine.astype(F32).at[:groups].add(crossed) + other.astype(F32)
        sums = lax.reduce_precision(sums, 8, 7).astype(BF16)
        terms = gather_terms(sums, "dp")
        results = pair_outputs(held, halo, made[8:])
    else:
        joined = (key.astype(F32) * value.astype(F32)).astype(BF16)
        own = (grad.astype(F32) * keep_mask.astype(F32) * query.astype(F32)).astype(BF16)
        before = lax.ppermute(joined, "ctx", [(i, i + 1) for i in range(shards - 1)])
        following = lax.ppermute(own, "ctx", [(i + 1, i) for i in range(shards - 1)])
        mine = local_sums(groups, keep_mask, query, key, value, grad)
        crossed = cross_sums(own, before, groups)
        sums = lax.psum(mine.at[:groups].add(crossed), "ctx")
        terms = gather_terms(sums, "dp")
        results = outputs(keep_mask, filter_taps, skip_gain, query, key, value, grad, before, following)
    filter_grad, skip_grad = totals(terms, groups, tap_scale, skip_scale, "dp")
    return (*(result[None] for result in results), filter_grad, skip_grad.reshape(channels))


def solution(mesh):
    large = P("dp", "tp", "ctx")
    return jax.shard_map(
        body,
        mesh=mesh,
        in_specs=(large, large, large, large, P("dp", "ctx"), P("tp", None), P("tp")),
        out_specs=(large, large, large, large, P("tp", None), P("tp")),
        check_vma=False,
    )
```

```python
import functools
import math

import jax
import jax.numpy as jnp
from jax import lax
from jax.experimental import pallas as pl
from jax.experimental.pallas import tpu as pltpu
from jax.sharding import PartitionSpec as P

BF16 = jnp.bfloat16
F32 = jnp.float32
PARTS = 2
PHASES = 4
ROWS_BY_ROWS = (((1,), (1,)), ((), ()))


def in_hbm(array):
    return pltpu.with_memory_space_constraint(array, pltpu.HBM)


def in_vmem(array):
    return pltpu.with_memory_space_constraint(array, pltpu.VMEM)


def iotas(rows, columns):
    return (
        lax.broadcasted_iota(jnp.int32, (rows, columns), 0),
        lax.broadcasted_iota(jnp.int32, (rows, columns), 1),
    )


def flip(block):
    length = block.shape[1]
    row, column = iotas(length, length)
    mirror = (row + column == length - 1).astype(F32).astype(BF16)
    return jnp.dot(block, mirror, preferred_element_type=F32).astype(BF16)


def grad_side(grad, per_group):
    length = grad.shape[1]
    span = length // PHASES
    across = grad.T
    left = jnp.concatenate([across[p * span : (p + 1) * span] for p in range(PHASES)], axis=1)
    owner = iotas(1, PHASES * length)[1] % length // per_group
    nothing = jnp.zeros((), BF16)
    return jnp.concatenate(
        [jnp.where(owner == g, left, nothing) for g in range(length // per_group)], axis=0
    )


def joined_side(joined, crossing):
    length = joined.shape[1]
    lane = iotas(1, length)[1]
    nothing = jnp.zeros((), BF16)
    mirrored = flip(joined).astype(F32)
    right = []
    for phase in range(PHASES):
        shift = length // PHASES * (phase + 1)
        turned = (mirrored if shift == length else pltpu.roll(mirrored, shift, 1)).astype(BF16)
        if crossing:
            earlier = jnp.where(lane >= shift, turned, nothing)
            right.append(jnp.concatenate([earlier, turned], axis=1))
        else:
            right.append(jnp.where(lane < shift, turned, nothing))
    return jnp.concatenate(right, axis=0)


def side_sums(sides, length, crossing):
    span = length // PHASES
    row, column = iotas(span, length)
    near = row + column >= span - 1
    sums = []
    for left, right in sides:
        grams = jnp.dot(left, right, preferred_element_type=F32)
        for start in range(0, grams.shape[0], span):
            gram = grams[start : start + span]
            gram = jnp.where(near, gram[:, :length], gram[:, length:] if crossing else 0.0)
            turned = pltpu.roll(gram, 0, 1, stride=1, stride_axis=0)
            sums.append(jnp.sum(turned, axis=0, keepdims=True))
    return pltpu.roll(jnp.concatenate(sums, axis=0), length - span + 1, 1)


def blocks_of(array):
    length = array.shape[1]
    return [array[start : start + length] for start in range(0, array.shape[0], length)]


def lag_sums(grad, joined, per_group, crossing):
    sides = [
        (grad_side(one, per_group), joined_side(two, crossing))
        for one, two in zip(blocks_of(grad), blocks_of(joined))
    ]
    return side_sums(sides, grad.shape[1], crossing)


def own_kernel(*refs):
    sources, own_ref, held, sems = refs[:5], refs[5], refs[6:13], refs[13]
    first = lax.axis_index("ctx") == 0
    channels = own_ref.shape[0]
    rows = channels // PARTS

    def run(one, two, masked):
        def copies_of(part):
            window = pl.ds(part * rows, rows)
            return [
                pltpu.make_async_copy(
                    sources[index].at[window], held[index].at[window], sems.at[2 * part + side]
                )
                for side, index in enumerate((one, two))
            ]

        keep_copy = pltpu.make_async_copy(sources[0], held[0], sems.at[2 * PARTS])
        keep_copy.start()
        for part in range(PARTS):
            for copy in copies_of(part):
                copy.start()
        keep_copy.wait()
        for part in range(PARTS):
            for copy in copies_of(part):
                copy.wait()
            window = pl.ds(part * rows, rows)
            scaled = held[two][window].astype(F32)
            if masked:
                scaled = scaled * held[0][...].astype(F32)
            own_ref[window] = (scaled * held[one][window].astype(F32)).astype(BF16)

    pl.when(first)(functools.partial(run, 2, 3, False))
    pl.when(jnp.logical_not(first))(functools.partial(run, 1, 4, True))


def first_kernel(per_group, *refs):
    sources, (own_ref, *held), sums_ref, out_refs = refs[:7], refs[7:15], refs[15], refs[16:20]
    own_sems, sems, made_refs, out_sems = refs[20], refs[21], refs[22:24], refs[24]
    own_kernel(*sources[:5], own_ref, *held, own_sems)
    turn_part(per_group, 0, sources[1:], held, sums_ref, sems, out_refs, made_refs, out_sems)


def first_turn(*sources):
    channels, length = sources[1].shape
    groups = sources[5].shape[0]
    whole = pl.BlockSpec(memory_space=pltpu.VMEM)
    hbm = pl.BlockSpec(memory_space=pltpu.HBM)
    return pl.pallas_call(
        functools.partial(first_kernel, channels // groups),
        in_specs=[hbm] * 7,
        out_specs=[whole] * 9 + [hbm] * 4,
        out_shape=[pltpu.VMEM((channels, length), BF16)]
        + [pltpu.VMEM(source.shape, source.dtype) for source in sources]
        + [pltpu.VMEM((groups + channels // length, length), BF16)]
        + [jax.ShapeDtypeStruct((channels, length), BF16)] * 4,
        scratch_shapes=[pltpu.SemaphoreType.DMA((2 * PARTS + 1,)), pltpu.SemaphoreType.DMA((4,))]
        + [pltpu.VMEM((channels, length), BF16)] * 2
        + [pltpu.SemaphoreType.DMA((8,))],
        compiler_params=pltpu.CompilerParams(vmem_limit_bytes=12 * 2**20),
        name="first_turn",
    )(*map(in_hbm, sources))


def turn_kernel(per_group, *refs):
    turn_part(per_group, 1, refs[:6], refs[14:21], refs[21], refs[22])


def turn_part(per_group, turn, sources, held, sums_ref, sems, out_refs=(), made_refs=(), out_sems=None):
    query, key, value, grad, taps, skips = zip(sources, held[1:])

    def load(*pairs):
        return [
            pltpu.make_async_copy(source, target, sems.at[index])
            for index, (source, target) in enumerate(pairs)
        ]

    @pl.when(lax.axis_index("tp") % 2 == 1 - turn)
    def _():
        first = lax.axis_index("ctx") == 0

        @pl.when(first)
        def _():
            for copy in load(query, grad, taps, skips):
                copy.start()

        @pl.when(jnp.logical_not(first))
        def _():
            for copy in load(key, value, taps, skips):
                copy.start()

        for copy in load(key, value, taps, skips):
            copy.wait()
        local_part(per_group, held, sums_ref)
        if turn == 0:
            bounds = (0, 3 * held[5].shape[0] // 8, 3 * held[5].shape[0] // 4)
            filters(per_group, held, None, out_refs, made_refs, out_sems, [("free", bounds)])


def turn_sums(sources, *given):
    channels = given[1].shape[0]
    whole = pl.BlockSpec(memory_space=pltpu.VMEM)
    return pl.pallas_call(
        functools.partial(turn_kernel, channels // given[5].shape[0]),
        in_specs=[pl.BlockSpec(memory_space=pltpu.HBM)] * 6 + [whole] * 8,
        out_specs=[whole] * 8,
        out_shape=[pltpu.VMEM(array.shape, array.dtype) for array in given],
        input_output_aliases={6 + index: index for index in range(8)},
        scratch_shapes=[pltpu.SemaphoreType.DMA((4,))],
        cost_estimate=pl.CostEstimate(flops=2**26, bytes_accessed=2**23, transcendentals=0),
        compiler_params=pltpu.CompilerParams(vmem_limit_bytes=12 * 2**20),
        name="turn_sums",
    )(*map(in_hbm, sources[1:]), *map(in_vmem, given))


def local_kernel(per_group, *refs):
    local_part(per_group, refs[:5], refs[5])


def local_part(per_group, held, sums_ref):
    keep_ref, query_ref, key_ref, value_ref, grad_ref = held[:5]
    channels, length = query_ref.shape
    groups = channels // per_group
    joined = (key_ref[...].astype(F32) * value_ref[...].astype(F32)).astype(BF16)
    scaled = grad_ref[...].astype(F32) * keep_ref[...].astype(F32)
    mixed = (scaled * query_ref[...].astype(F32)).astype(BF16)
    sums_ref[:groups] = lag_sums(mixed, joined, per_group, False).astype(sums_ref.dtype)
    both = joined.astype(F32) * mixed.astype(F32)
    high = both.astype(BF16)
    low = (both - high.astype(F32)).astype(BF16)
    ones = jnp.ones((8, length), BF16)
    direct = lax.dot_general(ones, high, ROWS_BY_ROWS, preferred_element_type=F32)
    direct += lax.dot_general(ones, low, ROWS_BY_ROWS, preferred_element_type=F32)
    for block in range(channels // length):
        sums_ref[groups + block : groups + block + 1] = direct[
            :1, block * length : (block + 1) * length
        ].astype(sums_ref.dtype)


def local_sums(groups, *arrays):
    channels, length = arrays[1].shape
    return pl.pallas_call(
        functools.partial(local_kernel, channels // groups),
        out_shape=jax.ShapeDtypeStruct((groups + channels // length, length), F32),
        cost_estimate=pl.CostEstimate(flops=2**26, bytes_accessed=2**23, transcendentals=0),
        name="local_sums",
    )(*arrays)


def cross_kernel(per_group, own_ref, halo_ref, sums_ref):
    sums_ref[...] = lag_sums(own_ref[...], halo_ref[...], per_group, True)


def cross_sums(own, halo, groups):
    channels, length = own.shape
    return pl.pallas_call(
        functools.partial(cross_kernel, channels // groups),
        out_shape=jax.ShapeDtypeStruct((groups, length), F32),
        cost_estimate=pl.CostEstimate(flops=2**26, bytes_accessed=2**23, transcendentals=0),
        name="cross_sums",
    )(own, halo)


def ready_kernel(per_group, own_ref, _, left_ref, right_ref):
    first = lax.axis_index("ctx") == 0

    @pl.when(first)
    def _():
        for block, own in enumerate(blocks_of(own_ref[...])):
            right_ref[block] = joined_side(own, True)

    @pl.when(jnp.logical_not(first))
    def _():
        for block, own in enumerate(blocks_of(own_ref[...])):
            left_ref[block] = grad_side(own, per_group)


def halo_kernel(per_group, halo_ref, left_ref, right_ref, sums_ref):
    length = halo_ref.shape[1]
    first = lax.axis_index("ctx") == 0

    @pl.when(first)
    def _():
        grads = blocks_of(halo_ref[...])
        sides = [(grad_side(grad, per_group), right_ref[block]) for block, grad in enumerate(grads)]
        sums_ref[...] = side_sums(sides, length, True)

    @pl.when(jnp.logical_not(first))
    def _():
        sides = [
            (left_ref[block], joined_side(joined, True))
            for block, joined in enumerate(blocks_of(halo_ref[...]))
        ]
        sums_ref[...] = side_sums(sides, length, True)


def ready_sides(own, per_group, after):
    channels, length = own.shape
    blocks = channels // length
    spread = length // PHASES * (length // per_group)
    whole = pl.BlockSpec(memory_space=pltpu.VMEM)
    return pl.pallas_call(
        functools.partial(ready_kernel, per_group),
        in_specs=[whole] * 2,
        out_specs=[whole] * 2,
        out_shape=[
            pltpu.VMEM((blocks, spread, PHASES * length), BF16),
            pltpu.VMEM((blocks, PHASES * length, 2 * length), BF16),
        ],
        cost_estimate=pl.CostEstimate(flops=2**26, bytes_accessed=2**23, transcendentals=0),
        compiler_params=pltpu.CompilerParams(vmem_limit_bytes=12 * 2**20),
        name="ready_sides",
    )(in_vmem(own), in_vmem(after))


def halo_sums(halo, sides, per_group):
    channels, length = halo.shape
    whole = pl.BlockSpec(memory_space=pltpu.VMEM)
    return pl.pallas_call(
        functools.partial(halo_kernel, per_group),
        in_specs=[whole] * 3,
        out_specs=whole,
        out_shape=pltpu.VMEM((channels // per_group, length), F32),
        cost_estimate=pl.CostEstimate(flops=2**26, bytes_accessed=2**23, transcendentals=0),
        compiler_params=pltpu.CompilerParams(vmem_limit_bytes=12 * 2**20),
        name="halo_sums",
    )(in_vmem(halo), *map(in_vmem, sides))


def output_kernel(
    per_group, keep_ref, tap_ref, skip_ref, query_ref, key_ref, value_ref, grad_ref,
    before_ref, following_ref, out_ref, query_grad_ref, key_grad_ref, value_grad_ref,
):
    channels, length = query_ref.shape
    row, column = iotas(length, length)
    causal = column >= row
    keep = keep_ref[...].astype(F32)
    skips = skip_ref[0].T
    for group in range(channels // per_group):
        part = slice(group * per_group, (group + 1) * per_group)
        query = query_ref[part].astype(F32)
        key = key_ref[part].astype(F32)
        value = value_ref[part].astype(F32)
        scaled = grad_ref[part].astype(F32) * keep
        joined = (key * value).astype(BF16)
        mixed = (scaled * query).astype(BF16)
        before, following = before_ref[part], following_ref[part]
        taps = jnp.broadcast_to(tap_ref[group : group + 1], (length, length))
        circle = pltpu.roll(taps, 0, 1, stride=1, stride_axis=0)
        lower = jnp.where(causal, circle, 0.0).astype(BF16)
        upper = jnp.where(causal, 0.0, circle).astype(BF16)
        start = group * per_group
        skip = skips[start % length : start % length + per_group, start // length : start // length + 1]
        forward = jnp.dot(
            jnp.concatenate([before, joined], axis=1),
            jnp.concatenate([upper, lower], axis=0),
            preferred_element_type=F32,
        )
        forward += skip * joined.astype(F32)
        backward = lax.dot_general(
            jnp.concatenate([mixed, following], axis=1),
            jnp.concatenate([lower, upper], axis=1),
            ROWS_BY_ROWS,
            preferred_element_type=F32,
        )
        backward += skip * mixed.astype(F32)
        out_ref[part] = (query * forward).astype(BF16)
        query_grad_ref[part] = (scaled * forward).astype(BF16)
        key_grad_ref[part] = (backward * value).astype(BF16)
        value_grad_ref[part] = (backward * key).astype(BF16)


def outputs(keep, taps, skip, query, key, value, grad, before, following):
    channels, length = query.shape
    groups = taps.shape[0]
    steps = 2
    large = pl.BlockSpec((channels // steps, length), lambda i: (i, 0))
    skip_rows = skip.reshape(steps, channels // length // steps, length)
    return pl.pallas_call(
        functools.partial(output_kernel, channels // groups),
        grid=(steps,),
        in_specs=[
            pl.BlockSpec((1, length), lambda i: (0, 0)),
            pl.BlockSpec((groups // steps, length), lambda i: (i, 0)),
            pl.BlockSpec((1,) + skip_rows.shape[1:], lambda i: (i, 0, 0)),
        ]
        + [large] * 6,
        out_specs=[large] * 4,
        out_shape=[jax.ShapeDtypeStruct((channels, length), BF16)] * 4,
        cost_estimate=pl.CostEstimate(flops=2**28, bytes_accessed=2**24, transcendentals=0),
        compiler_params=pltpu.CompilerParams(vmem_limit_bytes=12 * 2**20),
        name="outputs",
    )(keep, taps, skip_rows, query, key, value, grad, before, following)


def filters(per_group, held, halo_ref, out_refs, made_refs, sems, tasks):
    first = lax.axis_index("ctx") == 0

    def run(here):
        copies = []
        for index, (chosen, bounds) in enumerate(tasks):
            forward = chosen == "all" or (chosen == "free") == here
            backward = chosen == "all" or (chosen == "free") != here
            copies += filter_groups(
                per_group, held, halo_ref, out_refs, made_refs, sems, here, forward, backward, bounds, 8 * index
            )
        for copy in copies:
            copy.wait()

    pl.when(first)(functools.partial(run, True))
    pl.when(jnp.logical_not(first))(functools.partial(run, False))


def filter_groups(
    per_group, held, halo_ref, out_refs, made_refs, sems, first, forward, backward, bounds, sem
):
    keep_ref, query_ref, key_ref, value_ref, grad_ref, tap_ref, skip_ref = held
    out_refs = out_refs[0 if forward else 2 : 4 if backward else 2]
    made_refs = made_refs[: len(out_refs)]
    length = query_ref.shape[1]
    row, column = iotas(length, length)
    causal = column >= row
    keep = keep_ref[...].astype(F32)
    skips = skip_ref[...].T
    copies = []
    for group in range(bounds[0], bounds[-1]):
        start = group * per_group
        part = slice(start, start + per_group)
        query = query_ref[part].astype(F32)
        key = key_ref[part].astype(F32)
        value = value_ref[part].astype(F32)
        scaled = grad_ref[part].astype(F32) * keep
        joined = (key * value).astype(BF16)
        mixed = (scaled * query).astype(BF16)
        taps = jnp.broadcast_to(tap_ref[group : group + 1], (length, length))
        circle = pltpu.roll(taps, 0, 1, stride=1, stride_axis=0)
        lower = jnp.where(causal, circle, 0.0).astype(BF16)
        upper = jnp.where(causal, 0.0, circle).astype(BF16)
        skip = skips[
            start % length : start % length + per_group, start // length : start // length + 1
        ]
        if halo_ref is not None:
            halo = halo_ref[part]
        results = []
        if forward:
            source, matrix = joined, lower
            if not first:
                source = jnp.concatenate([halo, joined], axis=1)
                matrix = jnp.concatenate([upper, lower], axis=0)
            mixed_sum = jnp.dot(source, matrix, preferred_element_type=F32)
            mixed_sum += skip * joined.astype(F32)
            results += [query * mixed_sum, scaled * mixed_sum]
        if backward:
            source, matrix = mixed, lower
            if first:
                source = jnp.concatenate([mixed, halo], axis=1)
                matrix = jnp.concatenate([lower, upper], axis=1)
            joined_grad = lax.dot_general(source, matrix, ROWS_BY_ROWS, preferred_element_type=F32)
            joined_grad += skip * mixed.astype(F32)
            results += [joined_grad * value, joined_grad * key]
        for made, result in zip(made_refs, results):
            made[part] = result.astype(BF16)
        if group + 1 in bounds:
            begin = bounds[bounds.index(group + 1) - 1] * per_group
            window = pl.ds(begin, start + per_group - begin)
            for made, out in zip(made_refs, out_refs):
                copies.append(
                    pltpu.make_async_copy(made.at[window], out.at[window], sems.at[sem + len(copies)])
                )
                copies[-1].start()
    return copies


def pair_kernel(per_group, *refs):
    held, halo_ref, out_refs = refs[:7], refs[7], refs[12:16]
    made_refs, sems = refs[16:20], refs[20]
    groups = held[5].shape[0]
    even = lax.axis_index("tp") % 2 == 0
    rest = (per_group, held, halo_ref, out_refs, made_refs, sems)
    pl.when(even)(functools.partial(filters, *rest, [("all", (0, groups // 2, groups))]))
    tasks = [("bound", (0, 3 * groups // 8, 3 * groups // 4)), ("all", (3 * groups // 4, groups))]
    pl.when(jnp.logical_not(even))(functools.partial(filters, *rest, tasks))


def pair_outputs(held, halo, results):
    channels, length = held[1].shape
    hbm = pl.BlockSpec(memory_space=pltpu.HBM)
    return pl.pallas_call(
        functools.partial(pair_kernel, channels // held[5].shape[0]),
        in_specs=[pl.BlockSpec(memory_space=pltpu.VMEM)] * 8 + [hbm] * 4,
        out_specs=[hbm] * 4,
        out_shape=[jax.ShapeDtypeStruct((channels, length), BF16)] * 4,
        input_output_aliases={8: 0, 9: 1, 10: 2, 11: 3},
        scratch_shapes=[pltpu.VMEM((channels, length), BF16)] * 4
        + [pltpu.SemaphoreType.DMA((16,))],
        cost_estimate=pl.CostEstimate(flops=2**28, bytes_accessed=2**23, transcendentals=0),
        compiler_params=pltpu.CompilerParams(vmem_limit_bytes=12 * 2**20),
        name="pair_outputs",
    )(*map(in_vmem, (*held, halo)), *results)


def exchanges(size):
    if size == 4:
        return [(2, 3, 1, 0), (3, 2, 0, 1), (1, 0, 3, 2)]
    return [tuple((i + step) % size for i in range(size)) for step in range(1, size)]


def gather_terms(sums, axis):
    return [sums] + [
        lax.ppermute(sums, axis, list(enumerate(targets)))
        for targets in exchanges(lax.axis_size(axis))
    ]


def total_kernel(groups, tap_scale, skip_scale, axis, order, *refs):
    *term_refs, tap_ref, skip_ref = refs
    taken = [term_refs[order.index(place)][...].astype(F32) for place in range(len(term_refs))]
    size = lax.axis_size(axis)
    here = lax.axis_index(axis)
    terms = [taken[0]] * size
    for received, targets in zip(taken[1:], exchanges(size)):
        for source, target in enumerate(targets):
            if source != target:
                terms[source] = jnp.where(here == target, received, terms[source])
    total = terms[0]
    for term in terms[1:]:
        total = total + term
    tap_ref[...] = total[:groups] * tap_scale
    skip_ref[...] = total[groups:] * skip_scale


def totals(terms, groups, tap_scale, skip_scale, axis):
    rows, length = terms[0].shape
    order = list(range(len(terms)))
    return pl.pallas_call(
        functools.partial(total_kernel, groups, tap_scale, skip_scale, axis, order),
        in_specs=[pl.BlockSpec(memory_space=pltpu.VMEM)] * len(terms),
        out_shape=[
            jax.ShapeDtypeStruct((groups, length), F32),
            jax.ShapeDtypeStruct((rows - groups, length), F32),
        ],
        compiler_params=pltpu.CompilerParams(vmem_limit_bytes=12 * 2**20),
        name="totals",
    )(*(in_vmem(terms[place]) for place in order))


def body(query_act, key_act, value_act, out_grad, keep_mask, filter_taps, skip_gain):
    windows, channels, length = query_act.shape
    groups, tap_count = filter_taps.shape
    assert windows == 1 and length == tap_count
    shards = lax.axis_size("ctx")
    per_group = channels // groups
    positions = windows * lax.axis_size("dp") * length * shards
    tap_scale = 1.0 / math.sqrt(positions * per_group)
    skip_scale = 1.0 / math.sqrt(positions)
    query, key, value, grad = query_act[0], key_act[0], value_act[0], out_grad[0]
    if shards == 2:
        swap = [(0, 1), (1, 0)]
        skips = skip_gain.reshape(channels // length, length)
        sources = (keep_mask, query, key, value, grad, filter_taps, skips)
        own, *made = first_turn(*sources)
        halo = lax.ppermute(own, "ctx", swap)
        *held, mine = turn_sums(sources, *made[:8])
        other = lax.ppermute(mine, "ctx", swap)
        crossed = halo_sums(halo, ready_sides(own, per_group, mine), per_group)
        sums = mine.astype(F32).at[:groups].add(crossed) + other.astype(F32)
        sums = lax.reduce_precision(sums, 8, 7).astype(BF16)
        terms = gather_terms(sums, "dp")
        results = pair_outputs(held, halo, made[8:])
    else:
        joined = (key.astype(F32) * value.astype(F32)).astype(BF16)
        own = (grad.astype(F32) * keep_mask.astype(F32) * query.astype(F32)).astype(BF16)
        before = lax.ppermute(joined, "ctx", [(i, i + 1) for i in range(shards - 1)])
        following = lax.ppermute(own, "ctx", [(i + 1, i) for i in range(shards - 1)])
        mine = local_sums(groups, keep_mask, query, key, value, grad)
        crossed = cross_sums(own, before, groups)
        sums = lax.psum(mine.at[:groups].add(crossed), "ctx")
        terms = gather_terms(sums, "dp")
        results = outputs(keep_mask, filter_taps, skip_gain, query, key, value, grad, before, following)
    filter_grad, skip_grad = totals(terms, groups, tap_scale, skip_scale, "dp")
    return (*(result[None] for result in results), filter_grad, skip_grad.reshape(channels))


def solution(mesh):
    large = P("dp", "tp", "ctx")
    return jax.shard_map(
        body,
        mesh=mesh,
        in_specs=(large, large, large, large, P("dp", "ctx"), P("tp", None), P("tp")),
        out_specs=(large, large, large, large, P("tp", None), P("tp")),
        check_vma=False,
    )
```

```python
import functools
import math

import jax
import jax.numpy as jnp
from jax import lax
from jax.experimental import pallas as pl
from jax.experimental.pallas import tpu as pltpu
from jax.sharding import PartitionSpec as P

BF16 = jnp.bfloat16
F32 = jnp.float32
PARTS = 2
PHASES = 4
ROWS_BY_ROWS = (((1,), (1,)), ((), ()))


def in_hbm(array):
    return pltpu.with_memory_space_constraint(array, pltpu.HBM)


def in_vmem(array):
    return pltpu.with_memory_space_constraint(array, pltpu.VMEM)


def iotas(rows, columns):
    return (
        lax.broadcasted_iota(jnp.int32, (rows, columns), 0),
        lax.broadcasted_iota(jnp.int32, (rows, columns), 1),
    )


def flip(block):
    length = block.shape[1]
    row, column = iotas(length, length)
    mirror = (row + column == length - 1).astype(F32).astype(BF16)
    return jnp.dot(block, mirror, preferred_element_type=F32).astype(BF16)


def grad_side(grad, per_group):
    length = grad.shape[1]
    span = length // PHASES
    across = grad.T
    left = jnp.concatenate([across[p * span : (p + 1) * span] for p in range(PHASES)], axis=1)
    owner = iotas(1, PHASES * length)[1] % length // per_group
    nothing = jnp.zeros((), BF16)
    return jnp.concatenate(
        [jnp.where(owner == g, left, nothing) for g in range(length // per_group)], axis=0
    )


def joined_side(joined, crossing):
    length = joined.shape[1]
    lane = iotas(1, length)[1]
    nothing = jnp.zeros((), BF16)
    mirrored = flip(joined).astype(F32)
    right = []
    for phase in range(PHASES):
        shift = length // PHASES * (phase + 1)
        turned = (mirrored if shift == length else pltpu.roll(mirrored, shift, 1)).astype(BF16)
        if crossing:
            earlier = jnp.where(lane >= shift, turned, nothing)
            right.append(jnp.concatenate([earlier, turned], axis=1))
        else:
            right.append(jnp.where(lane < shift, turned, nothing))
    return jnp.concatenate(right, axis=0)


def side_sums(sides, length, crossing):
    span = length // PHASES
    row, column = iotas(span, length)
    near = row + column >= span - 1
    sums = []
    for left, right in sides:
        grams = jnp.dot(left, right, preferred_element_type=F32)
        for start in range(0, grams.shape[0], span):
            gram = grams[start : start + span]
            gram = jnp.where(near, gram[:, :length], gram[:, length:] if crossing else 0.0)
            turned = pltpu.roll(gram, 0, 1, stride=1, stride_axis=0)
            sums.append(jnp.sum(turned, axis=0, keepdims=True))
    return pltpu.roll(jnp.concatenate(sums, axis=0), length - span + 1, 1)


def blocks_of(array):
    length = array.shape[1]
    return [array[start : start + length] for start in range(0, array.shape[0], length)]


def lag_sums(grad, joined, per_group, crossing):
    sides = [
        (grad_side(one, per_group), joined_side(two, crossing))
        for one, two in zip(blocks_of(grad), blocks_of(joined))
    ]
    return side_sums(sides, grad.shape[1], crossing)


def own_kernel(*refs):
    sources, own_ref, held, sems = refs[:5], refs[5], refs[6:13], refs[13]
    first = lax.axis_index("ctx") == 0
    channels = own_ref.shape[0]
    rows = channels // PARTS

    def run(one, two, masked):
        def copies_of(part):
            window = pl.ds(part * rows, rows)
            return [
                pltpu.make_async_copy(
                    sources[index].at[window], held[index].at[window], sems.at[2 * part + side]
                )
                for side, index in enumerate((one, two))
            ]

        keep_copy = pltpu.make_async_copy(sources[0], held[0], sems.at[2 * PARTS])
        keep_copy.start()
        for part in range(PARTS):
            for copy in copies_of(part):
                copy.start()
        keep_copy.wait()
        for part in range(PARTS):
            for copy in copies_of(part):
                copy.wait()
            window = pl.ds(part * rows, rows)
            scaled = held[two][window].astype(F32)
            if masked:
                scaled = scaled * held[0][...].astype(F32)
            own_ref[window] = (scaled * held[one][window].astype(F32)).astype(BF16)

    pl.when(first)(functools.partial(run, 2, 3, False))
    pl.when(jnp.logical_not(first))(functools.partial(run, 1, 4, True))


def first_kernel(per_group, *refs):
    sources, (own_ref, *held), sums_ref, out_refs = refs[:7], refs[7:15], refs[15], refs[16:20]
    own_sems, sems, made_refs, out_sems = refs[20], refs[21], refs[22:24], refs[24]
    own_kernel(*sources[:5], own_ref, *held, own_sems)
    turn_part(per_group, 0, sources[1:], held, sums_ref, sems, out_refs, made_refs, out_sems)


def first_turn(*sources):
    channels, length = sources[1].shape
    groups = sources[5].shape[0]
    whole = pl.BlockSpec(memory_space=pltpu.VMEM)
    hbm = pl.BlockSpec(memory_space=pltpu.HBM)
    return pl.pallas_call(
        functools.partial(first_kernel, channels // groups),
        in_specs=[hbm] * 7,
        out_specs=[whole] * 9 + [hbm] * 4,
        out_shape=[pltpu.VMEM((channels, length), BF16)]
        + [pltpu.VMEM(source.shape, source.dtype) for source in sources]
        + [pltpu.VMEM((groups + channels // length, length), BF16)]
        + [jax.ShapeDtypeStruct((channels, length), BF16)] * 4,
        scratch_shapes=[pltpu.SemaphoreType.DMA((2 * PARTS + 1,)), pltpu.SemaphoreType.DMA((4,))]
        + [pltpu.VMEM((channels, length), BF16)] * 2
        + [pltpu.SemaphoreType.DMA((8,))],
        compiler_params=pltpu.CompilerParams(vmem_limit_bytes=12 * 2**20),
        name="first_turn",
    )(*map(in_hbm, sources))


def turn_kernel(per_group, *refs):
    turn_part(per_group, 1, refs[:6], refs[14:21], refs[21], refs[22])


def turn_part(per_group, turn, sources, held, sums_ref, sems, out_refs=(), made_refs=(), out_sems=None):
    query, key, value, grad, taps, skips = zip(sources, held[1:])

    def load(*pairs):
        return [
            pltpu.make_async_copy(source, target, sems.at[index])
            for index, (source, target) in enumerate(pairs)
        ]

    @pl.when(lax.axis_index("tp") % 2 == 1 - turn)
    def _():
        first = lax.axis_index("ctx") == 0

        @pl.when(first)
        def _():
            for copy in load(query, grad, taps, skips):
                copy.start()

        @pl.when(jnp.logical_not(first))
        def _():
            for copy in load(key, value, taps, skips):
                copy.start()

        for copy in load(key, value, taps, skips):
            copy.wait()
        local_part(per_group, held, sums_ref)
        if turn == 0:
            filters(per_group, held, None, out_refs, made_refs, out_sems, ahead)


def turn_sums(sources, *given):
    channels = given[1].shape[0]
    whole = pl.BlockSpec(memory_space=pltpu.VMEM)
    return pl.pallas_call(
        functools.partial(turn_kernel, channels // given[5].shape[0]),
        in_specs=[pl.BlockSpec(memory_space=pltpu.HBM)] * 6 + [whole] * 8,
        out_specs=[whole] * 8,
        out_shape=[pltpu.VMEM(array.shape, array.dtype) for array in given],
        input_output_aliases={6 + index: index for index in range(8)},
        scratch_shapes=[pltpu.SemaphoreType.DMA((4,))],
        cost_estimate=pl.CostEstimate(flops=2**26, bytes_accessed=2**23, transcendentals=0),
        compiler_params=pltpu.CompilerParams(vmem_limit_bytes=12 * 2**20),
        name="turn_sums",
    )(*map(in_hbm, sources[1:]), *map(in_vmem, given))


def local_kernel(per_group, *refs):
    local_part(per_group, refs[:5], refs[5])


def local_part(per_group, held, sums_ref):
    keep_ref, query_ref, key_ref, value_ref, grad_ref = held[:5]
    channels, length = query_ref.shape
    groups = channels // per_group
    joined = (key_ref[...].astype(F32) * value_ref[...].astype(F32)).astype(BF16)
    scaled = grad_ref[...].astype(F32) * keep_ref[...].astype(F32)
    mixed = (scaled * query_ref[...].astype(F32)).astype(BF16)
    sums_ref[:groups] = lag_sums(mixed, joined, per_group, False).astype(sums_ref.dtype)
    both = joined.astype(F32) * mixed.astype(F32)
    high = both.astype(BF16)
    low = (both - high.astype(F32)).astype(BF16)
    ones = jnp.ones((8, length), BF16)
    direct = lax.dot_general(ones, high, ROWS_BY_ROWS, preferred_element_type=F32)
    direct += lax.dot_general(ones, low, ROWS_BY_ROWS, preferred_element_type=F32)
    for block in range(channels // length):
        sums_ref[groups + block : groups + block + 1] = direct[
            :1, block * length : (block + 1) * length
        ].astype(sums_ref.dtype)


def local_sums(groups, *arrays):
    channels, length = arrays[1].shape
    return pl.pallas_call(
        functools.partial(local_kernel, channels // groups),
        out_shape=jax.ShapeDtypeStruct((groups + channels // length, length), F32),
        cost_estimate=pl.CostEstimate(flops=2**26, bytes_accessed=2**23, transcendentals=0),
        name="local_sums",
    )(*arrays)


def cross_kernel(per_group, own_ref, halo_ref, sums_ref):
    sums_ref[...] = lag_sums(own_ref[...], halo_ref[...], per_group, True)


def cross_sums(own, halo, groups):
    channels, length = own.shape
    return pl.pallas_call(
        functools.partial(cross_kernel, channels // groups),
        out_shape=jax.ShapeDtypeStruct((groups, length), F32),
        cost_estimate=pl.CostEstimate(flops=2**26, bytes_accessed=2**23, transcendentals=0),
        name="cross_sums",
    )(own, halo)


def ready_kernel(per_group, own_ref, _, left_ref, right_ref):
    first = lax.axis_index("ctx") == 0

    @pl.when(first)
    def _():
        for block, own in enumerate(blocks_of(own_ref[...])):
            right_ref[block] = joined_side(own, True)

    @pl.when(jnp.logical_not(first))
    def _():
        for block, own in enumerate(blocks_of(own_ref[...])):
            left_ref[block] = grad_side(own, per_group)


def halo_kernel(per_group, halo_ref, left_ref, right_ref, sums_ref):
    length = halo_ref.shape[1]
    first = lax.axis_index("ctx") == 0

    @pl.when(first)
    def _():
        grads = blocks_of(halo_ref[...])
        sides = [(grad_side(grad, per_group), right_ref[block]) for block, grad in enumerate(grads)]
        sums_ref[...] = side_sums(sides, length, True)

    @pl.when(jnp.logical_not(first))
    def _():
        sides = [
            (left_ref[block], joined_side(joined, True))
            for block, joined in enumerate(blocks_of(halo_ref[...]))
        ]
        sums_ref[...] = side_sums(sides, length, True)


def ready_sides(own, per_group, after):
    channels, length = own.shape
    blocks = channels // length
    spread = length // PHASES * (length // per_group)
    whole = pl.BlockSpec(memory_space=pltpu.VMEM)
    return pl.pallas_call(
        functools.partial(ready_kernel, per_group),
        in_specs=[whole] * 2,
        out_specs=[whole] * 2,
        out_shape=[
            pltpu.VMEM((blocks, spread, PHASES * length), BF16),
            pltpu.VMEM((blocks, PHASES * length, 2 * length), BF16),
        ],
        cost_estimate=pl.CostEstimate(flops=2**26, bytes_accessed=2**23, transcendentals=0),
        compiler_params=pltpu.CompilerParams(vmem_limit_bytes=12 * 2**20),
        name="ready_sides",
    )(in_vmem(own), in_vmem(after))


def halo_sums(halo, sides, per_group):
    channels, length = halo.shape
    whole = pl.BlockSpec(memory_space=pltpu.VMEM)
    return pl.pallas_call(
        functools.partial(halo_kernel, per_group),
        in_specs=[whole] * 3,
        out_specs=whole,
        out_shape=pltpu.VMEM((channels // per_group, length), F32),
        cost_estimate=pl.CostEstimate(flops=2**26, bytes_accessed=2**23, transcendentals=0),
        compiler_params=pltpu.CompilerParams(vmem_limit_bytes=12 * 2**20),
        name="halo_sums",
    )(in_vmem(halo), *map(in_vmem, sides))


def output_kernel(
    per_group, keep_ref, tap_ref, skip_ref, query_ref, key_ref, value_ref, grad_ref,
    before_ref, following_ref, out_ref, query_grad_ref, key_grad_ref, value_grad_ref,
):
    channels, length = query_ref.shape
    row, column = iotas(length, length)
    causal = column >= row
    keep = keep_ref[...].astype(F32)
    skips = skip_ref[0].T
    for group in range(channels // per_group):
        part = slice(group * per_group, (group + 1) * per_group)
        query = query_ref[part].astype(F32)
        key = key_ref[part].astype(F32)
        value = value_ref[part].astype(F32)
        scaled = grad_ref[part].astype(F32) * keep
        joined = (key * value).astype(BF16)
        mixed = (scaled * query).astype(BF16)
        before, following = before_ref[part], following_ref[part]
        taps = jnp.broadcast_to(tap_ref[group : group + 1], (length, length))
        circle = pltpu.roll(taps, 0, 1, stride=1, stride_axis=0)
        lower = jnp.where(causal, circle, 0.0).astype(BF16)
        upper = jnp.where(causal, 0.0, circle).astype(BF16)
        start = group * per_group
        skip = skips[start % length : start % length + per_group, start // length : start // length + 1]
        forward = jnp.dot(
            jnp.concatenate([before, joined], axis=1),
            jnp.concatenate([upper, lower], axis=0),
            preferred_element_type=F32,
        )
        forward += skip * joined.astype(F32)
        backward = lax.dot_general(
            jnp.concatenate([mixed, following], axis=1),
            jnp.concatenate([lower, upper], axis=1),
            ROWS_BY_ROWS,
            preferred_element_type=F32,
        )
        backward += skip * mixed.astype(F32)
        out_ref[part] = (query * forward).astype(BF16)
        query_grad_ref[part] = (scaled * forward).astype(BF16)
        key_grad_ref[part] = (backward * value).astype(BF16)
        value_grad_ref[part] = (backward * key).astype(BF16)


def outputs(keep, taps, skip, query, key, value, grad, before, following):
    channels, length = query.shape
    groups = taps.shape[0]
    steps = 2
    large = pl.BlockSpec((channels // steps, length), lambda i: (i, 0))
    skip_rows = skip.reshape(steps, channels // length // steps, length)
    return pl.pallas_call(
        functools.partial(output_kernel, channels // groups),
        grid=(steps,),
        in_specs=[
            pl.BlockSpec((1, length), lambda i: (0, 0)),
            pl.BlockSpec((groups // steps, length), lambda i: (i, 0)),
            pl.BlockSpec((1,) + skip_rows.shape[1:], lambda i: (i, 0, 0)),
        ]
        + [large] * 6,
        out_specs=[large] * 4,
        out_shape=[jax.ShapeDtypeStruct((channels, length), BF16)] * 4,
        cost_estimate=pl.CostEstimate(flops=2**28, bytes_accessed=2**24, transcendentals=0),
        compiler_params=pltpu.CompilerParams(vmem_limit_bytes=12 * 2**20),
        name="outputs",
    )(keep, taps, skip_rows, query, key, value, grad, before, following)


def ahead(groups, first):
    share = groups * (12 if first else 8) // 16
    return [("free", (0, share // 2, share))]


def behind(groups, first):
    bounds = ahead(groups, first)[0][1]
    return [("bound", bounds)] + [("all", (bounds[-1], groups))] * (bounds[-1] < groups)


def whole(groups, first):
    return [("all", (0, groups // 2, groups))]


def filters(per_group, held, halo_ref, out_refs, made_refs, sems, tasks):
    first = lax.axis_index("ctx") == 0

    def run(here):
        copies = []
        for index, (chosen, bounds) in enumerate(tasks(held[5].shape[0], here)):
            forward = chosen == "all" or (chosen == "free") == here
            backward = chosen == "all" or (chosen == "free") != here
            copies += filter_groups(
                per_group, held, halo_ref, out_refs, made_refs, sems, here, forward, backward, bounds, 8 * index
            )
        for copy in copies:
            copy.wait()

    pl.when(first)(functools.partial(run, True))
    pl.when(jnp.logical_not(first))(functools.partial(run, False))


def filter_groups(
    per_group, held, halo_ref, out_refs, made_refs, sems, first, forward, backward, bounds, sem
):
    keep_ref, query_ref, key_ref, value_ref, grad_ref, tap_ref, skip_ref = held
    out_refs = out_refs[0 if forward else 2 : 4 if backward else 2]
    made_refs = made_refs[: len(out_refs)]
    length = query_ref.shape[1]
    row, column = iotas(length, length)
    causal = column >= row
    keep = keep_ref[...].astype(F32)
    skips = skip_ref[...].T
    copies = []
    for group in range(bounds[0], bounds[-1]):
        start = group * per_group
        part = slice(start, start + per_group)
        query = query_ref[part].astype(F32)
        key = key_ref[part].astype(F32)
        value = value_ref[part].astype(F32)
        scaled = grad_ref[part].astype(F32) * keep
        joined = (key * value).astype(BF16)
        mixed = (scaled * query).astype(BF16)
        taps = jnp.broadcast_to(tap_ref[group : group + 1], (length, length))
        circle = pltpu.roll(taps, 0, 1, stride=1, stride_axis=0)
        lower = jnp.where(causal, circle, 0.0).astype(BF16)
        upper = jnp.where(causal, 0.0, circle).astype(BF16)
        skip = skips[
            start % length : start % length + per_group, start // length : start // length + 1
        ]
        if halo_ref is not None:
            halo = halo_ref[part]
        results = []
        if forward:
            source, matrix = joined, lower
            if not first:
                source = jnp.concatenate([halo, joined], axis=1)
                matrix = jnp.concatenate([upper, lower], axis=0)
            mixed_sum = jnp.dot(source, matrix, preferred_element_type=F32)
            mixed_sum += skip * joined.astype(F32)
            results += [query * mixed_sum, scaled * mixed_sum]
        if backward:
            source, matrix = mixed, lower
            if first:
                source = jnp.concatenate([mixed, halo], axis=1)
                matrix = jnp.concatenate([lower, upper], axis=1)
            joined_grad = lax.dot_general(source, matrix, ROWS_BY_ROWS, preferred_element_type=F32)
            joined_grad += skip * mixed.astype(F32)
            results += [joined_grad * value, joined_grad * key]
        for made, result in zip(made_refs, results):
            made[part] = result.astype(BF16)
        if group + 1 in bounds:
            begin = bounds[bounds.index(group + 1) - 1] * per_group
            window = pl.ds(begin, start + per_group - begin)
            for made, out in zip(made_refs, out_refs):
                copies.append(
                    pltpu.make_async_copy(made.at[window], out.at[window], sems.at[sem + len(copies)])
                )
                copies[-1].start()
    return copies


def pair_kernel(per_group, *refs):
    held, halo_ref, out_refs = refs[:7], refs[7], refs[12:16]
    made_refs, sems = refs[16:20], refs[20]
    even = lax.axis_index("tp") % 2 == 0
    rest = (per_group, held, halo_ref, out_refs, made_refs, sems)
    pl.when(even)(functools.partial(filters, *rest, whole))
    pl.when(jnp.logical_not(even))(functools.partial(filters, *rest, behind))


def pair_outputs(held, halo, results):
    channels, length = held[1].shape
    hbm = pl.BlockSpec(memory_space=pltpu.HBM)
    return pl.pallas_call(
        functools.partial(pair_kernel, channels // held[5].shape[0]),
        in_specs=[pl.BlockSpec(memory_space=pltpu.VMEM)] * 8 + [hbm] * 4,
        out_specs=[hbm] * 4,
        out_shape=[jax.ShapeDtypeStruct((channels, length), BF16)] * 4,
        input_output_aliases={8: 0, 9: 1, 10: 2, 11: 3},
        scratch_shapes=[pltpu.VMEM((channels, length), BF16)] * 4
        + [pltpu.SemaphoreType.DMA((16,))],
        cost_estimate=pl.CostEstimate(flops=2**28, bytes_accessed=2**23, transcendentals=0),
        compiler_params=pltpu.CompilerParams(vmem_limit_bytes=12 * 2**20),
        name="pair_outputs",
    )(*map(in_vmem, (*held, halo)), *results)


def exchanges(size):
    if size == 4:
        return [(2, 3, 1, 0), (3, 2, 0, 1), (1, 0, 3, 2)]
    return [tuple((i + step) % size for i in range(size)) for step in range(1, size)]


def gather_terms(sums, axis):
    return [sums] + [
        lax.ppermute(sums, axis, list(enumerate(targets)))
        for targets in exchanges(lax.axis_size(axis))
    ]


def total_kernel(groups, tap_scale, skip_scale, axis, order, *refs):
    *term_refs, tap_ref, skip_ref = refs
    taken = [term_refs[order.index(place)][...].astype(F32) for place in range(len(term_refs))]
    size = lax.axis_size(axis)
    here = lax.axis_index(axis)
    terms = [taken[0]] * size
    for received, targets in zip(taken[1:], exchanges(size)):
        for source, target in enumerate(targets):
            if source != target:
                terms[source] = jnp.where(here == target, received, terms[source])
    total = terms[0]
    for term in terms[1:]:
        total = total + term
    tap_ref[...] = total[:groups] * tap_scale
    skip_ref[...] = total[groups:] * skip_scale


def totals(terms, groups, tap_scale, skip_scale, axis):
    rows, length = terms[0].shape
    order = list(range(len(terms)))
    return pl.pallas_call(
        functools.partial(total_kernel, groups, tap_scale, skip_scale, axis, order),
        in_specs=[pl.BlockSpec(memory_space=pltpu.VMEM)] * len(terms),
        out_shape=[
            jax.ShapeDtypeStruct((groups, length), F32),
            jax.ShapeDtypeStruct((rows - groups, length), F32),
        ],
        compiler_params=pltpu.CompilerParams(vmem_limit_bytes=12 * 2**20),
        name="totals",
    )(*(in_vmem(terms[place]) for place in order))


def body(query_act, key_act, value_act, out_grad, keep_mask, filter_taps, skip_gain):
    windows, channels, length = query_act.shape
    groups, tap_count = filter_taps.shape
    assert windows == 1 and length == tap_count
    shards = lax.axis_size("ctx")
    per_group = channels // groups
    positions = windows * lax.axis_size("dp") * length * shards
    tap_scale = 1.0 / math.sqrt(positions * per_group)
    skip_scale = 1.0 / math.sqrt(positions)
    query, key, value, grad = query_act[0], key_act[0], value_act[0], out_grad[0]
    if shards == 2:
        swap = [(0, 1), (1, 0)]
        skips = skip_gain.reshape(channels // length, length)
        sources = (keep_mask, query, key, value, grad, filter_taps, skips)
        own, *made = first_turn(*sources)
        halo = lax.ppermute(own, "ctx", swap)
        *held, mine = turn_sums(sources, *made[:8])
        other = lax.ppermute(mine, "ctx", swap)
        crossed = halo_sums(halo, ready_sides(own, per_group, mine), per_group)
        sums = mine.astype(F32).at[:groups].add(crossed) + other.astype(F32)
        sums = lax.reduce_precision(sums, 8, 7).astype(BF16)
        terms = gather_terms(sums, "dp")
        results = pair_outputs(held, halo, made[8:])
    else:
        joined = (key.astype(F32) * value.astype(F32)).astype(BF16)
        own = (grad.astype(F32) * keep_mask.astype(F32) * query.astype(F32)).astype(BF16)
        before = lax.ppermute(joined, "ctx", [(i, i + 1) for i in range(shards - 1)])
        following = lax.ppermute(own, "ctx", [(i + 1, i) for i in range(shards - 1)])
        mine = local_sums(groups, keep_mask, query, key, value, grad)
        crossed = cross_sums(own, before, groups)
        sums = lax.psum(mine.at[:groups].add(crossed), "ctx")
        terms = gather_terms(sums, "dp")
        results = outputs(keep_mask, filter_taps, skip_gain, query, key, value, grad, before, following)
    filter_grad, skip_grad = totals(terms, groups, tap_scale, skip_scale, "dp")
    return (*(result[None] for result in results), filter_grad, skip_grad.reshape(channels))


def solution(mesh):
    large = P("dp", "tp", "ctx")
    return jax.shard_map(
        body,
        mesh=mesh,
        in_specs=(large, large, large, large, P("dp", "ctx"), P("tp", None), P("tp")),
        out_specs=(large, large, large, large, P("tp", None), P("tp")),
        check_vma=False,
    )
```
